256 devices in a mesh: gx: 32 (over y, z), gy: 8 (over x, core).
Axes of the slice: x: 4, y: 4, z: 8, core: 2. Of those that a mesh axis runs over, the one named last changes fastest.
Arguments:
- normed: bfloat16 [163840, 1024], P(('gx', 'gy')), may hold values from -6 to 6
- grad_query: bfloat16 [163840, 1024], P(('gx', 'gy')), may hold values from -0.25 to 0.25
- grad_key: bfloat16 [163840, 1024], P(('gx', 'gy')), may hold values from -0.25 to 0.25
- error: bfloat16 [512, 1024, 1024], P(('gx', 'gy')), may hold values from -8 to 8
- start_factor: float32 [2, 32, 1024], replicated, may hold values from -6 to 6
Outputs:
- new_error: bfloat16 [512, 1024, 1024], P(('gx', 'gy'))
- left_factor: float32 [2, 32, 1024], replicated
- right_factor: float32 [2, 32, 1024], replicated
The draws below stay inside these ranges and needn't reach their ends.
All inputs are finite; a program needn't handle non-finite values.
Results may differ from the reference program's by a relative error of at most 0.001.
Values sent between devices are 32-bit elements; how exact they have to be, the bound alone decides.
A program may use at most 64 MiB of HBM per device.

```python
import jax
import jax.numpy as jnp
from jax import lax

DM = 1024
DO = 1024
RANK = 32
TOK_DEV = 640
REPLICAS = 256
TOKENS = 163840


def draw_error(key, part):
    groups = RANK // 2
    row_key = jax.random.fold_in(key, 101)
    column_key = jax.random.fold_in(key, 202)
    noise_key = jax.random.fold_in(key, 303)
    row_values = jnp.clip(jax.random.normal(row_key, (2, DM), jnp.float32), -3.0, 3.0)
    column_values = jnp.clip(jax.random.normal(column_key, (2, groups, DO), jnp.float32), -3.0, 3.0)
    noise_part = jnp.clip(jax.random.normal(noise_key, (REPLICAS, 2, DM, DO), jnp.float32), -4.0, 4.0)
    group_index = jnp.arange(DM) % groups
    picked = jnp.take(column_values, group_index, axis=1)
    shared = row_values[:, :, None] * picked
    combined = jnp.clip(noise_part + shared[None], -8.0, 8.0)
    return combined.reshape(2 * REPLICAS, DM, DO).astype(jnp.bfloat16)


def level_of(own_key, extent, shards, smallest, high):
    factor_of = 1.0
    for axis_at, blocks in shards:
        draws = jax.random.uniform(jax.random.fold_in(jax.random.fold_in(own_key, 6), axis_at), (blocks,), jnp.float32, smallest / len(shards), high / len(shards))
        factor_of = factor_of * jnp.repeat(jnp.exp(draws), extent[axis_at] // blocks).reshape((-1,) + (1,) * (len(extent) - 1 - axis_at))
    return factor_of


def scatter_about(key, dims, scale, most, split=(), kind=jnp.bfloat16):
    level = level_of(key, dims, split, -0.22, 0.18) if split else 1.0
    result = jax.random.normal(key, dims, jnp.float32) * scale * level
    return jnp.minimum(jnp.maximum(result, -most), most).astype(kind)


def setup_inputs(seed: int = 0) -> dict:
    seeds = jax.random.split(jax.random.key(seed), 6)
    normed = scatter_about(seeds[0], (TOKENS, DM), 1.0, 6.0, ((0, 256),))
    grad_query = scatter_about(seeds[1], (TOKENS, DO), 0.04, 0.25, ((0, 256),))
    grad_key = scatter_about(seeds[2], (TOKENS, DO), 0.04, 0.25, ((0, 256),))
    error = draw_error(jax.random.fold_in(seeds[5], 71), 0)
    start_factor = scatter_about(seeds[4], (2, RANK, DO), 1.0, 6.0, (), jnp.float32)
    return {"normed": normed, "grad_query": grad_query, "grad_key": grad_key, "error": error, "start_factor": start_factor}


HIGHEST = lax.Precision.HIGHEST

def merged_terms(activations, query_cot, key_cot, error_pair):
    contract = (((0,), (0,)), ((), ()))
    query_grad = lax.dot_general(activations.astype(jnp.float32), query_cot.astype(jnp.float32), contract, preferred_element_type=jnp.float32)
    key_grad = lax.dot_general(activations.astype(jnp.float32), key_cot.astype(jnp.float32), contract, preferred_element_type=jnp.float32)
    return jnp.stack([query_grad, key_grad]) + error_pair.astype(jnp.float32)

def orthonormal_rows(left_total):
    gram_matrix = jnp.einsum('bki,bli->bkl', left_total, left_total, precision=HIGHEST)
    width = gram_matrix.shape[-1]
    identity = jnp.eye(width, dtype=gram_matrix.dtype)
    trace_value = jnp.trace(gram_matrix, axis1=1, axis2=2)
    shift_value = 1e-06 * (trace_value / width + 1.0)
    lower_factor = jnp.linalg.cholesky(gram_matrix + shift_value[:, None, None] * identity)
    return lax.linalg.triangular_solve(lower_factor, left_total, left_side=True, lower=True)

def reference(normed, grad_query, grad_key, error, start_factor):
    activations = normed.reshape(REPLICAS, TOK_DEV, DM)
    query_cots = grad_query.reshape(REPLICAS, TOK_DEV, DO)
    key_cots = grad_key.reshape(REPLICAS, TOK_DEV, DO)
    error_pairs = error.reshape(REPLICAS, 2, DM, DO)
    replica_data = (activations, query_cots, key_cots, error_pairs)

    def accumulate(totals, item):
        left_sum, merged_sum = totals
        merged = merged_terms(*item)
        local_term = jnp.einsum('bkj,bij->bki', start_factor, merged, precision=HIGHEST)
        return ((left_sum + local_term, merged_sum + merged), None)
    initial = (jnp.zeros((2, RANK, DM), jnp.float32), jnp.zeros((2, DM, DO), jnp.float32))
    (left_total, merged_total), unused = lax.scan(accumulate, initial, replica_data)
    left_rows = orthonormal_rows(left_total)
    right_rows = jnp.einsum('bki,bij->bkj', left_rows, merged_total, precision=HIGHEST) / REPLICAS
    approx = jnp.einsum('bki,bkj->bij', left_rows, right_rows, precision=HIGHEST)

    def residual(item):
        return (merged_terms(*item) - approx).astype(jnp.bfloat16)
    new_error = lax.map(residual, replica_data).reshape(2 * REPLICAS, DM, DO)
    return (new_error, left_rows, right_rows)
```

```python
import functools

import jax
import jax.numpy as jnp
from jax import lax
from jax.experimental import pallas as pl
from jax.experimental.pallas import tpu as pltpu
from jax.sharding import PartitionSpec as P

HIGHEST = lax.Precision.HIGHEST
CONTRACT = (((0,), (0,)), ((), ()))
MESH_ID = pl.DeviceIdType.MESH
LANES = 128
SUB = 8


def allreduce_kernel(nx, ny, x_ref, o_ref, recv_a, p_t, recv_b, recv_c, recv_d,
                     sa, ra, sb, rb, sc, rc, sd, rd):
    h = lax.axis_index("gx")
    a = lax.axis_index("gy")
    nb, rows = x_ref.shape[0], x_ref.shape[1]
    kb = rows // SUB
    nt = nb * kb

    barrier = pltpu.get_barrier_semaphore()

    def signal_y(j, carry):
        pl.semaphore_signal(barrier, 1, device_id=(h, lax.rem(a + j, ny)),
                            device_id_type=MESH_ID)
        return carry

    def signal_x(j, carry):
        pl.semaphore_signal(barrier, 1, device_id=(lax.rem(h + j, nx), a),
                            device_id_type=MESH_ID)
        return carry

    lax.fori_loop(1, ny, signal_y, 0)
    lax.fori_loop(1, nx, signal_x, 0)
    pl.semaphore_wait(barrier, (ny - 1) + (nx - 1))

    def copy_a(peer, slot_src):
        return pltpu.make_async_remote_copy(
            src_ref=x_ref.at[:, :, pl.ds(pl.multiple_of(peer * LANES, LANES), LANES)],
            dst_ref=recv_a.at[slot_src],
            send_sem=sa.at[peer],
            recv_sem=ra.at[slot_src],
            device_id=(h, peer),
            device_id_type=MESH_ID,
        )

    def start_a(j, carry):
        copy_a(lax.rem(a + j, ny), a).start()
        return carry

    lax.fori_loop(1, ny, start_a, 0)
    recv_a[a] = x_ref[:, :, pl.ds(pl.multiple_of(a * LANES, LANES), LANES)]

    def wait_a(j, carry):
        copy_a(lax.rem(a + j, ny), a).wait_send()
        copy_a(a, lax.rem(a + j, ny)).wait_recv()
        return carry

    lax.fori_loop(1, ny, wait_a, 0)
    part = jnp.sum(recv_a[...], axis=0)
    for u in range(nt):
        p_t[u] = part[u // kb, (u % kb) * SUB:(u % kb + 1) * SUB, :]

    def copy_b(peer, slot_src, tile):
        return pltpu.make_async_remote_copy(
            src_ref=p_t.at[tile],
            dst_ref=recv_b.at[slot_src],
            send_sem=sb.at[peer],
            recv_sem=rb.at[slot_src],
            device_id=(peer, a),
            device_id_type=MESH_ID,
        )

    def start_b(j, carry):
        peer = lax.rem(h + j, nx)
        copy_b(peer, h, lax.rem(peer, nt)).start()
        return carry

    lax.fori_loop(1, nx, start_b, 0)
    own = lax.rem(h, nt)
    recv_b[h] = p_t[own]

    def wait_b(j, carry):
        peer = lax.rem(h + j, nx)
        copy_b(peer, h, lax.rem(peer, nt)).wait_send()
        copy_b(h, peer, own).wait_recv()
        return carry

    lax.fori_loop(1, nx, wait_b, 0)
    recv_c[own] = jnp.sum(recv_b[...], axis=0)

    base = h - own

    def copy_c(peer_tile, slot_tile):
        return pltpu.make_async_remote_copy(
            src_ref=recv_c.at[slot_tile],
            dst_ref=recv_c.at[slot_tile],
            send_sem=sc.at[peer_tile],
            recv_sem=rc.at[slot_tile],
            device_id=(base + peer_tile, a),
            device_id_type=MESH_ID,
        )

    def start_c(j, carry):
        copy_c(lax.rem(own + j, nt), own).start()
        return carry

    lax.fori_loop(1, nt, start_c, 0)

    def wait_c(j, carry):
        other = lax.rem(own + j, nt)
        copy_c(other, own).wait_send()
        copy_c(own, other).wait_recv()
        return carry

    lax.fori_loop(1, nt, wait_c, 0)
    for u in range(nt):
        recv_d[a, u // kb, (u % kb) * SUB:(u % kb + 1) * SUB, :] = recv_c[u]

    def copy_d(peer, slot_src):
        return pltpu.make_async_remote_copy(
            src_ref=recv_d.at[slot_src],
            dst_ref=recv_d.at[slot_src],
            send_sem=sd.at[peer],
            recv_sem=rd.at[slot_src],
            device_id=(h, peer),
            device_id_type=MESH_ID,
        )

    def start_d(j, carry):
        copy_d(lax.rem(a + j, ny), a).start()
        return carry

    lax.fori_loop(1, ny, start_d, 0)

    def wait_d(j, carry):
        copy_d(lax.rem(a + j, ny), a).wait_send()
        copy_d(a, lax.rem(a + j, ny)).wait_recv()
        return carry

    lax.fori_loop(1, ny, wait_d, 0)
    for s in range(ny):
        o_ref[:, :, s * LANES:(s + 1) * LANES] = recv_d[s]


def allreduce(x, nx, ny, collective_id):
    nb, rows, cols = x.shape
    assert cols == ny * LANES and rows % SUB == 0
    nt = nb * (rows // SUB)
    assert nx % nt == 0
    vmem = pltpu.VMEM
    return pl.pallas_call(
        functools.partial(allreduce_kernel, nx, ny),
        out_shape=jax.ShapeDtypeStruct(x.shape, jnp.float32),
        in_specs=[pl.BlockSpec(memory_space=vmem)],
        out_specs=pl.BlockSpec(memory_space=vmem),
        scratch_shapes=[
            vmem((ny, nb, rows, LANES), jnp.float32),
            vmem((nt, SUB, LANES), jnp.float32),
            vmem((nx, SUB, LANES), jnp.float32),
            vmem((nt, SUB, LANES), jnp.float32),
            vmem((ny, nb, rows, LANES), jnp.float32),
            pltpu.SemaphoreType.DMA((ny,)),
            pltpu.SemaphoreType.DMA((ny,)),
            pltpu.SemaphoreType.DMA((nx,)),
            pltpu.SemaphoreType.DMA((nx,)),
            pltpu.SemaphoreType.DMA((nt,)),
            pltpu.SemaphoreType.DMA((nt,)),
            pltpu.SemaphoreType.DMA((ny,)),
            pltpu.SemaphoreType.DMA((ny,)),
        ],
        compiler_params=pltpu.CompilerParams(
            collective_id=collective_id, has_side_effects=True
        ),
    )(x)


def gram_of(factor_rows):
    return jnp.einsum("bki,bli->bkl", factor_rows, factor_rows, precision=HIGHEST)


def solve_rows(gram_matrix, factor_rows):
    width = gram_matrix.shape[-1]
    identity = jnp.eye(width, dtype=jnp.float32)
    trace_value = jnp.trace(gram_matrix, axis1=1, axis2=2)
    shift_value = 1e-06 * (trace_value / width + 1.0)
    lower_factor = jnp.linalg.cholesky(gram_matrix + shift_value[:, None, None] * identity)
    return lax.linalg.triangular_solve(lower_factor, factor_rows, left_side=True, lower=True)


def on_device(nx, ny, normed, grad_query, grad_key, error, start_factor):
    replicas = nx * ny
    query_grad = lax.dot_general(normed, grad_query, CONTRACT, preferred_element_type=jnp.float32)
    key_grad = lax.dot_general(normed, grad_key, CONTRACT, preferred_element_type=jnp.float32)
    merged = jnp.stack([query_grad, key_grad]) + error.astype(jnp.float32)
    left_local = jnp.einsum("bkj,bij->bki", start_factor, merged, precision=HIGHEST)
    left_total = allreduce(left_local, nx, ny, 0)
    left_rows = solve_rows(gram_of(left_total), left_total)
    right_local = jnp.einsum("bki,bij->bkj", left_rows, merged, precision=HIGHEST)
    right_rows = allreduce(right_local, nx, ny, 1) / replicas
    approx = jnp.einsum("bki,bkj->bij", left_rows, right_rows, precision=HIGHEST)
    return ((merged - approx).astype(jnp.bfloat16), left_rows, right_rows)


def solution(mesh):
    nx, ny = mesh.shape["gx"], mesh.shape["gy"]
    placed = (
        P(("gx", "gy"), None),
        P(("gx", "gy"), None),
        P(("gx", "gy"), None),
        P(("gx", "gy"), None, None),
        P(),
    )
    return jax.shard_map(
        functools.partial(on_device, nx, ny),
        mesh=mesh,
        in_specs=placed,
        out_specs=(P(("gx", "gy"), None, None), P(), P()),
        check_vma=False,
    )
```

```python
import functools

import jax
import jax.numpy as jnp
from jax import lax
from jax.experimental import pallas as pl
from jax.experimental.pallas import tpu as pltpu
from jax.sharding import PartitionSpec as P

HIGHEST = lax.Precision.HIGHEST
HIGH = lax.Precision.HIGH
CONTRACT = (((0,), (0,)), ((), ()))
MESH_ID = pl.DeviceIdType.MESH
LANES = 128
SUB = 8


def allreduce_kernel(nx, ny, x_ref, o_ref, recv_a, p_t, recv_b, recv_c, recv_d,
                     sa, ra, sb, rb, sc, rc, sd, rd):
    h = lax.axis_index("gx")
    a = lax.axis_index("gy")
    nb, rows = x_ref.shape[0], x_ref.shape[1]
    kb = rows // SUB
    nt = nb * kb

    barrier = pltpu.get_barrier_semaphore()

    def signal_y(j, carry):
        pl.semaphore_signal(barrier, 1, device_id=(h, lax.rem(a + j, ny)),
                            device_id_type=MESH_ID)
        return carry

    def signal_x(j, carry):
        pl.semaphore_signal(barrier, 1, device_id=(lax.rem(h + j, nx), a),
                            device_id_type=MESH_ID)
        return carry

    lax.fori_loop(1, ny, signal_y, 0)
    lax.fori_loop(1, nx, signal_x, 0)
    pl.semaphore_wait(barrier, (ny - 1) + (nx - 1))

    def copy_a(peer, slot_src):
        return pltpu.make_async_remote_copy(
            src_ref=x_ref.at[:, :, pl.ds(pl.multiple_of(peer * LANES, LANES), LANES)],
            dst_ref=recv_a.at[slot_src],
            send_sem=sa.at[peer],
            recv_sem=ra.at[slot_src],
            device_id=(h, peer),
            device_id_type=MESH_ID,
        )

    def start_a(j, carry):
        copy_a(lax.rem(a + j, ny), a).start()
        return carry

    lax.fori_loop(1, ny, start_a, 0)
    recv_a[a] = x_ref[:, :, pl.ds(pl.multiple_of(a * LANES, LANES), LANES)]

    def wait_a(j, carry):
        copy_a(lax.rem(a + j, ny), a).wait_send()
        copy_a(a, lax.rem(a + j, ny)).wait_recv()
        return carry

    lax.fori_loop(1, ny, wait_a, 0)
    part = jnp.sum(recv_a[...], axis=0)
    for u in range(nt):
        p_t[u] = part[u // kb, (u % kb) * SUB:(u % kb + 1) * SUB, :]

    def copy_b(peer, slot_src, tile):
        return pltpu.make_async_remote_copy(
            src_ref=p_t.at[tile],
            dst_ref=recv_b.at[slot_src],
            send_sem=sb.at[peer],
            recv_sem=rb.at[slot_src],
            device_id=(peer, a),
            device_id_type=MESH_ID,
        )

    def start_b(j, carry):
        peer = lax.rem(h + j, nx)
        copy_b(peer, h, lax.rem(peer, nt)).start()
        return carry

    lax.fori_loop(1, nx, start_b, 0)
    own = lax.rem(h, nt)
    recv_b[h] = p_t[own]

    def wait_b(j, carry):
        peer = lax.rem(h + j, nx)
        copy_b(peer, h, lax.rem(peer, nt)).wait_send()
        copy_b(h, peer, own).wait_recv()
        return carry

    lax.fori_loop(1, nx, wait_b, 0)
    recv_c[own] = jnp.sum(recv_b[...], axis=0)

    base = h - own

    def copy_c(peer_tile, slot_tile):
        return pltpu.make_async_remote_copy(
            src_ref=recv_c.at[slot_tile],
            dst_ref=recv_c.at[slot_tile],
            send_sem=sc.at[peer_tile],
            recv_sem=rc.at[slot_tile],
            device_id=(base + peer_tile, a),
            device_id_type=MESH_ID,
        )

    def start_c(j, carry):
        copy_c(lax.rem(own + j, nt), own).start()
        return carry

    lax.fori_loop(1, nt, start_c, 0)

    def wait_c(j, carry):
        other = lax.rem(own + j, nt)
        copy_c(other, own).wait_send()
        copy_c(own, other).wait_recv()
        return carry

    lax.fori_loop(1, nt, wait_c, 0)
    for u in range(nt):
        recv_d[a, u // kb, (u % kb) * SUB:(u % kb + 1) * SUB, :] = recv_c[u]

    def copy_d(peer, slot_src):
        return pltpu.make_async_remote_copy(
            src_ref=recv_d.at[slot_src],
            dst_ref=recv_d.at[slot_src],
            send_sem=sd.at[peer],
            recv_sem=rd.at[slot_src],
            device_id=(h, peer),
            device_id_type=MESH_ID,
        )

    def start_d(j, carry):
        copy_d(lax.rem(a + j, ny), a).start()
        return carry

    lax.fori_loop(1, ny, start_d, 0)

    def wait_d(j, carry):
        copy_d(lax.rem(a + j, ny), a).wait_send()
        copy_d(a, lax.rem(a + j, ny)).wait_recv()
        return carry

    lax.fori_loop(1, ny, wait_d, 0)
    for s in range(ny):
        o_ref[:, :, s * LANES:(s + 1) * LANES] = recv_d[s]


def allreduce(x, nx, ny, collective_id):
    nb, rows, cols = x.shape
    assert cols == ny * LANES and rows % SUB == 0
    nt = nb * (rows // SUB)
    assert nx % nt == 0
    vmem = pltpu.VMEM
    return pl.pallas_call(
        functools.partial(allreduce_kernel, nx, ny),
        out_shape=jax.ShapeDtypeStruct(x.shape, jnp.float32),
        in_specs=[pl.BlockSpec(memory_space=vmem)],
        out_specs=pl.BlockSpec(memory_space=vmem),
        scratch_shapes=[
            vmem((ny, nb, rows, LANES), jnp.float32),
            vmem((nt, SUB, LANES), jnp.float32),
            vmem((nx, SUB, LANES), jnp.float32),
            vmem((nt, SUB, LANES), jnp.float32),
            vmem((ny, nb, rows, LANES), jnp.float32),
            pltpu.SemaphoreType.DMA((ny,)),
            pltpu.SemaphoreType.DMA((ny,)),
            pltpu.SemaphoreType.DMA((nx,)),
            pltpu.SemaphoreType.DMA((nx,)),
            pltpu.SemaphoreType.DMA((nt,)),
            pltpu.SemaphoreType.DMA((nt,)),
            pltpu.SemaphoreType.DMA((ny,)),
            pltpu.SemaphoreType.DMA((ny,)),
        ],
        compiler_params=pltpu.CompilerParams(
            collective_id=collective_id, has_side_effects=True
        ),
    )(x)


def gram_of(factor_rows):
    return jnp.einsum("bki,bli->bkl", factor_rows, factor_rows, precision=HIGHEST)


def solve_rows(gram_matrix, factor_rows):
    width = gram_matrix.shape[-1]
    identity = jnp.eye(width, dtype=jnp.float32)
    trace_value = jnp.trace(gram_matrix, axis1=1, axis2=2)
    shift_value = 1e-06 * (trace_value / width + 1.0)
    lower_factor = jnp.linalg.cholesky(gram_matrix + shift_value[:, None, None] * identity)
    return lax.linalg.triangular_solve(lower_factor, factor_rows, left_side=True, lower=True)


def on_device(nx, ny, normed, grad_query, grad_key, error, start_factor):
    replicas = nx * ny
    query_grad = lax.dot_general(normed, grad_query, CONTRACT, preferred_element_type=jnp.float32)
    key_grad = lax.dot_general(normed, grad_key, CONTRACT, preferred_element_type=jnp.float32)
    merged = jnp.stack([query_grad, key_grad]) + error.astype(jnp.float32)
    left_local = jnp.einsum("bkj,bij->bki", start_factor, merged, precision=HIGHEST)
    left_total = allreduce(left_local, nx, ny, 0)
    left_rows = solve_rows(gram_of(left_total), left_total)
    right_local = jnp.einsum("bki,bij->bkj", left_rows, merged, precision=HIGH)
    right_rows = allreduce(right_local, nx, ny, 1) / replicas
    approx = jnp.einsum("bki,bkj->bij", left_rows, right_rows, precision=HIGH)
    return ((merged - approx).astype(jnp.bfloat16), left_rows, right_rows)


def solution(mesh):
    nx, ny = mesh.shape["gx"], mesh.shape["gy"]
    placed = (
        P(("gx", "gy"), None),
        P(("gx", "gy"), None),
        P(("gx", "gy"), None),
        P(("gx", "gy"), None, None),
        P(),
    )
    return jax.shard_map(
        functools.partial(on_device, nx, ny),
        mesh=mesh,
        in_specs=placed,
        out_specs=(P(("gx", "gy"), None, None), P(), P()),
        check_vma=False,
    )
```

```python
import functools

import jax
import jax.numpy as jnp
from jax import lax
from jax.experimental import pallas as pl
from jax.experimental.pallas import tpu as pltpu
from jax.sharding import PartitionSpec as P

HIGHEST = lax.Precision.HIGHEST
HIGH = lax.Precision.HIGH
CONTRACT = (((0,), (0,)), ((), ()))
MESH_ID = pl.DeviceIdType.MESH
LANES = 128
SUB = 8


def allreduce_kernel(nx, ny, orthonormalize, x_ref, o_ref, recv_a, p_t, recv_b, recv_c, recv_d,
                     sa, ra, sb, rb, sc, rc, sd, rd):
    h = lax.axis_index("gx")
    a = lax.axis_index("gy")
    nb, rows = x_ref.shape[0], x_ref.shape[1]
    kb = rows // SUB
    nt = nb * kb

    barrier = pltpu.get_barrier_semaphore()

    def signal_y(j, carry):
        pl.semaphore_signal(barrier, 1, device_id=(h, lax.rem(a + j, ny)),
                            device_id_type=MESH_ID)
        return carry

    def signal_x(j, carry):
        pl.semaphore_signal(barrier, 1, device_id=(lax.rem(h + j, nx), a),
                            device_id_type=MESH_ID)
        return carry

    lax.fori_loop(1, ny, signal_y, 0)
    lax.fori_loop(1, nx, signal_x, 0)
    pl.semaphore_wait(barrier, (ny - 1) + (nx - 1))

    def copy_a(peer, slot_src):
        return pltpu.make_async_remote_copy(
            src_ref=x_ref.at[:, :, pl.ds(pl.multiple_of(peer * LANES, LANES), LANES)],
            dst_ref=recv_a.at[slot_src],
            send_sem=sa.at[peer],
            recv_sem=ra.at[slot_src],
            device_id=(h, peer),
            device_id_type=MESH_ID,
        )

    def start_a(j, carry):
        copy_a(lax.rem(a + j, ny), a).start()
        return carry

    lax.fori_loop(1, ny, start_a, 0)
    recv_a[a] = x_ref[:, :, pl.ds(pl.multiple_of(a * LANES, LANES), LANES)]

    def wait_a(j, carry):
        copy_a(lax.rem(a + j, ny), a).wait_send()
        copy_a(a, lax.rem(a + j, ny)).wait_recv()
        return carry

    lax.fori_loop(1, ny, wait_a, 0)
    part = jnp.sum(recv_a[...], axis=0)
    for u in range(nt):
        p_t[u] = part[u // kb, (u % kb) * SUB:(u % kb + 1) * SUB, :]

    def copy_b(peer, slot_src, tile):
        return pltpu.make_async_remote_copy(
            src_ref=p_t.at[tile],
            dst_ref=recv_b.at[slot_src],
            send_sem=sb.at[peer],
            recv_sem=rb.at[slot_src],
            device_id=(peer, a),
            device_id_type=MESH_ID,
        )

    def start_b(j, carry):
        peer = lax.rem(h + j, nx)
        copy_b(peer, h, lax.rem(peer, nt)).start()
        return carry

    lax.fori_loop(1, nx, start_b, 0)
    own = lax.rem(h, nt)
    recv_b[h] = p_t[own]

    def wait_b(j, carry):
        peer = lax.rem(h + j, nx)
        copy_b(peer, h, lax.rem(peer, nt)).wait_send()
        copy_b(h, peer, own).wait_recv()
        return carry

    lax.fori_loop(1, nx, wait_b, 0)
    recv_c[own] = jnp.sum(recv_b[...], axis=0)

    base = h - own

    def copy_c(peer_tile, slot_tile):
        return pltpu.make_async_remote_copy(
            src_ref=recv_c.at[slot_tile],
            dst_ref=recv_c.at[slot_tile],
            send_sem=sc.at[peer_tile],
            recv_sem=rc.at[slot_tile],
            device_id=(base + peer_tile, a),
            device_id_type=MESH_ID,
        )

    def start_c(j, carry):
        copy_c(lax.rem(own + j, nt), own).start()
        return carry

    lax.fori_loop(1, nt, start_c, 0)

    def wait_c(j, carry):
        other = lax.rem(own + j, nt)
        copy_c(other, own).wait_send()
        copy_c(own, other).wait_recv()
        return carry

    lax.fori_loop(1, nt, wait_c, 0)
    for u in range(nt):
        recv_d[a, u // kb, (u % kb) * SUB:(u % kb + 1) * SUB, :] = recv_c[u]

    def copy_d(peer, slot_src):
        return pltpu.make_async_remote_copy(
            src_ref=recv_d.at[slot_src],
            dst_ref=recv_d.at[slot_src],
            send_sem=sd.at[peer],
            recv_sem=rd.at[slot_src],
            device_id=(h, peer),
            device_id_type=MESH_ID,
        )

    def start_d(j, carry):
        copy_d(lax.rem(a + j, ny), a).start()
        return carry

    lax.fori_loop(1, ny, start_d, 0)

    def wait_d(j, carry):
        copy_d(lax.rem(a + j, ny), a).wait_send()
        copy_d(a, lax.rem(a + j, ny)).wait_recv()
        return carry

    lax.fori_loop(1, ny, wait_d, 0)
    for s in range(ny):
        o_ref[:, :, s * LANES:(s + 1) * LANES] = recv_d[s]
    if orthonormalize:
        for b in range(nb):
            orthonormal_rows(o_ref.at[b])


def orthonormal_rows(rows_ref):
    k = rows_ref.shape[0]
    rows = rows_ref[...]
    gram = lax.dot_general(rows, rows, (((1,), (1,)), ((), ())),
                           precision=HIGHEST, preferred_element_type=jnp.float32)
    r_idx = lax.broadcasted_iota(jnp.int32, (k, k), 0)
    c_idx = lax.broadcasted_iota(jnp.int32, (k, k), 1)
    diag = r_idx == c_idx
    trace_value = jnp.sum(jnp.where(diag, gram, 0.0))
    shift_value = 1e-06 * (trace_value / k + 1.0)
    work = gram + jnp.where(diag, shift_value, 0.0)
    cols, pivots = [], []
    for j in range(k):
        pivot = jnp.sum(jnp.where(diag & (r_idx == j), work, 0.0))
        root = jnp.sqrt(pivot)
        col = jnp.sum(jnp.where(c_idx == j, work, 0.0), axis=1, keepdims=True)
        row = jnp.sum(jnp.where(r_idx == j, work, 0.0), axis=0, keepdims=True)
        col = jnp.where(r_idx[:, :1] >= j, col / root, 0.0)
        row = jnp.where(c_idx[:1, :] >= j, row / root, 0.0)
        work = work - col * row
        cols.append(col)
        pivots.append(root)
    sub_idx = lax.broadcasted_iota(jnp.int32, (k, 1), 0)
    for i in range(k):
        solved = rows_ref[i:i + 1, :] / pivots[i]
        rows_ref[i:i + 1, :] = solved
        if i + 1 < k:
            start = ((i + 1) // SUB) * SUB
            below = jnp.where(sub_idx[start:] > i, cols[i][start:], 0.0)
            rows_ref[start:, :] = rows_ref[start:, :] - below * solved


def allreduce(x, nx, ny, collective_id, orthonormalize=False):
    nb, rows, cols = x.shape
    assert cols == ny * LANES and rows % SUB == 0
    nt = nb * (rows // SUB)
    assert nx % nt == 0
    vmem = pltpu.VMEM
    return pl.pallas_call(
        functools.partial(allreduce_kernel, nx, ny, orthonormalize),
        out_shape=jax.ShapeDtypeStruct(x.shape, jnp.float32),
        in_specs=[pl.BlockSpec(memory_space=vmem)],
        out_specs=pl.BlockSpec(memory_space=vmem),
        scratch_shapes=[
            vmem((ny, nb, rows, LANES), jnp.float32),
            vmem((nt, SUB, LANES), jnp.float32),
            vmem((nx, SUB, LANES), jnp.float32),
            vmem((nt, SUB, LANES), jnp.float32),
            vmem((ny, nb, rows, LANES), jnp.float32),
            pltpu.SemaphoreType.DMA((ny,)),
            pltpu.SemaphoreType.DMA((ny,)),
            pltpu.SemaphoreType.DMA((nx,)),
            pltpu.SemaphoreType.DMA((nx,)),
            pltpu.SemaphoreType.DMA((nt,)),
            pltpu.SemaphoreType.DMA((nt,)),
            pltpu.SemaphoreType.DMA((ny,)),
            pltpu.SemaphoreType.DMA((ny,)),
        ],
        compiler_params=pltpu.CompilerParams(
            collective_id=collective_id, has_side_effects=True
        ),
    )(x)


def gram_of(factor_rows):
    return jnp.einsum("bki,bli->bkl", factor_rows, factor_rows, precision=HIGHEST)


def solve_rows(gram_matrix, factor_rows):
    width = gram_matrix.shape[-1]
    identity = jnp.eye(width, dtype=jnp.float32)
    trace_value = jnp.trace(gram_matrix, axis1=1, axis2=2)
    shift_value = 1e-06 * (trace_value / width + 1.0)
    lower_factor = jnp.linalg.cholesky(gram_matrix + shift_value[:, None, None] * identity)
    return lax.linalg.triangular_solve(lower_factor, factor_rows, left_side=True, lower=True)


def on_device(nx, ny, normed, grad_query, grad_key, error, start_factor):
    replicas = nx * ny
    query_grad = lax.dot_general(normed, grad_query, CONTRACT, preferred_element_type=jnp.float32)
    key_grad = lax.dot_general(normed, grad_key, CONTRACT, preferred_element_type=jnp.float32)
    merged = jnp.stack([query_grad, key_grad]) + error.astype(jnp.float32)
    left_local = jnp.einsum("bkj,bij->bki", start_factor, merged, precision=HIGHEST)
    left_rows = allreduce(left_local, nx, ny, 0, orthonormalize=True)
    right_local = jnp.einsum("bki,bij->bkj", left_rows, merged, precision=HIGH)
    right_rows = allreduce(right_local, nx, ny, 1) / replicas
    approx = jnp.einsum("bki,bkj->bij", left_rows, right_rows, precision=HIGH)
    return ((merged - approx).astype(jnp.bfloat16), left_rows, right_rows)


def solution(mesh):
    nx, ny = mesh.shape["gx"], mesh.shape["gy"]
    placed = (
        P(("gx", "gy"), None),
        P(("gx", "gy"), None),
        P(("gx", "gy"), None),
        P(("gx", "gy"), None, None),
        P(),
    )
    return jax.shard_map(
        functools.partial(on_device, nx, ny),
        mesh=mesh,
        in_specs=placed,
        out_specs=(P(("gx", "gy"), None, None), P(), P()),
        check_vma=False,
    )
```

```python
import functools

import jax
import jax.numpy as jnp
from jax import lax
from jax.experimental import pallas as pl
from jax.experimental.pallas import tpu as pltpu
from jax.sharding import PartitionSpec as P

HIGHEST = lax.Precision.HIGHEST
HIGH = lax.Precision.HIGH
CONTRACT = (((0,), (0,)), ((), ()))
MESH_ID = pl.DeviceIdType.MESH
LANES = 128
SUB = 8


def allreduce_kernel(nx, ny, orthonormalize, x_ref, o_ref, recv_a, p_t, recv_b, recv_c, recv_d,
                     sa, ra, sb, rb, sc, rc, sd, rd):
    h = lax.axis_index("gx")
    a = lax.axis_index("gy")
    nb, rows = x_ref.shape[0], x_ref.shape[1]
    kb = rows // SUB
    nt = nb * kb

    barrier = pltpu.get_barrier_semaphore()

    def signal_y(j, carry):
        pl.semaphore_signal(barrier, 1, device_id=(h, lax.rem(a + j, ny)),
                            device_id_type=MESH_ID)
        return carry

    def signal_x(j, carry):
        pl.semaphore_signal(barrier, 1, device_id=(lax.rem(h + j, nx), a),
                            device_id_type=MESH_ID)
        return carry

    lax.fori_loop(1, ny, signal_y, 0)
    lax.fori_loop(1, nx, signal_x, 0)
    pl.semaphore_wait(barrier, (ny - 1) + (nx - 1))

    def copy_a(peer, slot_src):
        return pltpu.make_async_remote_copy(
            src_ref=x_ref.at[:, :, pl.ds(pl.multiple_of(peer * LANES, LANES), LANES)],
            dst_ref=recv_a.at[slot_src],
            send_sem=sa.at[peer],
            recv_sem=ra.at[slot_src],
            device_id=(h, peer),
            device_id_type=MESH_ID,
        )

    def start_a(j, carry):
        copy_a(lax.rem(a + j, ny), a).start()
        return carry

    lax.fori_loop(1, ny, start_a, 0)
    recv_a[a] = x_ref[:, :, pl.ds(pl.multiple_of(a * LANES, LANES), LANES)]

    def wait_a(j, carry):
        copy_a(lax.rem(a + j, ny), a).wait_send()
        copy_a(a, lax.rem(a + j, ny)).wait_recv()
        return carry

    lax.fori_loop(1, ny, wait_a, 0)
    part = jnp.sum(recv_a[...], axis=0)
    for u in range(nt):
        p_t[u] = part[u // kb, (u % kb) * SUB:(u % kb + 1) * SUB, :]

    def copy_b(peer, slot_src, tile):
        return pltpu.make_async_remote_copy(
            src_ref=p_t.at[tile],
            dst_ref=recv_b.at[slot_src],
            send_sem=sb.at[peer],
            recv_sem=rb.at[slot_src],
            device_id=(peer, a),
            device_id_type=MESH_ID,
        )

    def start_b(j, carry):
        peer = lax.rem(h + j, nx)
        copy_b(peer, h, lax.rem(peer, nt)).start()
        return carry

    lax.fori_loop(1, nx, start_b, 0)
    own = lax.rem(h, nt)
    recv_b[h] = p_t[own]

    def wait_b(j, carry):
        peer = lax.rem(h + j, nx)
        copy_b(peer, h, lax.rem(peer, nt)).wait_send()
        copy_b(h, peer, own).wait_recv()
        return carry

    lax.fori_loop(1, nx, wait_b, 0)
    recv_c[own] = jnp.sum(recv_b[...], axis=0)

    base = h - own

    def copy_c(peer_tile, slot_tile):
        return pltpu.make_async_remote_copy(
            src_ref=recv_c.at[slot_tile],
            dst_ref=recv_c.at[slot_tile],
            send_sem=sc.at[peer_tile],
            recv_sem=rc.at[slot_tile],
            device_id=(base + peer_tile, a),
            device_id_type=MESH_ID,
        )

    def start_c(j, carry):
        copy_c(lax.rem(own + j, nt), own).start()
        return carry

    lax.fori_loop(1, nt, start_c, 0)

    def wait_c(j, carry):
        other = lax.rem(own + j, nt)
        copy_c(other, own).wait_send()
        copy_c(own, other).wait_recv()
        return carry

    lax.fori_loop(1, nt, wait_c, 0)
    for u in range(nt):
        recv_d[a, u // kb, (u % kb) * SUB:(u % kb + 1) * SUB, :] = recv_c[u]

    def copy_d(peer, slot_src):
        return pltpu.make_async_remote_copy(
            src_ref=recv_d.at[slot_src],
            dst_ref=recv_d.at[slot_src],
            send_sem=sd.at[peer],
            recv_sem=rd.at[slot_src],
            device_id=(h, peer),
            device_id_type=MESH_ID,
        )

    def start_d(j, carry):
        copy_d(lax.rem(a + j, ny), a).start()
        return carry

    lax.fori_loop(1, ny, start_d, 0)

    def wait_d(j, carry):
        copy_d(lax.rem(a + j, ny), a).wait_send()
        copy_d(a, lax.rem(a + j, ny)).wait_recv()
        return carry

    lax.fori_loop(1, ny, wait_d, 0)
    for s in range(ny):
        o_ref[:, :, s * LANES:(s + 1) * LANES] = recv_d[s]
    if orthonormalize:
        for b in range(nb):
            orthonormal_rows(o_ref.at[b])


def orthonormal_rows(rows_ref):
    k = rows_ref.shape[0]
    rows = rows_ref[...]
    gram = lax.dot_general(rows, rows, (((1,), (1,)), ((), ())),
                           precision=HIGHEST, preferred_element_type=jnp.float32)
    r_idx = lax.broadcasted_iota(jnp.int32, (k, k), 0)
    c_idx = lax.broadcasted_iota(jnp.int32, (k, k), 1)
    diag = r_idx == c_idx
    trace_value = jnp.sum(jnp.where(diag, gram, 0.0))
    shift_value = 1e-06 * (trace_value / k + 1.0)
    work = gram + jnp.where(diag, shift_value, 0.0)
    sub_idx = r_idx[:, :1]
    inverse = jnp.where(diag, 1.0, 0.0)
    for j in range(k):
        row = work[j:j + 1, :]
        root = jnp.sqrt(row[:, j:j + 1])
        col = jnp.sum(jnp.where(c_idx == j, work, 0.0), axis=1, keepdims=True)
        col = jnp.where(sub_idx >= j, col / root, 0.0)
        row = jnp.where(c_idx[:1, :] >= j, row / root, 0.0)
        work = work - col * row
        solved = inverse[j:j + 1, :] / root
        below = jnp.where(sub_idx > j, col, 0.0)
        inverse = jnp.where(sub_idx == j, solved, inverse - below * solved)
    rows_ref[...] = jnp.dot(inverse, rows, precision=HIGHEST,
                            preferred_element_type=jnp.float32)


def allreduce(x, nx, ny, collective_id, orthonormalize=False):
    nb, rows, cols = x.shape
    assert cols == ny * LANES and rows % SUB == 0
    nt = nb * (rows // SUB)
    assert nx % nt == 0
    vmem = pltpu.VMEM
    return pl.pallas_call(
        functools.partial(allreduce_kernel, nx, ny, orthonormalize),
        out_shape=jax.ShapeDtypeStruct(x.shape, jnp.float32),
        in_specs=[pl.BlockSpec(memory_space=vmem)],
        out_specs=pl.BlockSpec(memory_space=vmem),
        scratch_shapes=[
            vmem((ny, nb, rows, LANES), jnp.float32),
            vmem((nt, SUB, LANES), jnp.float32),
            vmem((nx, SUB, LANES), jnp.float32),
            vmem((nt, SUB, LANES), jnp.float32),
            vmem((ny, nb, rows, LANES), jnp.float32),
            pltpu.SemaphoreType.DMA((ny,)),
            pltpu.SemaphoreType.DMA((ny,)),
            pltpu.SemaphoreType.DMA((nx,)),
            pltpu.SemaphoreType.DMA((nx,)),
            pltpu.SemaphoreType.DMA((nt,)),
            pltpu.SemaphoreType.DMA((nt,)),
            pltpu.SemaphoreType.DMA((ny,)),
            pltpu.SemaphoreType.DMA((ny,)),
        ],
        compiler_params=pltpu.CompilerParams(
            collective_id=collective_id, has_side_effects=True
        ),
    )(x)


def gram_of(factor_rows):
    return jnp.einsum("bki,bli->bkl", factor_rows, factor_rows, precision=HIGHEST)


def solve_rows(gram_matrix, factor_rows):
    width = gram_matrix.shape[-1]
    identity = jnp.eye(width, dtype=jnp.float32)
    trace_value = jnp.trace(gram_matrix, axis1=1, axis2=2)
    shift_value = 1e-06 * (trace_value / width + 1.0)
    lower_factor = jnp.linalg.cholesky(gram_matrix + shift_value[:, None, None] * identity)
    return lax.linalg.triangular_solve(lower_factor, factor_rows, left_side=True, lower=True)


def on_device(nx, ny, normed, grad_query, grad_key, error, start_factor):
    replicas = nx * ny
    query_grad = lax.dot_general(normed, grad_query, CONTRACT, preferred_element_type=jnp.float32)
    key_grad = lax.dot_general(normed, grad_key, CONTRACT, preferred_element_type=jnp.float32)
    merged = jnp.stack([query_grad, key_grad]) + error.astype(jnp.float32)
    left_local = jnp.einsum("bkj,bij->bki", start_factor, merged, precision=HIGHEST)
    left_rows = allreduce(left_local, nx, ny, 0, orthonormalize=True)
    right_local = jnp.einsum("bki,bij->bkj", left_rows, merged, precision=HIGH)
    right_rows = allreduce(right_local, nx, ny, 1) / replicas
    approx = jnp.einsum("bki,bkj->bij", left_rows, right_rows, precision=HIGH)
    return ((merged - approx).astype(jnp.bfloat16), left_rows, right_rows)


def solution(mesh):
    nx, ny = mesh.shape["gx"], mesh.shape["gy"]
    placed = (
        P(("gx", "gy"), None),
        P(("gx", "gy"), None),
        P(("gx", "gy"), None),
        P(("gx", "gy"), None, None),
        P(),
    )
    return jax.shard_map(
        functools.partial(on_device, nx, ny),
        mesh=mesh,
        in_specs=placed,
        out_specs=(P(("gx", "gy"), None, None), P(), P()),
        check_vma=False,
    )
```

```python
import functools

import jax
import jax.numpy as jnp
from jax import lax
from jax.experimental import pallas as pl
from jax.experimental.pallas import tpu as pltpu
from jax.sharding import PartitionSpec as P

HIGHEST = lax.Precision.HIGHEST
HIGH = lax.Precision.HIGH
CONTRACT = (((0,), (0,)), ((), ()))
MESH_ID = pl.DeviceIdType.MESH
LANES = 128
SUB = 8


def allreduce_kernel(nx, ny, orthonormalize, x_ref, o_ref, recv_a, p_t, recv_b, recv_c, recv_d,
                     sa, ra, sb, rb, sc, rc, sd, rd):
    h = lax.axis_index("gx")
    a = lax.axis_index("gy")
    nb, rows = x_ref.shape[0], x_ref.shape[1]
    kb = rows // SUB
    nt = nb * kb

    barrier = pltpu.get_barrier_semaphore()

    def signal_y(j, carry):
        pl.semaphore_signal(barrier, 1, device_id=(h, lax.rem(a + j, ny)),
                            device_id_type=MESH_ID)
        return carry

    def signal_x(j, carry):
        pl.semaphore_signal(barrier, 1, device_id=(lax.rem(h + j, nx), a),
                            device_id_type=MESH_ID)
        return carry

    lax.fori_loop(1, ny, signal_y, 0)
    lax.fori_loop(1, nx, signal_x, 0)
    pl.semaphore_wait(barrier, (ny - 1) + (nx - 1))

    def copy_a(peer, slot_src):
        return pltpu.make_async_remote_copy(
            src_ref=x_ref.at[:, :, pl.ds(pl.multiple_of(peer * LANES, LANES), LANES)],
            dst_ref=recv_a.at[slot_src],
            send_sem=sa.at[peer],
            recv_sem=ra.at[slot_src],
            device_id=(h, peer),
            device_id_type=MESH_ID,
        )

    def start_a(j, carry):
        copy_a(lax.rem(a + j, ny), a).start()
        return carry

    lax.fori_loop(1, ny, start_a, 0)
    recv_a[a] = x_ref[:, :, pl.ds(pl.multiple_of(a * LANES, LANES), LANES)]

    def wait_a(j, carry):
        copy_a(lax.rem(a + j, ny), a).wait_send()
        copy_a(a, lax.rem(a + j, ny)).wait_recv()
        return carry

    lax.fori_loop(1, ny, wait_a, 0)
    part = jnp.sum(recv_a[...], axis=0)
    for u in range(nt):
        p_t[u] = part[u // kb, (u % kb) * SUB:(u % kb + 1) * SUB, :]

    def copy_b(peer, slot_src, tile):
        return pltpu.make_async_remote_copy(
            src_ref=p_t.at[tile],
            dst_ref=recv_b.at[slot_src],
            send_sem=sb.at[peer],
            recv_sem=rb.at[slot_src],
            device_id=(peer, a),
            device_id_type=MESH_ID,
        )

    def start_b(j, carry):
        peer = lax.rem(h + j, nx)
        copy_b(peer, h, lax.rem(peer, nt)).start()
        return carry

    lax.fori_loop(1, nx, start_b, 0)
    own = lax.rem(h, nt)
    recv_b[h] = p_t[own]

    def wait_b(j, carry):
        peer = lax.rem(h + j, nx)
        copy_b(peer, h, lax.rem(peer, nt)).wait_send()
        copy_b(h, peer, own).wait_recv()
        return carry

    lax.fori_loop(1, nx, wait_b, 0)
    recv_c[own] = jnp.sum(recv_b[...], axis=0)

    base = h - own

    def copy_c(peer_tile, slot_tile):
        return pltpu.make_async_remote_copy(
            src_ref=recv_c.at[slot_tile],
            dst_ref=recv_c.at[slot_tile],
            send_sem=sc.at[peer_tile],
            recv_sem=rc.at[slot_tile],
            device_id=(base + peer_tile, a),
            device_id_type=MESH_ID,
        )

    def start_c(j, carry):
        copy_c(lax.rem(own + j, nt), own).start()
        return carry

    lax.fori_loop(1, nt, start_c, 0)

    def wait_c(j, carry):
        other = lax.rem(own + j, nt)
        copy_c(other, own).wait_send()
        copy_c(own, other).wait_recv()
        return carry

    lax.fori_loop(1, nt, wait_c, 0)
    for u in range(nt):
        recv_d[a, u // kb, (u % kb) * SUB:(u % kb + 1) * SUB, :] = recv_c[u]

    def copy_d(peer, slot_src):
        return pltpu.make_async_remote_copy(
            src_ref=recv_d.at[slot_src],
            dst_ref=recv_d.at[slot_src],
            send_sem=sd.at[peer],
            recv_sem=rd.at[slot_src],
            device_id=(h, peer),
            device_id_type=MESH_ID,
        )

    def start_d(j, carry):
        copy_d(lax.rem(a + j, ny), a).start()
        return carry

    lax.fori_loop(1, ny, start_d, 0)

    def wait_d(j, carry):
        copy_d(lax.rem(a + j, ny), a).wait_send()
        copy_d(a, lax.rem(a + j, ny)).wait_recv()
        return carry

    lax.fori_loop(1, ny, wait_d, 0)
    for s in range(ny):
        o_ref[:, :, s * LANES:(s + 1) * LANES] = recv_d[s]
    if orthonormalize:
        orthonormal_rows(o_ref)


def orthonormal_rows(rows_ref):
    nb, k = rows_ref.shape[0], rows_ref.shape[1]
    gram = jnp.stack([
        lax.dot_general(rows_ref[b], rows_ref[b], (((1,), (1,)), ((), ())),
                        precision=HIGHEST, preferred_element_type=jnp.float32)
        for b in range(nb)
    ])
    r_idx = lax.broadcasted_iota(jnp.int32, (nb, k, k), 1)
    c_idx = lax.broadcasted_iota(jnp.int32, (nb, k, k), 2)
    diag = r_idx == c_idx
    trace_value = jnp.sum(jnp.sum(jnp.where(diag, gram, 0.0), axis=2, keepdims=True),
                          axis=1, keepdims=True)
    shift_value = 1e-06 * (trace_value / k + 1.0)
    work = gram + jnp.where(diag, shift_value, 0.0)
    sub_idx = r_idx[:, :, :1]
    lane_idx = c_idx[:, :1, :]
    inverse = jnp.where(diag, 1.0, 0.0)
    for j in range(k):
        row = work[:, j:j + 1, :]
        inv_root = lax.rsqrt(row[:, :, j:j + 1])
        col = jnp.where(sub_idx >= j, work[:, :, j:j + 1] * inv_root, 0.0)
        row = jnp.where(lane_idx >= j, row * inv_root, 0.0)
        work = work - col * row
        solved = inverse[:, j:j + 1, :] * inv_root
        below = jnp.where(sub_idx > j, col, 0.0)
        inverse = jnp.where(sub_idx == j, solved, inverse - below * solved)
    for b in range(nb):
        rows_ref[b] = jnp.dot(inverse[b], rows_ref[b], precision=HIGHEST,
                              preferred_element_type=jnp.float32)


def allreduce(x, nx, ny, collective_id, orthonormalize=False):
    nb, rows, cols = x.shape
    assert cols == ny * LANES and rows % SUB == 0
    nt = nb * (rows // SUB)
    assert nx % nt == 0
    vmem = pltpu.VMEM
    return pl.pallas_call(
        functools.partial(allreduce_kernel, nx, ny, orthonormalize),
        out_shape=jax.ShapeDtypeStruct(x.shape, jnp.float32),
        in_specs=[pl.BlockSpec(memory_space=vmem)],
        out_specs=pl.BlockSpec(memory_space=vmem),
        scratch_shapes=[
            vmem((ny, nb, rows, LANES), jnp.float32),
            vmem((nt, SUB, LANES), jnp.float32),
            vmem((nx, SUB, LANES), jnp.float32),
            vmem((nt, SUB, LANES), jnp.float32),
            vmem((ny, nb, rows, LANES), jnp.float32),
            pltpu.SemaphoreType.DMA((ny,)),
            pltpu.SemaphoreType.DMA((ny,)),
            pltpu.SemaphoreType.DMA((nx,)),
            pltpu.SemaphoreType.DMA((nx,)),
            pltpu.SemaphoreType.DMA((nt,)),
            pltpu.SemaphoreType.DMA((nt,)),
            pltpu.SemaphoreType.DMA((ny,)),
            pltpu.SemaphoreType.DMA((ny,)),
        ],
        compiler_params=pltpu.CompilerParams(
            collective_id=collective_id, has_side_effects=True
        ),
    )(x)


def gram_of(factor_rows):
    return jnp.einsum("bki,bli->bkl", factor_rows, factor_rows, precision=HIGHEST)


def solve_rows(gram_matrix, factor_rows):
    width = gram_matrix.shape[-1]
    identity = jnp.eye(width, dtype=jnp.float32)
    trace_value = jnp.trace(gram_matrix, axis1=1, axis2=2)
    shift_value = 1e-06 * (trace_value / width + 1.0)
    lower_factor = jnp.linalg.cholesky(gram_matrix + shift_value[:, None, None] * identity)
    return lax.linalg.triangular_solve(lower_factor, factor_rows, left_side=True, lower=True)


def on_device(nx, ny, normed, grad_query, grad_key, error, start_factor):
    replicas = nx * ny
    query_grad = lax.dot_general(normed, grad_query, CONTRACT, preferred_element_type=jnp.float32)
    key_grad = lax.dot_general(normed, grad_key, CONTRACT, preferred_element_type=jnp.float32)
    merged = jnp.stack([query_grad, key_grad]) + error.astype(jnp.float32)
    left_local = jnp.einsum("bkj,bij->bki", start_factor, merged, precision=HIGHEST)
    left_rows = allreduce(left_local, nx, ny, 0, orthonormalize=True)
    right_local = jnp.einsum("bki,bij->bkj", left_rows, merged, precision=HIGH)
    right_rows = allreduce(right_local, nx, ny, 1) / replicas
    approx = jnp.einsum("bki,bkj->bij", left_rows, right_rows, precision=HIGH)
    return ((merged - approx).astype(jnp.bfloat16), left_rows, right_rows)


def solution(mesh):
    nx, ny = mesh.shape["gx"], mesh.shape["gy"]
    placed = (
        P(("gx", "gy"), None),
        P(("gx", "gy"), None),
        P(("gx", "gy"), None),
        P(("gx", "gy"), None, None),
        P(),
    )
    return jax.shard_map(
        functools.partial(on_device, nx, ny),
        mesh=mesh,
        in_specs=placed,
        out_specs=(P(("gx", "gy"), None, None), P(), P()),
        check_vma=False,
    )
```

```python
import functools

import jax
import jax.numpy as jnp
from jax import lax
from jax.experimental import pallas as pl
from jax.experimental.pallas import tpu as pltpu
from jax.sharding import PartitionSpec as P

HIGHEST = lax.Precision.HIGHEST
HIGH = lax.Precision.HIGH
CONTRACT = (((0,), (0,)), ((), ()))
MESH_ID = pl.DeviceIdType.MESH
LANES = 128
SUB = 8


def allreduce_kernel(nx, ny, orthonormalize, divisor, x_ref, o_ref, recv_a, p_t, recv_b, q_t,
                     final, sa, ra, sb, rb, se, re):
    h = lax.axis_index("gx")
    a = lax.axis_index("gy")
    nb, rows = x_ref.shape[0], x_ref.shape[1]
    kb = rows // SUB
    nt = nb * kb

    barrier = pltpu.get_barrier_semaphore()

    def signal_y(j, carry):
        pl.semaphore_signal(barrier, 1, device_id=(h, lax.rem(a + j, ny)),
                            device_id_type=MESH_ID)
        return carry

    def signal_x(j, carry):
        pl.semaphore_signal(barrier, 1, device_id=(lax.rem(h + j, nx), a),
                            device_id_type=MESH_ID)
        return carry

    own = lax.rem(h, nt)
    base = h - own

    def signal_xy(i, carry):
        peer_x = base + lax.rem(own + 1 + i // (ny - 1), nt)
        peer_y = lax.rem(a + 1 + lax.rem(i, ny - 1), ny)
        pl.semaphore_signal(barrier, 1, device_id=(peer_x, peer_y),
                            device_id_type=MESH_ID)
        return carry

    lax.fori_loop(1, ny, signal_y, 0)
    lax.fori_loop(1, nx, signal_x, 0)
    lax.fori_loop(0, (nt - 1) * (ny - 1), signal_xy, 0)
    pl.semaphore_wait(barrier, (ny - 1) + (nx - 1) + (nt - 1) * (ny - 1))

    def copy_a(peer, slot_src):
        return pltpu.make_async_remote_copy(
            src_ref=x_ref.at[:, :, pl.ds(pl.multiple_of(peer * LANES, LANES), LANES)],
            dst_ref=recv_a.at[slot_src],
            send_sem=sa.at[peer],
            recv_sem=ra.at[slot_src],
            device_id=(h, peer),
            device_id_type=MESH_ID,
        )

    def start_a(j, carry):
        copy_a(lax.rem(a + j, ny), a).start()
        return carry

    lax.fori_loop(1, ny, start_a, 0)
    recv_a[a] = x_ref[:, :, pl.ds(pl.multiple_of(a * LANES, LANES), LANES)]

    def wait_a(j, carry):
        copy_a(lax.rem(a + j, ny), a).wait_send()
        copy_a(a, lax.rem(a + j, ny)).wait_recv()
        return carry

    lax.fori_loop(1, ny, wait_a, 0)
    part = jnp.sum(recv_a[...], axis=0)
    for u in range(nt):
        p_t[u] = part[u // kb, (u % kb) * SUB:(u % kb + 1) * SUB, :]

    def copy_b(peer, slot_src, tile):
        return pltpu.make_async_remote_copy(
            src_ref=p_t.at[tile],
            dst_ref=recv_b.at[slot_src],
            send_sem=sb.at[peer],
            recv_sem=rb.at[slot_src],
            device_id=(peer, a),
            device_id_type=MESH_ID,
        )

    def start_b(j, carry):
        peer = lax.rem(h + j, nx)
        copy_b(peer, h, lax.rem(peer, nt)).start()
        return carry

    lax.fori_loop(1, nx, start_b, 0)
    recv_b[h] = p_t[own]

    def wait_b(j, carry):
        peer = lax.rem(h + j, nx)
        copy_b(peer, h, lax.rem(peer, nt)).wait_send()
        copy_b(h, peer, own).wait_recv()
        return carry

    lax.fori_loop(1, nx, wait_b, 0)
    q_t[...] = jnp.sum(recv_b[...], axis=0)

    block = nt * ny
    mine = a * nt + own

    def copy_e(dest, slot):
        return pltpu.make_async_remote_copy(
            src_ref=q_t,
            dst_ref=final.at[slot // nt, lax.rem(slot, nt)],
            send_sem=se.at[dest],
            recv_sem=re.at[slot],
            device_id=(base + lax.rem(dest, nt), dest // nt),
            device_id_type=MESH_ID,
        )

    def start_e(i, carry):
        copy_e(lax.rem(mine + i, block), mine).start()
        return carry

    lax.fori_loop(1, block, start_e, 0)
    final[a, own] = q_t[...]

    def wait_e(i, carry):
        other = lax.rem(mine + i, block)
        copy_e(other, mine).wait_send()
        copy_e(mine, other).wait_recv()
        return carry

    lax.fori_loop(1, block, wait_e, 0)
    for s in range(ny):
        for u in range(nt):
            tile = final[s, u]
            if divisor is not None:
                tile = tile / divisor
            o_ref[u // kb, (u % kb) * SUB:(u % kb + 1) * SUB, s * LANES:(s + 1) * LANES] = tile
    if orthonormalize:
        orthonormal_rows(o_ref)


def orthonormal_rows(rows_ref):
    nb, k = rows_ref.shape[0], rows_ref.shape[1]
    gram = jnp.stack([
        lax.dot_general(rows_ref[b], rows_ref[b], (((1,), (1,)), ((), ())),
                        precision=HIGHEST, preferred_element_type=jnp.float32)
        for b in range(nb)
    ])
    r_idx = lax.broadcasted_iota(jnp.int32, (nb, k, k), 1)
    c_idx = lax.broadcasted_iota(jnp.int32, (nb, k, k), 2)
    diag = r_idx == c_idx
    trace_value = jnp.sum(jnp.sum(jnp.where(diag, gram, 0.0), axis=2, keepdims=True),
                          axis=1, keepdims=True)
    shift_value = 1e-06 * (trace_value / k + 1.0)
    work = gram + jnp.where(diag, shift_value, 0.0)
    sub_idx = r_idx[:, :, :1]
    lane_idx = c_idx[:, :1, :]
    inverse = jnp.where(diag, 1.0, 0.0)
    for j in range(k):
        row = work[:, j:j + 1, :]
        inv_root = lax.rsqrt(row[:, :, j:j + 1])
        col = jnp.where(sub_idx >= j, work[:, :, j:j + 1] * inv_root, 0.0)
        row = jnp.where(lane_idx >= j, row * inv_root, 0.0)
        work = work - col * row
        solved = inverse[:, j:j + 1, :] * inv_root
        below = jnp.where(sub_idx > j, col, 0.0)
        inverse = jnp.where(sub_idx == j, solved, inverse - below * solved)
    for b in range(nb):
        rows_ref[b] = jnp.dot(inverse[b], rows_ref[b], precision=HIGHEST,
                              preferred_element_type=jnp.float32)


def allreduce(x, nx, ny, collective_id, orthonormalize=False, divisor=None):
    nb, rows, cols = x.shape
    assert cols == ny * LANES and rows % SUB == 0
    nt = nb * (rows // SUB)
    assert nx % nt == 0
    vmem = pltpu.VMEM
    return pl.pallas_call(
        functools.partial(allreduce_kernel, nx, ny, orthonormalize, divisor),
        out_shape=jax.ShapeDtypeStruct(x.shape, jnp.float32),
        in_specs=[pl.BlockSpec(memory_space=vmem)],
        out_specs=pl.BlockSpec(memory_space=vmem),
        scratch_shapes=[
            vmem((ny, nb, rows, LANES), jnp.float32),
            vmem((nt, SUB, LANES), jnp.float32),
            vmem((nx, SUB, LANES), jnp.float32),
            vmem((SUB, LANES), jnp.float32),
            vmem((ny, nt, SUB, LANES), jnp.float32),
            pltpu.SemaphoreType.DMA((ny,)),
            pltpu.SemaphoreType.DMA((ny,)),
            pltpu.SemaphoreType.DMA((nx,)),
            pltpu.SemaphoreType.DMA((nx,)),
            pltpu.SemaphoreType.DMA((nt * ny,)),
            pltpu.SemaphoreType.DMA((nt * ny,)),
        ],
        compiler_params=pltpu.CompilerParams(
            collective_id=collective_id, has_side_effects=True
        ),
    )(x)


def gram_of(factor_rows):
    return jnp.einsum("bki,bli->bkl", factor_rows, factor_rows, precision=HIGHEST)


def solve_rows(gram_matrix, factor_rows):
    width = gram_matrix.shape[-1]
    identity = jnp.eye(width, dtype=jnp.float32)
    trace_value = jnp.trace(gram_matrix, axis1=1, axis2=2)
    shift_value = 1e-06 * (trace_value / width + 1.0)
    lower_factor = jnp.linalg.cholesky(gram_matrix + shift_value[:, None, None] * identity)
    return lax.linalg.triangular_solve(lower_factor, factor_rows, left_side=True, lower=True)


def on_device(nx, ny, normed, grad_query, grad_key, error, start_factor):
    replicas = nx * ny
    query_grad = lax.dot_general(normed, grad_query, CONTRACT, preferred_element_type=jnp.float32)
    key_grad = lax.dot_general(normed, grad_key, CONTRACT, preferred_element_type=jnp.float32)
    merged = jnp.stack([query_grad, key_grad]) + error.astype(jnp.float32)
    left_local = jnp.einsum("bkj,bij->bki", start_factor, merged, precision=HIGHEST)
    left_rows = allreduce(left_local, nx, ny, 0, orthonormalize=True)
    right_local = jnp.einsum("bki,bij->bkj", left_rows, merged, precision=HIGH)
    right_rows = allreduce(right_local, nx, ny, 1, divisor=float(replicas))
    approx = jnp.einsum("bki,bkj->bij", left_rows, right_rows, precision=HIGH)
    return ((merged - approx).astype(jnp.bfloat16), left_rows, right_rows)


def solution(mesh):
    nx, ny = mesh.shape["gx"], mesh.shape["gy"]
    placed = (
        P(("gx", "gy"), None),
        P(("gx", "gy"), None),
        P(("gx", "gy"), None),
        P(("gx", "gy"), None, None),
        P(),
    )
    return jax.shard_map(
        functools.partial(on_device, nx, ny),
        mesh=mesh,
        in_specs=placed,
        out_specs=(P(("gx", "gy"), None, None), P(), P()),
        check_vma=False,
    )
```

```python
import functools

import jax
import jax.numpy as jnp
from jax import lax
from jax.experimental import pallas as pl
from jax.experimental.pallas import tpu as pltpu
from jax.sharding import PartitionSpec as P

HIGHEST = lax.Precision.HIGHEST
HIGH = lax.Precision.HIGH
CONTRACT = (((0,), (0,)), ((), ()))
MESH_ID = pl.DeviceIdType.MESH
LANES = 128
SUB = 8


def allreduce_kernel(nx, ny, orthonormalize, x_ref, o_ref, recv_a, p_t, recv_b, recv_c, recv_d,
                     sa, ra, sb, rb, sc, rc, sd, rd):
    h = lax.axis_index("gx")
    a = lax.axis_index("gy")
    nb, rows = x_ref.shape[0], x_ref.shape[1]
    kb = rows // SUB
    nt = nb * kb

    barrier = pltpu.get_barrier_semaphore()

    def signal_y(j, carry):
        pl.semaphore_signal(barrier, 1, device_id=(h, lax.rem(a + j, ny)),
                            device_id_type=MESH_ID)
        return carry

    def signal_x(j, carry):
        pl.semaphore_signal(barrier, 1, device_id=(lax.rem(h + j, nx), a),
                            device_id_type=MESH_ID)
        return carry

    lax.fori_loop(1, ny, signal_y, 0)
    lax.fori_loop(1, nx, signal_x, 0)
    pl.semaphore_wait(barrier, (ny - 1) + (nx - 1))

    def copy_a(peer, slot_src):
        return pltpu.make_async_remote_copy(
            src_ref=x_ref.at[:, :, pl.ds(pl.multiple_of(peer * LANES, LANES), LANES)],
            dst_ref=recv_a.at[slot_src],
            send_sem=sa.at[peer],
            recv_sem=ra.at[slot_src],
            device_id=(h, peer),
            device_id_type=MESH_ID,
        )

    def start_a(j, carry):
        copy_a(lax.rem(a + j, ny), a).start()
        return carry

    lax.fori_loop(1, ny, start_a, 0)
    recv_a[a] = x_ref[:, :, pl.ds(pl.multiple_of(a * LANES, LANES), LANES)]

    def wait_a(j, carry):
        copy_a(lax.rem(a + j, ny), a).wait_send()
        copy_a(a, lax.rem(a + j, ny)).wait_recv()
        return carry

    lax.fori_loop(1, ny, wait_a, 0)
    part = jnp.sum(recv_a[...], axis=0)
    for u in range(nt):
        p_t[u] = part[u // kb, (u % kb) * SUB:(u % kb + 1) * SUB, :]

    def copy_b(peer, slot_src, tile):
        return pltpu.make_async_remote_copy(
            src_ref=p_t.at[tile],
            dst_ref=recv_b.at[slot_src],
            send_sem=sb.at[peer],
            recv_sem=rb.at[slot_src],
            device_id=(peer, a),
            device_id_type=MESH_ID,
        )

    def start_b(j, carry):
        peer = lax.rem(h + j, nx)
        copy_b(peer, h, lax.rem(peer, nt)).start()
        return carry

    lax.fori_loop(1, nx, start_b, 0)
    own = lax.rem(h, nt)
    recv_b[h] = p_t[own]

    def wait_b(j, carry):
        peer = lax.rem(h + j, nx)
        copy_b(peer, h, lax.rem(peer, nt)).wait_send()
        copy_b(h, peer, own).wait_recv()
        return carry

    lax.fori_loop(1, nx, wait_b, 0)
    recv_c[own] = jnp.sum(recv_b[...], axis=0)

    base = h - own

    def copy_c(peer_tile, slot_tile):
        return pltpu.make_async_remote_copy(
            src_ref=recv_c.at[slot_tile],
            dst_ref=recv_c.at[slot_tile],
            send_sem=sc.at[peer_tile],
            recv_sem=rc.at[slot_tile],
            device_id=(base + peer_tile, a),
            device_id_type=MESH_ID,
        )

    def start_c(j, carry):
        copy_c(lax.rem(own + j, nt), own).start()
        return carry

    lax.fori_loop(1, nt, start_c, 0)

    def wait_c(j, carry):
        other = lax.rem(own + j, nt)
        copy_c(other, own).wait_send()
        copy_c(own, other).wait_recv()
        return carry

    lax.fori_loop(1, nt, wait_c, 0)
    for u in range(nt):
        recv_d[a, u // kb, (u % kb) * SUB:(u % kb + 1) * SUB, :] = recv_c[u]

    def copy_d(peer, slot_src):
        return pltpu.make_async_remote_copy(
            src_ref=recv_d.at[slot_src],
            dst_ref=recv_d.at[slot_src],
            send_sem=sd.at[peer],
            recv_sem=rd.at[slot_src],
            device_id=(h, peer),
            device_id_type=MESH_ID,
        )

    def start_d(j, carry):
        copy_d(lax.rem(a + j, ny), a).start()
        return carry

    lax.fori_loop(1, ny, start_d, 0)

    def wait_d(j, carry):
        copy_d(lax.rem(a + j, ny), a).wait_send()
        copy_d(a, lax.rem(a + j, ny)).wait_recv()
        return carry

    lax.fori_loop(1, ny, wait_d, 0)
    for s in range(ny):
        o_ref[:, :, s * LANES:(s + 1) * LANES] = recv_d[s]
    if orthonormalize:
        orthonormal_rows(o_ref)


def orthonormal_rows(rows_ref):
    nb, k = rows_ref.shape[0], rows_ref.shape[1]
    gram = jnp.stack([
        lax.dot_general(rows_ref[b], rows_ref[b], (((1,), (1,)), ((), ())),
                        precision=HIGHEST, preferred_element_type=jnp.float32)
        for b in range(nb)
    ])
    r_idx = lax.broadcasted_iota(jnp.int32, (nb, k, k), 1)
    c_idx = lax.broadcasted_iota(jnp.int32, (nb, k, k), 2)
    diag = r_idx == c_idx
    trace_value = jnp.sum(jnp.sum(jnp.where(diag, gram, 0.0), axis=2, keepdims=True),
                          axis=1, keepdims=True)
    shift_value = 1e-06 * (trace_value / k + 1.0)
    work = gram + jnp.where(diag, shift_value, 0.0)
    sub_idx = r_idx[:, :, :1]
    lane_idx = c_idx[:, :1, :]
    inverse = jnp.where(diag, 1.0, 0.0)
    for j in range(k):
        row = work[:, j:j + 1, :]
        inv_root = lax.rsqrt(row[:, :, j:j + 1])
        col = jnp.where(sub_idx >= j, work[:, :, j:j + 1] * inv_root, 0.0)
        row = jnp.where(lane_idx >= j, row * inv_root, 0.0)
        work = work - col * row
        solved = inverse[:, j:j + 1, :] * inv_root
        below = jnp.where(sub_idx > j, col, 0.0)
        inverse = jnp.where(sub_idx == j, solved, inverse - below * solved)
    for b in range(nb):
        rows_ref[b] = jnp.dot(inverse[b], rows_ref[b], precision=HIGHEST,
                              preferred_element_type=jnp.float32)


def allreduce(x, nx, ny, collective_id, orthonormalize=False):
    nb, rows, cols = x.shape
    assert cols == ny * LANES and rows % SUB == 0
    nt = nb * (rows // SUB)
    assert nx % nt == 0
    vmem = pltpu.VMEM
    return pl.pallas_call(
        functools.partial(allreduce_kernel, nx, ny, orthonormalize),
        out_shape=jax.ShapeDtypeStruct(x.shape, jnp.float32),
        in_specs=[pl.BlockSpec(memory_space=vmem)],
        out_specs=pl.BlockSpec(memory_space=vmem),
        scratch_shapes=[
            vmem((ny, nb, rows, LANES), jnp.float32),
            vmem((nt, SUB, LANES), jnp.float32),
            vmem((nx, SUB, LANES), jnp.float32),
            vmem((nt, SUB, LANES), jnp.float32),
            vmem((ny, nb, rows, LANES), jnp.float32),
            pltpu.SemaphoreType.DMA((ny,)),
            pltpu.SemaphoreType.DMA((ny,)),
            pltpu.SemaphoreType.DMA((nx,)),
            pltpu.SemaphoreType.DMA((nx,)),
            pltpu.SemaphoreType.DMA((nt,)),
            pltpu.SemaphoreType.DMA((nt,)),
            pltpu.SemaphoreType.DMA((ny,)),
            pltpu.SemaphoreType.DMA((ny,)),
        ],
        compiler_params=pltpu.CompilerParams(
            collective_id=collective_id, has_side_effects=True
        ),
    )(x)


def gram_of(factor_rows):
    return jnp.einsum("bki,bli->bkl", factor_rows, factor_rows, precision=HIGHEST)


def solve_rows(gram_matrix, factor_rows):
    width = gram_matrix.shape[-1]
    identity = jnp.eye(width, dtype=jnp.float32)
    trace_value = jnp.trace(gram_matrix, axis1=1, axis2=2)
    shift_value = 1e-06 * (trace_value / width + 1.0)
    lower_factor = jnp.linalg.cholesky(gram_matrix + shift_value[:, None, None] * identity)
    return lax.linalg.triangular_solve(lower_factor, factor_rows, left_side=True, lower=True)


def on_device(nx, ny, normed, grad_query, grad_key, error, start_factor):
    replicas = nx * ny
    query_grad = lax.dot_general(normed, grad_query, CONTRACT, preferred_element_type=jnp.float32)
    key_grad = lax.dot_general(normed, grad_key, CONTRACT, preferred_element_type=jnp.float32)
    merged = jnp.stack([query_grad, key_grad]) + error.astype(jnp.float32)
    m_hi, m_mid, m_lo = split3(merged)
    s_hi, s_mid, s_lo = split3(start_factor)
    left_local = combine6(*rows_times(
        [[s_hi, s_mid, s_lo], [s_hi, s_mid], [s_hi]], [m_hi, m_mid, m_lo], "bkj,bij->bki"))
    left_rows = allreduce(left_local, nx, ny, 0, orthonormalize=True)
    l_hi, l_mid, l_lo = split3(left_rows)
    first, second = rows_times([[l_hi, l_mid], [l_hi]], [m_hi, m_mid], "bki,bij->bkj")
    right_local = first[0] + (first[1] + second[0])
    right_rows = allreduce(right_local, nx, ny, 1) / replicas
    r_hi, r_mid, r_lo = split3(right_rows)
    lefts = jnp.concatenate([l_hi, l_hi, l_mid, l_hi, l_mid, l_lo], axis=1)
    rights = jnp.concatenate([r_hi, r_mid, r_hi, r_lo, r_mid, r_hi], axis=1)
    approx = jnp.einsum("bki,bkj->bij", lefts, rights, preferred_element_type=jnp.float32)
    return ((merged - approx).astype(jnp.bfloat16), left_rows, right_rows)


def split3(x):
    hi = lax.reduce_precision(x, exponent_bits=8, mantissa_bits=7)
    rest = x - hi
    mid = lax.reduce_precision(rest, exponent_bits=8, mantissa_bits=7)
    lo = rest - mid
    return (hi.astype(jnp.bfloat16), mid.astype(jnp.bfloat16), lo.astype(jnp.bfloat16))


def rows_times(row_groups, big_pieces, spec):
    out = []
    for group, big in zip(row_groups, big_pieces):
        k = group[0].shape[1]
        prod = jnp.einsum(spec, jnp.concatenate(group, axis=1), big,
                          preferred_element_type=jnp.float32)
        out.append([prod[:, g * k:(g + 1) * k] for g in range(len(group))])
    return out


def combine6(first, second, third):
    small = (first[2] + second[1]) + third[0]
    return first[0] + ((first[1] + second[0]) + small)


def solution(mesh):
    nx, ny = mesh.shape["gx"], mesh.shape["gy"]
    placed = (
        P(("gx", "gy"), None),
        P(("gx", "gy"), None),
        P(("gx", "gy"), None),
        P(("gx", "gy"), None, None),
        P(),
    )
    return jax.shard_map(
        functools.partial(on_device, nx, ny),
        mesh=mesh,
        in_specs=placed,
        out_specs=(P(("gx", "gy"), None, None), P(), P()),
        check_vma=False,
    )
```

```python
import functools

import jax
import jax.numpy as jnp
from jax import lax
from jax.experimental import pallas as pl
from jax.experimental.pallas import tpu as pltpu
from jax.sharding import PartitionSpec as P

HIGHEST = lax.Precision.HIGHEST
HIGH = lax.Precision.HIGH
CONTRACT = (((0,), (0,)), ((), ()))
MESH_ID = pl.DeviceIdType.MESH
LANES = 128
SUB = 8


def allreduce_kernel(nx, ny, orthonormalize, divisor, patterns, x_ref, o_ref, *refs):
    stacked = refs[:len(patterns)]
    allreduce_body(nx, ny, orthonormalize, divisor, x_ref, o_ref, *refs[len(patterns):])
    for b in range(o_ref.shape[0]):
        value = o_ref[b]
        k = value.shape[0]
        hi = value.astype(jnp.bfloat16)
        rest = value - hi.astype(jnp.float32)
        mid = rest.astype(jnp.bfloat16)
        lo = (rest - mid.astype(jnp.float32)).astype(jnp.bfloat16)
        parts = (hi, mid, lo)
        for pattern, out_ref in zip(patterns, stacked):
            for g, piece in enumerate(pattern):
                out_ref[b, g * k:(g + 1) * k, :] = parts[piece]


def allreduce_body(nx, ny, orthonormalize, divisor, x_ref, o_ref, recv_a, p_t, recv_b, recv_c, recv_d,
                     sa, ra, sb, rb, sc, rc, sd, rd):
    h = lax.axis_index("gx")
    a = lax.axis_index("gy")
    nb, rows = x_ref.shape[0], x_ref.shape[1]
    kb = rows // SUB
    nt = nb * kb

    barrier = pltpu.get_barrier_semaphore()

    def signal_y(j, carry):
        pl.semaphore_signal(barrier, 1, device_id=(h, lax.rem(a + j, ny)),
                            device_id_type=MESH_ID)
        return carry

    def signal_x(j, carry):
        pl.semaphore_signal(barrier, 1, device_id=(lax.rem(h + j, nx), a),
                            device_id_type=MESH_ID)
        return carry

    lax.fori_loop(1, ny, signal_y, 0)
    lax.fori_loop(1, nx, signal_x, 0)
    pl.semaphore_wait(barrier, (ny - 1) + (nx - 1))

    def copy_a(peer, slot_src):
        return pltpu.make_async_remote_copy(
            src_ref=x_ref.at[:, :, pl.ds(pl.multiple_of(peer * LANES, LANES), LANES)],
            dst_ref=recv_a.at[slot_src],
            send_sem=sa.at[peer],
            recv_sem=ra.at[slot_src],
            device_id=(h, peer),
            device_id_type=MESH_ID,
        )

    def start_a(j, carry):
        copy_a(lax.rem(a + j, ny), a).start()
        return carry

    lax.fori_loop(1, ny, start_a, 0)
    recv_a[a] = x_ref[:, :, pl.ds(pl.multiple_of(a * LANES, LANES), LANES)]

    def wait_a(j, carry):
        copy_a(lax.rem(a + j, ny), a).wait_send()
        copy_a(a, lax.rem(a + j, ny)).wait_recv()
        return carry

    lax.fori_loop(1, ny, wait_a, 0)
    part = jnp.sum(recv_a[...], axis=0)
    for u in range(nt):
        p_t[u] = part[u // kb, (u % kb) * SUB:(u % kb + 1) * SUB, :]

    def copy_b(peer, slot_src, tile):
        return pltpu.make_async_remote_copy(
            src_ref=p_t.at[tile],
            dst_ref=recv_b.at[slot_src],
            send_sem=sb.at[peer],
            recv_sem=rb.at[slot_src],
            device_id=(peer, a),
            device_id_type=MESH_ID,
        )

    def start_b(j, carry):
        peer = lax.rem(h + j, nx)
        copy_b(peer, h, lax.rem(peer, nt)).start()
        return carry

    lax.fori_loop(1, nx, start_b, 0)
    own = lax.rem(h, nt)
    recv_b[h] = p_t[own]

    def wait_b(j, carry):
        peer = lax.rem(h + j, nx)
        copy_b(peer, h, lax.rem(peer, nt)).wait_send()
        copy_b(h, peer, own).wait_recv()
        return carry

    lax.fori_loop(1, nx, wait_b, 0)
    recv_c[own] = jnp.sum(recv_b[...], axis=0)

    base = h - own

    def copy_c(peer_tile, slot_tile):
        return pltpu.make_async_remote_copy(
            src_ref=recv_c.at[slot_tile],
            dst_ref=recv_c.at[slot_tile],
            send_sem=sc.at[peer_tile],
            recv_sem=rc.at[slot_tile],
            device_id=(base + peer_tile, a),
            device_id_type=MESH_ID,
        )

    def start_c(j, carry):
        copy_c(lax.rem(own + j, nt), own).start()
        return carry

    lax.fori_loop(1, nt, start_c, 0)

    def wait_c(j, carry):
        other = lax.rem(own + j, nt)
        copy_c(other, own).wait_send()
        copy_c(own, other).wait_recv()
        return carry

    lax.fori_loop(1, nt, wait_c, 0)
    for u in range(nt):
        recv_d[a, u // kb, (u % kb) * SUB:(u % kb + 1) * SUB, :] = recv_c[u]

    def copy_d(peer, slot_src):
        return pltpu.make_async_remote_copy(
            src_ref=recv_d.at[slot_src],
            dst_ref=recv_d.at[slot_src],
            send_sem=sd.at[peer],
            recv_sem=rd.at[slot_src],
            device_id=(h, peer),
            device_id_type=MESH_ID,
        )

    def start_d(j, carry):
        copy_d(lax.rem(a + j, ny), a).start()
        return carry

    lax.fori_loop(1, ny, start_d, 0)

    def wait_d(j, carry):
        copy_d(lax.rem(a + j, ny), a).wait_send()
        copy_d(a, lax.rem(a + j, ny)).wait_recv()
        return carry

    lax.fori_loop(1, ny, wait_d, 0)
    for s in range(ny):
        block = recv_d[s]
        if divisor is not None:
            block = block / divisor
        o_ref[:, :, s * LANES:(s + 1) * LANES] = block
    if orthonormalize:
        orthonormal_rows(o_ref)


def orthonormal_rows(rows_ref):
    nb, k = rows_ref.shape[0], rows_ref.shape[1]
    gram = jnp.stack([
        lax.dot_general(rows_ref[b], rows_ref[b], (((1,), (1,)), ((), ())),
                        precision=HIGHEST, preferred_element_type=jnp.float32)
        for b in range(nb)
    ])
    r_idx = lax.broadcasted_iota(jnp.int32, (nb, k, k), 1)
    c_idx = lax.broadcasted_iota(jnp.int32, (nb, k, k), 2)
    diag = r_idx == c_idx
    trace_value = jnp.sum(jnp.sum(jnp.where(diag, gram, 0.0), axis=2, keepdims=True),
                          axis=1, keepdims=True)
    shift_value = 1e-06 * (trace_value / k + 1.0)
    work = gram + jnp.where(diag, shift_value, 0.0)
    sub_idx = r_idx[:, :, :1]
    lane_idx = c_idx[:, :1, :]
    inverse = jnp.where(diag, 1.0, 0.0)
    for j in range(k):
        row = work[:, j:j + 1, :]
        inv_root = lax.rsqrt(row[:, :, j:j + 1])
        col = jnp.where(sub_idx >= j, work[:, :, j:j + 1] * inv_root, 0.0)
        row = jnp.where(lane_idx >= j, row * inv_root, 0.0)
        work = work - col * row
        solved = inverse[:, j:j + 1, :] * inv_root
        below = jnp.where(sub_idx > j, col, 0.0)
        inverse = jnp.where(sub_idx == j, solved, inverse - below * solved)
    for b in range(nb):
        rows_ref[b] = jnp.dot(inverse[b], rows_ref[b], precision=HIGHEST,
                              preferred_element_type=jnp.float32)


def allreduce(x, nx, ny, collective_id, orthonormalize=False, divisor=None, patterns=()):
    nb, rows, cols = x.shape
    assert cols == ny * LANES and rows % SUB == 0
    nt = nb * (rows // SUB)
    assert nx % nt == 0
    vmem = pltpu.VMEM
    return pl.pallas_call(
        functools.partial(allreduce_kernel, nx, ny, orthonormalize, divisor, patterns),
        out_shape=[jax.ShapeDtypeStruct(x.shape, jnp.float32)] + [
            jax.ShapeDtypeStruct((nb, len(p) * rows, cols), jnp.bfloat16) for p in patterns],
        in_specs=[pl.BlockSpec(memory_space=vmem)],
        out_specs=[pl.BlockSpec(memory_space=vmem)] * (1 + len(patterns)),
        scratch_shapes=[
            vmem((ny, nb, rows, LANES), jnp.float32),
            vmem((nt, SUB, LANES), jnp.float32),
            vmem((nx, SUB, LANES), jnp.float32),
            vmem((nt, SUB, LANES), jnp.float32),
            vmem((ny, nb, rows, LANES), jnp.float32),
            pltpu.SemaphoreType.DMA((ny,)),
            pltpu.SemaphoreType.DMA((ny,)),
            pltpu.SemaphoreType.DMA((nx,)),
            pltpu.SemaphoreType.DMA((nx,)),
            pltpu.SemaphoreType.DMA((nt,)),
            pltpu.SemaphoreType.DMA((nt,)),
            pltpu.SemaphoreType.DMA((ny,)),
            pltpu.SemaphoreType.DMA((ny,)),
        ],
        compiler_params=pltpu.CompilerParams(
            collective_id=collective_id, has_side_effects=True
        ),
    )(x)


def gram_of(factor_rows):
    return jnp.einsum("bki,bli->bkl", factor_rows, factor_rows, precision=HIGHEST)


def solve_rows(gram_matrix, factor_rows):
    width = gram_matrix.shape[-1]
    identity = jnp.eye(width, dtype=jnp.float32)
    trace_value = jnp.trace(gram_matrix, axis1=1, axis2=2)
    shift_value = 1e-06 * (trace_value / width + 1.0)
    lower_factor = jnp.linalg.cholesky(gram_matrix + shift_value[:, None, None] * identity)
    return lax.linalg.triangular_solve(lower_factor, factor_rows, left_side=True, lower=True)


def on_device(nx, ny, normed, grad_query, grad_key, error, start_factor):
    replicas = nx * ny
    query_grad = lax.dot_general(normed, grad_query, CONTRACT, preferred_element_type=jnp.float32)
    key_grad = lax.dot_general(normed, grad_key, CONTRACT, preferred_element_type=jnp.float32)
    merged = jnp.stack([query_grad, key_grad]) + error.astype(jnp.float32)
    m_hi, m_mid, m_lo = split3(merged)
    s_hi, s_mid, s_lo = split3(start_factor)
    left_local = combine6(*rows_times(
        [[s_hi, s_mid, s_lo], [s_hi, s_mid], [s_hi]], [m_hi, m_mid, m_lo], "bkj,bij->bki"))
    left_rows, lefts, left_pair = allreduce(
        left_local, nx, ny, 0, orthonormalize=True, patterns=((0, 0, 1, 0, 1, 2), (0, 1)))
    k = left_rows.shape[1]
    pair = jnp.einsum("bki,bij->bkj", left_pair, m_hi, preferred_element_type=jnp.float32)
    cross = jnp.einsum("bki,bij->bkj", lefts[:, :k], m_mid, preferred_element_type=jnp.float32)
    right_local = pair[:, :k] + (pair[:, k:] + cross)
    right_rows, rights = allreduce(
        right_local, nx, ny, 1, divisor=float(replicas), patterns=((0, 1, 0, 2, 1, 0),))
    approx = jnp.einsum("bki,bkj->bij", lefts, rights, preferred_element_type=jnp.float32)
    return ((merged - approx).astype(jnp.bfloat16), left_rows, right_rows)


def split3(x):
    hi = lax.reduce_precision(x, exponent_bits=8, mantissa_bits=7)
    rest = x - hi
    mid = lax.reduce_precision(rest, exponent_bits=8, mantissa_bits=7)
    lo = rest - mid
    return (hi.astype(jnp.bfloat16), mid.astype(jnp.bfloat16), lo.astype(jnp.bfloat16))


def rows_times(row_groups, big_pieces, spec):
    out = []
    for group, big in zip(row_groups, big_pieces):
        k = group[0].shape[1]
        prod = jnp.einsum(spec, jnp.concatenate(group, axis=1), big,
                          preferred_element_type=jnp.float32)
        out.append([prod[:, g * k:(g + 1) * k] for g in range(len(group))])
    return out


def combine6(first, second, third):
    small = (first[2] + second[1]) + third[0]
    return first[0] + ((first[1] + second[0]) + small)


def solution(mesh):
    nx, ny = mesh.shape["gx"], mesh.shape["gy"]
    placed = (
        P(("gx", "gy"), None),
        P(("gx", "gy"), None),
        P(("gx", "gy"), None),
        P(("gx", "gy"), None, None),
        P(),
    )
    return jax.shard_map(
        functools.partial(on_device, nx, ny),
        mesh=mesh,
        in_specs=placed,
        out_specs=(P(("gx", "gy"), None, None), P(), P()),
        check_vma=False,
    )
```

```python
import functools

import jax
import jax.numpy as jnp
from jax import lax
from jax.experimental import pallas as pl
from jax.experimental.pallas import tpu as pltpu
from jax.sharding import PartitionSpec as P

HIGHEST = lax.Precision.HIGHEST
HIGH = lax.Precision.HIGH
CONTRACT = (((0,), (0,)), ((), ()))
MESH_ID = pl.DeviceIdType.MESH
LANES = 128
SUB = 8


def allreduce_kernel(nx, ny, orthonormalize, divisor, patterns, x_ref, o_ref, *refs):
    stacked = refs[:len(patterns)]
    allreduce_body(nx, ny, orthonormalize, divisor, x_ref, o_ref, *refs[len(patterns):])
    for b in range(o_ref.shape[0]):
        value = o_ref[b]
        k = value.shape[0]
        hi = value.astype(jnp.bfloat16)
        rest = value - hi.astype(jnp.float32)
        mid = rest.astype(jnp.bfloat16)
        lo = (rest - mid.astype(jnp.float32)).astype(jnp.bfloat16)
        parts = (hi, mid, lo)
        for pattern, out_ref in zip(patterns, stacked):
            for g, piece in enumerate(pattern):
                out_ref[b, g * k:(g + 1) * k, :] = parts[piece]


def allreduce_body(nx, ny, orthonormalize, divisor, x_ref, o_ref, recv_a, p_t, recv_b, recv_c, recv_d,
                     sa, ra, sb, rb, sc, rc, sd, rd):
    h = lax.axis_index("gx")
    a = lax.axis_index("gy")
    nb, rows = x_ref.shape[0], x_ref.shape[1]
    kb = rows // SUB
    nt = nb * kb

    barrier = pltpu.get_barrier_semaphore()

    def signal_y(j, carry):
        pl.semaphore_signal(barrier, 1, device_id=(h, lax.rem(a + j, ny)),
                            device_id_type=MESH_ID)
        return carry

    def signal_x(j, carry):
        pl.semaphore_signal(barrier, 1, device_id=(lax.rem(h + j, nx), a),
                            device_id_type=MESH_ID)
        return carry

    lax.fori_loop(1, ny, signal_y, 0)
    lax.fori_loop(1, nx, signal_x, 0)
    pl.semaphore_wait(barrier, (ny - 1) + (nx - 1))

    def copy_a(peer, slot_src):
        return pltpu.make_async_remote_copy(
            src_ref=x_ref.at[:, :, pl.ds(pl.multiple_of(peer * LANES, LANES), LANES)],
            dst_ref=recv_a.at[slot_src],
            send_sem=sa.at[peer],
            recv_sem=ra.at[slot_src],
            device_id=(h, peer),
            device_id_type=MESH_ID,
        )

    def start_a(j, carry):
        copy_a(lax.rem(a + j, ny), a).start()
        return carry

    lax.fori_loop(1, ny, start_a, 0)
    recv_a[a] = x_ref[:, :, pl.ds(pl.multiple_of(a * LANES, LANES), LANES)]

    def wait_a(j, carry):
        copy_a(lax.rem(a + j, ny), a).wait_send()
        copy_a(a, lax.rem(a + j, ny)).wait_recv()
        return carry

    lax.fori_loop(1, ny, wait_a, 0)
    part = jnp.sum(recv_a[...], axis=0)
    for u in range(nt):
        p_t[u] = part[u // kb, (u % kb) * SUB:(u % kb + 1) * SUB, :]

    def copy_b(peer, slot_src, tile):
        return pltpu.make_async_remote_copy(
            src_ref=p_t.at[tile],
            dst_ref=recv_b.at[slot_src],
            send_sem=sb.at[peer],
            recv_sem=rb.at[slot_src],
            device_id=(peer, a),
            device_id_type=MESH_ID,
        )

    def start_b(j, carry):
        peer = lax.rem(h + j, nx)
        copy_b(peer, h, lax.rem(peer, nt)).start()
        return carry

    lax.fori_loop(1, nx, start_b, 0)
    own = lax.rem(h, nt)
    recv_b[h] = p_t[own]

    def wait_b(j, carry):
        peer = lax.rem(h + j, nx)
        copy_b(peer, h, lax.rem(peer, nt)).wait_send()
        copy_b(h, peer, own).wait_recv()
        return carry

    lax.fori_loop(1, nx, wait_b, 0)
    recv_c[own] = jnp.sum(recv_b[...], axis=0)

    base = h - own

    def copy_c(peer_tile, slot_tile):
        return pltpu.make_async_remote_copy(
            src_ref=recv_c.at[slot_tile],
            dst_ref=recv_c.at[slot_tile],
            send_sem=sc.at[peer_tile],
            recv_sem=rc.at[slot_tile],
            device_id=(base + peer_tile, a),
            device_id_type=MESH_ID,
        )

    def start_c(j, carry):
        copy_c(lax.rem(own + j, nt), own).start()
        return carry

    lax.fori_loop(1, nt, start_c, 0)

    def wait_c(j, carry):
        other = lax.rem(own + j, nt)
        copy_c(other, own).wait_send()
        copy_c(own, other).wait_recv()
        return carry

    lax.fori_loop(1, nt, wait_c, 0)
    for u in range(nt):
        recv_d[a, u // kb, (u % kb) * SUB:(u % kb + 1) * SUB, :] = recv_c[u]

    def copy_d(peer, slot_src):
        return pltpu.make_async_remote_copy(
            src_ref=recv_d.at[slot_src],
            dst_ref=recv_d.at[slot_src],
            send_sem=sd.at[peer],
            recv_sem=rd.at[slot_src],
            device_id=(h, peer),
            device_id_type=MESH_ID,
        )

    def start_d(j, carry):
        copy_d(lax.rem(a + j, ny), a).start()
        return carry

    lax.fori_loop(1, ny, start_d, 0)

    def wait_d(j, carry):
        copy_d(lax.rem(a + j, ny), a).wait_send()
        copy_d(a, lax.rem(a + j, ny)).wait_recv()
        return carry

    lax.fori_loop(1, ny, wait_d, 0)
    for s in range(ny):
        block = recv_d[s]
        if divisor is not None:
            block = block / divisor
        o_ref[:, :, s * LANES:(s + 1) * LANES] = block
    if orthonormalize:
        orthonormal_rows(o_ref)


def orthonormal_rows(rows_ref):
    nb, k = rows_ref.shape[0], rows_ref.shape[1]
    gram = jnp.stack([
        lax.dot_general(rows_ref[b], rows_ref[b], (((1,), (1,)), ((), ())),
                        precision=HIGHEST, preferred_element_type=jnp.float32)
        for b in range(nb)
    ])
    r_idx = lax.broadcasted_iota(jnp.int32, (nb, k, k), 1)
    c_idx = lax.broadcasted_iota(jnp.int32, (nb, k, k), 2)
    diag = r_idx == c_idx
    trace_value = jnp.sum(jnp.sum(jnp.where(diag, gram, 0.0), axis=2, keepdims=True),
                          axis=1, keepdims=True)
    shift_value = 1e-06 * (trace_value / k + 1.0)
    work = gram + jnp.where(diag, shift_value, 0.0)
    sub_idx = r_idx[:, :, :1]
    lane_idx = c_idx[:, :1, :]
    inverse = jnp.where(diag, 1.0, 0.0)
    for j in range(k):
        row = work[:, j:j + 1, :]
        inv_root = lax.rsqrt(row[:, :, j:j + 1])
        col = jnp.where(sub_idx >= j, work[:, :, j:j + 1] * inv_root, 0.0)
        row = jnp.where(lane_idx >= j, row * inv_root, 0.0)
        work = work - col * row
        solved = inverse[:, j:j + 1, :] * inv_root
        below = jnp.where(sub_idx > j, col, 0.0)
        inverse = jnp.where(sub_idx == j, solved, inverse - below * solved)
    for b in range(nb):
        rows_ref[b] = jnp.dot(inverse[b], rows_ref[b], precision=HIGHEST,
                              preferred_element_type=jnp.float32)


def allreduce(x, nx, ny, collective_id, orthonormalize=False, divisor=None, patterns=()):
    nb, rows, cols = x.shape
    assert cols == ny * LANES and rows % SUB == 0
    nt = nb * (rows // SUB)
    assert nx % nt == 0
    vmem = pltpu.VMEM
    return pl.pallas_call(
        functools.partial(allreduce_kernel, nx, ny, orthonormalize, divisor, patterns),
        out_shape=[jax.ShapeDtypeStruct(x.shape, jnp.float32)] + [
            jax.ShapeDtypeStruct((nb, len(p) * rows, cols), jnp.bfloat16) for p in patterns],
        in_specs=[pl.BlockSpec(memory_space=vmem)],
        out_specs=[pl.BlockSpec(memory_space=vmem)] * (1 + len(patterns)),
        scratch_shapes=[
            vmem((ny, nb, rows, LANES), jnp.float32),
            vmem((nt, SUB, LANES), jnp.float32),
            vmem((nx, SUB, LANES), jnp.float32),
            vmem((nt, SUB, LANES), jnp.float32),
            vmem((ny, nb, rows, LANES), jnp.float32),
            pltpu.SemaphoreType.DMA((ny,)),
            pltpu.SemaphoreType.DMA((ny,)),
            pltpu.SemaphoreType.DMA((nx,)),
            pltpu.SemaphoreType.DMA((nx,)),
            pltpu.SemaphoreType.DMA((nt,)),
            pltpu.SemaphoreType.DMA((nt,)),
            pltpu.SemaphoreType.DMA((ny,)),
            pltpu.SemaphoreType.DMA((ny,)),
        ],
        compiler_params=pltpu.CompilerParams(
            collective_id=collective_id, has_side_effects=True,
            vmem_limit_bytes=8 * 1024 * 1024,
        ),
    )(x)


def gram_of(factor_rows):
    return jnp.einsum("bki,bli->bkl", factor_rows, factor_rows, precision=HIGHEST)


def solve_rows(gram_matrix, factor_rows):
    width = gram_matrix.shape[-1]
    identity = jnp.eye(width, dtype=jnp.float32)
    trace_value = jnp.trace(gram_matrix, axis1=1, axis2=2)
    shift_value = 1e-06 * (trace_value / width + 1.0)
    lower_factor = jnp.linalg.cholesky(gram_matrix + shift_value[:, None, None] * identity)
    return lax.linalg.triangular_solve(lower_factor, factor_rows, left_side=True, lower=True)


def on_device(nx, ny, normed, grad_query, grad_key, error, start_factor):
    replicas = nx * ny
    query_grad = lax.dot_general(normed, grad_query, CONTRACT, preferred_element_type=jnp.float32)
    key_grad = lax.dot_general(normed, grad_key, CONTRACT, preferred_element_type=jnp.float32)
    merged = jnp.stack([query_grad, key_grad]) + error.astype(jnp.float32)
    m_hi, m_mid, m_lo = split3(merged)
    s_hi, s_mid, s_lo = split3(start_factor)
    left_local = combine6(*rows_times(
        [[s_hi, s_mid, s_lo], [s_hi, s_mid], [s_hi]], [m_hi, m_mid, m_lo], "bkj,bij->bki"))
    left_rows, lefts, left_pair = allreduce(
        left_local, nx, ny, 0, orthonormalize=True, patterns=((0, 0, 1, 0, 1, 2), (0, 1)))
    k = left_rows.shape[1]
    pair = jnp.einsum("bki,bij->bkj", left_pair, m_hi, preferred_element_type=jnp.float32)
    cross = jnp.einsum("bki,bij->bkj", lefts[:, :k], m_mid, preferred_element_type=jnp.float32)
    right_local = pair[:, :k] + (pair[:, k:] + cross)
    right_rows, rights = allreduce(
        right_local, nx, ny, 1, divisor=float(replicas), patterns=((0, 1, 0, 2, 1, 0),))
    approx = jnp.einsum("bki,bkj->bij", lefts, rights, preferred_element_type=jnp.float32)
    return ((merged - approx).astype(jnp.bfloat16), left_rows, right_rows)


def split3(x):
    hi = lax.reduce_precision(x, exponent_bits=8, mantissa_bits=7)
    rest = x - hi
    mid = lax.reduce_precision(rest, exponent_bits=8, mantissa_bits=7)
    lo = rest - mid
    return (hi.astype(jnp.bfloat16), mid.astype(jnp.bfloat16), lo.astype(jnp.bfloat16))


def rows_times(row_groups, big_pieces, spec):
    out = []
    for group, big in zip(row_groups, big_pieces):
        k = group[0].shape[1]
        prod = jnp.einsum(spec, jnp.concatenate(group, axis=1), big,
                          preferred_element_type=jnp.float32)
        out.append([prod[:, g * k:(g + 1) * k] for g in range(len(group))])
    return out


def combine6(first, second, third):
    small = (first[2] + second[1]) + third[0]
    return first[0] + ((first[1] + second[0]) + small)


def solution(mesh):
    nx, ny = mesh.shape["gx"], mesh.shape["gy"]
    placed = (
        P(("gx", "gy"), None),
        P(("gx", "gy"), None),
        P(("gx", "gy"), None),
        P(("gx", "gy"), None, None),
        P(),
    )
    return jax.shard_map(
        functools.partial(on_device, nx, ny),
        mesh=mesh,
        in_specs=placed,
        out_specs=(P(("gx", "gy"), None, None), P(), P()),
        check_vma=False,
    )
```

```python
import functools

import jax
import jax.numpy as jnp
from jax import lax
from jax.experimental import pallas as pl
from jax.experimental.pallas import tpu as pltpu
from jax.sharding import PartitionSpec as P

HIGHEST = lax.Precision.HIGHEST
HIGH = lax.Precision.HIGH
CONTRACT = (((0,), (0,)), ((), ()))
MESH_ID = pl.DeviceIdType.MESH
LANES = 128
SUB = 8


def allreduce_kernel(nx, ny, orthonormalize, divisor, patterns, x_ref, o_ref, *refs):
    stacked = refs[:len(patterns)]
    allreduce_body(nx, ny, orthonormalize, divisor, x_ref, o_ref, *refs[len(patterns):])
    for b in range(o_ref.shape[0]):
        value = o_ref[b]
        k = value.shape[0]
        hi = value.astype(jnp.bfloat16)
        rest = value - hi.astype(jnp.float32)
        mid = rest.astype(jnp.bfloat16)
        lo = (rest - mid.astype(jnp.float32)).astype(jnp.bfloat16)
        parts = (hi, mid, lo)
        for pattern, out_ref in zip(patterns, stacked):
            for g, piece in enumerate(pattern):
                out_ref[b, g * k:(g + 1) * k, :] = parts[piece]


def allreduce_body(nx, ny, orthonormalize, divisor, x_ref, o_ref, recv_a, p_t, recv_b, recv_c, recv_d,
                     sa, ra, sb, rb, sc, rc, sd, rd):
    h = lax.axis_index("gx")
    a = lax.axis_index("gy")
    nb, rows = x_ref.shape[0], x_ref.shape[1]
    kb = rows // SUB
    nt = nb * kb

    barrier = pltpu.get_barrier_semaphore()

    def signal_y(j, carry):
        pl.semaphore_signal(barrier, 1, device_id=(h, lax.rem(a + j, ny)),
                            device_id_type=MESH_ID)
        return carry

    def signal_x(j, carry):
        pl.semaphore_signal(barrier, 1, device_id=(lax.rem(h + j, nx), a),
                            device_id_type=MESH_ID)
        return carry

    lax.fori_loop(1, ny, signal_y, 0)
    lax.fori_loop(1, nx, signal_x, 0)
    pl.semaphore_wait(barrier, (ny - 1) + (nx - 1))

    def copy_a(peer, slot_src):
        return pltpu.make_async_remote_copy(
            src_ref=x_ref.at[:, :, pl.ds(pl.multiple_of(peer * LANES, LANES), LANES)],
            dst_ref=recv_a.at[slot_src],
            send_sem=sa.at[peer],
            recv_sem=ra.at[slot_src],
            device_id=(h, peer),
            device_id_type=MESH_ID,
        )

    def start_a(j, carry):
        copy_a(lax.rem(a + j, ny), a).start()
        return carry

    lax.fori_loop(1, ny, start_a, 0)
    recv_a[a] = x_ref[:, :, pl.ds(pl.multiple_of(a * LANES, LANES), LANES)]

    def wait_a(j, carry):
        copy_a(lax.rem(a + j, ny), a).wait_send()
        copy_a(a, lax.rem(a + j, ny)).wait_recv()
        return carry

    lax.fori_loop(1, ny, wait_a, 0)
    part = jnp.sum(recv_a[...], axis=0)
    for u in range(nt):
        p_t[u] = part[u // kb, (u % kb) * SUB:(u % kb + 1) * SUB, :]

    def copy_b(peer, slot_src, tile):
        return pltpu.make_async_remote_copy(
            src_ref=p_t.at[tile],
            dst_ref=recv_b.at[slot_src],
            send_sem=sb.at[peer],
            recv_sem=rb.at[slot_src],
            device_id=(peer, a),
            device_id_type=MESH_ID,
        )

    def start_b(j, carry):
        peer = lax.rem(h + j, nx)
        copy_b(peer, h, lax.rem(peer, nt)).start()
        return carry

    lax.fori_loop(1, nx, start_b, 0)
    own = lax.rem(h, nt)
    recv_b[h] = p_t[own]

    def wait_b(j, carry):
        peer = lax.rem(h + j, nx)
        copy_b(peer, h, lax.rem(peer, nt)).wait_send()
        copy_b(h, peer, own).wait_recv()
        return carry

    lax.fori_loop(1, nx, wait_b, 0)
    recv_c[own] = jnp.sum(recv_b[...], axis=0)

    base = h - own

    def copy_c(peer_tile, slot_tile):
        return pltpu.make_async_remote_copy(
            src_ref=recv_c.at[slot_tile],
            dst_ref=recv_c.at[slot_tile],
            send_sem=sc.at[peer_tile],
            recv_sem=rc.at[slot_tile],
            device_id=(base + peer_tile, a),
            device_id_type=MESH_ID,
        )

    def start_c(j, carry):
        copy_c(lax.rem(own + j, nt), own).start()
        return carry

    lax.fori_loop(1, nt, start_c, 0)

    def wait_c(j, carry):
        other = lax.rem(own + j, nt)
        copy_c(other, own).wait_send()
        copy_c(own, other).wait_recv()
        return carry

    lax.fori_loop(1, nt, wait_c, 0)
    for u in range(nt):
        recv_d[a, u // kb, (u % kb) * SUB:(u % kb + 1) * SUB, :] = recv_c[u]

    def copy_d(peer, slot_src):
        return pltpu.make_async_remote_copy(
            src_ref=recv_d.at[slot_src],
            dst_ref=recv_d.at[slot_src],
            send_sem=sd.at[peer],
            recv_sem=rd.at[slot_src],
            device_id=(h, peer),
            device_id_type=MESH_ID,
        )

    def start_d(j, carry):
        copy_d(lax.rem(a + j, ny), a).start()
        return carry

    lax.fori_loop(1, ny, start_d, 0)

    def wait_d(j, carry):
        copy_d(lax.rem(a + j, ny), a).wait_send()
        copy_d(a, lax.rem(a + j, ny)).wait_recv()
        return carry

    lax.fori_loop(1, ny, wait_d, 0)
    for s in range(ny):
        block = recv_d[s]
        if divisor is not None:
            block = block / divisor
        o_ref[:, :, s * LANES:(s + 1) * LANES] = block
    if orthonormalize:
        orthonormal_rows(o_ref)


def orthonormal_rows(rows_ref):
    nb, k = rows_ref.shape[0], rows_ref.shape[1]
    gram = jnp.stack([
        lax.dot_general(rows_ref[b], rows_ref[b], (((1,), (1,)), ((), ())),
                        precision=HIGHEST, preferred_element_type=jnp.float32)
        for b in range(nb)
    ])
    r_idx = lax.broadcasted_iota(jnp.int32, (nb, k, k), 1)
    c_idx = lax.broadcasted_iota(jnp.int32, (nb, k, k), 2)
    diag = r_idx == c_idx
    trace_value = jnp.sum(jnp.sum(jnp.where(diag, gram, 0.0), axis=2, keepdims=True),
                          axis=1, keepdims=True)
    shift_value = 1e-06 * (trace_value / k + 1.0)
    work = gram + jnp.where(diag, shift_value, 0.0)
    sub_idx = r_idx[:, :, :1]
    lane_idx = c_idx[:, :1, :]
    inverse = jnp.where(diag, 1.0, 0.0)
    for j in range(k):
        row = work[:, j:j + 1, :]
        inv_root = lax.rsqrt(row[:, :, j:j + 1])
        col = jnp.where(sub_idx >= j, work[:, :, j:j + 1] * inv_root, 0.0)
        row = jnp.where(lane_idx >= j, row * inv_root, 0.0)
        work = work - col * row
        solved = inverse[:, j:j + 1, :] * inv_root
        below = jnp.where(sub_idx > j, col, 0.0)
        inverse = jnp.where(sub_idx == j, solved, inverse - below * solved)
    for b in range(nb):
        rows_ref[b] = jnp.dot(inverse[b], rows_ref[b], precision=HIGHEST,
                              preferred_element_type=jnp.float32)


def allreduce(x, nx, ny, collective_id, orthonormalize=False, divisor=None, patterns=()):
    nb, rows, cols = x.shape
    assert cols == ny * LANES and rows % SUB == 0
    nt = nb * (rows // SUB)
    assert nx % nt == 0
    vmem = pltpu.VMEM
    return pl.pallas_call(
        functools.partial(allreduce_kernel, nx, ny, orthonormalize, divisor, patterns),
        out_shape=[jax.ShapeDtypeStruct(x.shape, jnp.float32)] + [
            jax.ShapeDtypeStruct((nb, len(p) * rows, cols), jnp.bfloat16) for p in patterns],
        in_specs=[pl.BlockSpec(memory_space=vmem)],
        out_specs=[pl.BlockSpec(memory_space=vmem)] * (1 + len(patterns)),
        scratch_shapes=[
            vmem((ny, nb, rows, LANES), jnp.float32),
            vmem((nt, SUB, LANES), jnp.float32),
            vmem((nx, SUB, LANES), jnp.float32),
            vmem((nt, SUB, LANES), jnp.float32),
            vmem((ny, nb, rows, LANES), jnp.float32),
            pltpu.SemaphoreType.DMA((ny,)),
            pltpu.SemaphoreType.DMA((ny,)),
            pltpu.SemaphoreType.DMA((nx,)),
            pltpu.SemaphoreType.DMA((nx,)),
            pltpu.SemaphoreType.DMA((nt,)),
            pltpu.SemaphoreType.DMA((nt,)),
            pltpu.SemaphoreType.DMA((ny,)),
            pltpu.SemaphoreType.DMA((ny,)),
        ],
        compiler_params=pltpu.CompilerParams(
            collective_id=collective_id, has_side_effects=True,
            vmem_limit_bytes=8 * 1024 * 1024,
        ),
    )(x)


def gram_of(factor_rows):
    return jnp.einsum("bki,bli->bkl", factor_rows, factor_rows, precision=HIGHEST)


def solve_rows(gram_matrix, factor_rows):
    width = gram_matrix.shape[-1]
    identity = jnp.eye(width, dtype=jnp.float32)
    trace_value = jnp.trace(gram_matrix, axis1=1, axis2=2)
    shift_value = 1e-06 * (trace_value / width + 1.0)
    lower_factor = jnp.linalg.cholesky(gram_matrix + shift_value[:, None, None] * identity)
    return lax.linalg.triangular_solve(lower_factor, factor_rows, left_side=True, lower=True)


def on_device(nx, ny, normed, grad_query, grad_key, error, start_factor):
    replicas = nx * ny
    query_grad = lax.dot_general(normed, grad_query, CONTRACT, preferred_element_type=jnp.float32)
    key_grad = lax.dot_general(normed, grad_key, CONTRACT, preferred_element_type=jnp.float32)
    merged = jnp.stack([query_grad + error[0].astype(jnp.float32),
                        key_grad + error[1].astype(jnp.float32)])
    m_hi, m_mid, m_lo = split3(merged)
    s_hi, s_mid, s_lo = split3(start_factor)
    left_local = combine6(*rows_times(
        [[s_hi, s_mid, s_lo], [s_hi, s_mid], [s_hi]], [m_hi, m_mid, m_lo], "bkj,bij->bki"))
    left_rows, lefts, left_pair = allreduce(
        left_local, nx, ny, 0, orthonormalize=True, patterns=((0, 0, 1, 0, 1, 2), (0, 1)))
    k = left_rows.shape[1]
    pair = jnp.einsum("bki,bij->bkj", left_pair, m_hi, preferred_element_type=jnp.float32)
    cross = jnp.einsum("bki,bij->bkj", lefts[:, :k], m_mid, preferred_element_type=jnp.float32)
    right_local = pair[:, :k] + (pair[:, k:] + cross)
    right_rows, rights = allreduce(
        right_local, nx, ny, 1, divisor=float(replicas), patterns=((0, 1, 0, 2, 1, 0),))
    approx = jnp.einsum("bki,bkj->bij", lefts, rights, preferred_element_type=jnp.float32)
    return ((merged - approx).astype(jnp.bfloat16), left_rows, right_rows)


def split3(x):
    hi = lax.reduce_precision(x, exponent_bits=8, mantissa_bits=7)
    rest = x - hi
    mid = lax.reduce_precision(rest, exponent_bits=8, mantissa_bits=7)
    lo = rest - mid
    return (hi.astype(jnp.bfloat16), mid.astype(jnp.bfloat16), lo.astype(jnp.bfloat16))


def rows_times(row_groups, big_pieces, spec):
    out = []
    for group, big in zip(row_groups, big_pieces):
        k = group[0].shape[1]
        prod = jnp.einsum(spec, jnp.concatenate(group, axis=1), big,
                          preferred_element_type=jnp.float32)
        out.append([prod[:, g * k:(g + 1) * k] for g in range(len(group))])
    return out


def combine6(first, second, third):
    small = (first[2] + second[1]) + third[0]
    return first[0] + ((first[1] + second[0]) + small)


def solution(mesh):
    nx, ny = mesh.shape["gx"], mesh.shape["gy"]
    placed = (
        P(("gx", "gy"), None),
        P(("gx", "gy"), None),
        P(("gx", "gy"), None),
        P(("gx", "gy"), None, None),
        P(),
    )
    return jax.shard_map(
        functools.partial(on_device, nx, ny),
        mesh=mesh,
        in_specs=placed,
        out_specs=(P(("gx", "gy"), None, None), P(), P()),
        check_vma=False,
    )
```

```python
import functools

import jax
import jax.numpy as jnp
from jax import lax
from jax.experimental import pallas as pl
from jax.experimental.pallas import tpu as pltpu
from jax.sharding import PartitionSpec as P

HIGHEST = lax.Precision.HIGHEST
HIGH = lax.Precision.HIGH
CONTRACT = (((0,), (0,)), ((), ()))
MESH_ID = pl.DeviceIdType.MESH
LANES = 128
SUB = 8


def allreduce_kernel(nx, ny, orthonormalize, divisor, patterns, x_ref, o_ref, *refs):
    stacked = refs[:len(patterns)]
    allreduce_body(nx, ny, orthonormalize, divisor, x_ref, o_ref, *refs[len(patterns):])
    for b in range(o_ref.shape[0]):
        value = o_ref[b]
        k = value.shape[0]
        hi = value.astype(jnp.bfloat16)
        rest = value - hi.astype(jnp.float32)
        mid = rest.astype(jnp.bfloat16)
        lo = (rest - mid.astype(jnp.float32)).astype(jnp.bfloat16)
        parts = (hi, mid, lo)
        for pattern, out_ref in zip(patterns, stacked):
            for g, piece in enumerate(pattern):
                out_ref[b, g * k:(g + 1) * k, :] = parts[piece]


def allreduce_body(nx, ny, orthonormalize, divisor, x_ref, o_ref, recv_a, p_t, recv_b, recv_c, recv_d,
                     sa, ra, sb, rb, sc, rc, sd, rd, with_barrier=True):
    h = lax.axis_index("gx")
    a = lax.axis_index("gy")
    nb, rows = x_ref.shape[0], x_ref.shape[1]
    kb = rows // SUB
    nt = nb * kb

    barrier = pltpu.get_barrier_semaphore()

    def signal_y(j, carry):
        pl.semaphore_signal(barrier, 1, device_id=(h, lax.rem(a + j, ny)),
                            device_id_type=MESH_ID)
        return carry

    def signal_x(j, carry):
        pl.semaphore_signal(barrier, 1, device_id=(lax.rem(h + j, nx), a),
                            device_id_type=MESH_ID)
        return carry

    if with_barrier:
        lax.fori_loop(1, ny, signal_y, 0)
        lax.fori_loop(1, nx, signal_x, 0)
        pl.semaphore_wait(barrier, (ny - 1) + (nx - 1))

    def copy_a(peer, slot_src):
        return pltpu.make_async_remote_copy(
            src_ref=x_ref.at[:, :, pl.ds(pl.multiple_of(peer * LANES, LANES), LANES)],
            dst_ref=recv_a.at[slot_src],
            send_sem=sa.at[peer],
            recv_sem=ra.at[slot_src],
            device_id=(h, peer),
            device_id_type=MESH_ID,
        )

    def start_a(j, carry):
        copy_a(lax.rem(a + j, ny), a).start()
        return carry

    lax.fori_loop(1, ny, start_a, 0)
    recv_a[a] = x_ref[:, :, pl.ds(pl.multiple_of(a * LANES, LANES), LANES)]

    def wait_a(j, carry):
        copy_a(lax.rem(a + j, ny), a).wait_send()
        copy_a(a, lax.rem(a + j, ny)).wait_recv()
        return carry

    lax.fori_loop(1, ny, wait_a, 0)
    part = jnp.sum(recv_a[...], axis=0)
    for u in range(nt):
        p_t[u] = part[u // kb, (u % kb) * SUB:(u % kb + 1) * SUB, :]

    def copy_b(peer, slot_src, tile):
        return pltpu.make_async_remote_copy(
            src_ref=p_t.at[tile],
            dst_ref=recv_b.at[slot_src],
            send_sem=sb.at[peer],
            recv_sem=rb.at[slot_src],
            device_id=(peer, a),
            device_id_type=MESH_ID,
        )

    def start_b(j, carry):
        peer = lax.rem(h + j, nx)
        copy_b(peer, h, lax.rem(peer, nt)).start()
        return carry

    lax.fori_loop(1, nx, start_b, 0)
    own = lax.rem(h, nt)
    recv_b[h] = p_t[own]

    def wait_b(j, carry):
        peer = lax.rem(h + j, nx)
        copy_b(peer, h, lax.rem(peer, nt)).wait_send()
        copy_b(h, peer, own).wait_recv()
        return carry

    lax.fori_loop(1, nx, wait_b, 0)
    recv_c[own] = jnp.sum(recv_b[...], axis=0)

    base = h - own

    def copy_c(peer_tile, slot_tile):
        return pltpu.make_async_remote_copy(
            src_ref=recv_c.at[slot_tile],
            dst_ref=recv_c.at[slot_tile],
            send_sem=sc.at[peer_tile],
            recv_sem=rc.at[slot_tile],
            device_id=(base + peer_tile, a),
            device_id_type=MESH_ID,
        )

    def start_c(j, carry):
        copy_c(lax.rem(own + j, nt), own).start()
        return carry

    lax.fori_loop(1, nt, start_c, 0)

    def wait_c(j, carry):
        other = lax.rem(own + j, nt)
        copy_c(other, own).wait_send()
        copy_c(own, other).wait_recv()
        return carry

    lax.fori_loop(1, nt, wait_c, 0)
    for u in range(nt):
        recv_d[a, u // kb, (u % kb) * SUB:(u % kb + 1) * SUB, :] = recv_c[u]

    def copy_d(peer, slot_src):
        return pltpu.make_async_remote_copy(
            src_ref=recv_d.at[slot_src],
            dst_ref=recv_d.at[slot_src],
            send_sem=sd.at[peer],
            recv_sem=rd.at[slot_src],
            device_id=(h, peer),
            device_id_type=MESH_ID,
        )

    def start_d(j, carry):
        copy_d(lax.rem(a + j, ny), a).start()
        return carry

    lax.fori_loop(1, ny, start_d, 0)

    def wait_d(j, carry):
        copy_d(lax.rem(a + j, ny), a).wait_send()
        copy_d(a, lax.rem(a + j, ny)).wait_recv()
        return carry

    lax.fori_loop(1, ny, wait_d, 0)
    for s in range(ny):
        block = recv_d[s]
        if divisor is not None:
            block = block / divisor
        o_ref[:, :, s * LANES:(s + 1) * LANES] = block
    if orthonormalize:
        orthonormal_rows(o_ref)


def orthonormal_rows(rows_ref):
    nb, k = rows_ref.shape[0], rows_ref.shape[1]
    gram = jnp.stack([
        lax.dot_general(rows_ref[b], rows_ref[b], (((1,), (1,)), ((), ())),
                        precision=HIGHEST, preferred_element_type=jnp.float32)
        for b in range(nb)
    ])
    r_idx = lax.broadcasted_iota(jnp.int32, (nb, k, k), 1)
    c_idx = lax.broadcasted_iota(jnp.int32, (nb, k, k), 2)
    diag = r_idx == c_idx
    trace_value = jnp.sum(jnp.sum(jnp.where(diag, gram, 0.0), axis=2, keepdims=True),
                          axis=1, keepdims=True)
    shift_value = 1e-06 * (trace_value / k + 1.0)
    work = gram + jnp.where(diag, shift_value, 0.0)
    sub_idx = r_idx[:, :, :1]
    lane_idx = c_idx[:, :1, :]
    inverse = jnp.where(diag, 1.0, 0.0)
    for j in range(k):
        row = work[:, j:j + 1, :]
        inv_root = lax.rsqrt(row[:, :, j:j + 1])
        col = jnp.where(sub_idx >= j, work[:, :, j:j + 1] * inv_root, 0.0)
        row = jnp.where(lane_idx >= j, row * inv_root, 0.0)
        work = work - col * row
        solved = inverse[:, j:j + 1, :] * inv_root
        below = jnp.where(sub_idx > j, col, 0.0)
        inverse = jnp.where(sub_idx == j, solved, inverse - below * solved)
    for b in range(nb):
        rows_ref[b] = jnp.dot(inverse[b], rows_ref[b], precision=HIGHEST,
                              preferred_element_type=jnp.float32)


def write_pieces(value_ref, patterns, stacked):
    for b in range(value_ref.shape[0]):
        value = value_ref[b]
        k = value.shape[0]
        hi = value.astype(jnp.bfloat16)
        rest = value - hi.astype(jnp.float32)
        mid = rest.astype(jnp.bfloat16)
        lo = (rest - mid.astype(jnp.float32)).astype(jnp.bfloat16)
        parts = (hi, mid, lo)
        for pattern, out_ref in zip(patterns, stacked):
            for g, piece in enumerate(pattern):
                out_ref[b, g * k:(g + 1) * k, :] = parts[piece]


def factors_kernel(nx, ny, divisor, x_ref, mq_ref, mk_ref, left_ref, lefts_ref, right_ref,
                   rights_ref, pair_ref, local_ref, *scratch):
    first, second = scratch[:13], scratch[13:]
    allreduce_body(nx, ny, True, None, x_ref, left_ref, *first)
    write_pieces(left_ref, ((0, 0, 1, 0, 1, 2), (0, 1)), (lefts_ref, pair_ref))
    k = left_ref.shape[1]
    width = 256
    for b, m_ref in enumerate((mq_ref, mk_ref)):
        pair = pair_ref[b]
        top = lefts_ref[b, :k, :]
        for c in range(m_ref.shape[1] // width):
            block = m_ref[:, c * width:(c + 1) * width]
            hi = block.astype(jnp.bfloat16)
            mid = (block - hi.astype(jnp.float32)).astype(jnp.bfloat16)
            both = jnp.dot(pair, hi, preferred_element_type=jnp.float32)
            cross = jnp.dot(top, mid, preferred_element_type=jnp.float32)
            local_ref[b, :, c * width:(c + 1) * width] = both[:k] + (both[k:] + cross)
    allreduce_body(nx, ny, False, divisor, local_ref, right_ref, *second, with_barrier=False)
    write_pieces(right_ref, ((0, 1, 0, 2, 1, 0),), (rights_ref,))


def allreduce_scratch(nx, ny, nb, rows):
    vmem = pltpu.VMEM
    nt = nb * (rows // SUB)
    return [
        vmem((ny, nb, rows, LANES), jnp.float32),
        vmem((nt, SUB, LANES), jnp.float32),
        vmem((nx, SUB, LANES), jnp.float32),
        vmem((nt, SUB, LANES), jnp.float32),
        vmem((ny, nb, rows, LANES), jnp.float32),
        pltpu.SemaphoreType.DMA((ny,)),
        pltpu.SemaphoreType.DMA((ny,)),
        pltpu.SemaphoreType.DMA((nx,)),
        pltpu.SemaphoreType.DMA((nx,)),
        pltpu.SemaphoreType.DMA((nt,)),
        pltpu.SemaphoreType.DMA((nt,)),
        pltpu.SemaphoreType.DMA((ny,)),
        pltpu.SemaphoreType.DMA((ny,)),
    ]


def factors(x, query_merged, key_merged, nx, ny, divisor):
    nb, rows, cols = x.shape
    assert cols == ny * LANES and rows % SUB == 0
    assert nx % (nb * (rows // SUB)) == 0
    vmem = pltpu.VMEM
    f32, bf16 = jnp.float32, jnp.bfloat16
    return pl.pallas_call(
        functools.partial(factors_kernel, nx, ny, divisor),
        out_shape=[
            jax.ShapeDtypeStruct(x.shape, f32),
            jax.ShapeDtypeStruct((nb, 6 * rows, cols), bf16),
            jax.ShapeDtypeStruct(x.shape, f32),
            jax.ShapeDtypeStruct((nb, 6 * rows, cols), bf16),
        ],
        in_specs=[pl.BlockSpec(memory_space=vmem)] * 3,
        out_specs=[pl.BlockSpec(memory_space=vmem)] * 4,
        scratch_shapes=[vmem((nb, 2 * rows, cols), bf16), vmem(x.shape, f32)]
        + allreduce_scratch(nx, ny, nb, rows) + allreduce_scratch(nx, ny, nb, rows),
        compiler_params=pltpu.CompilerParams(
            collective_id=0, has_side_effects=True,
            vmem_limit_bytes=24 * 1024 * 1024,
        ),
    )(x, query_merged, key_merged)


def allreduce(x, nx, ny, collective_id, orthonormalize=False, divisor=None, patterns=()):
    nb, rows, cols = x.shape
    assert cols == ny * LANES and rows % SUB == 0
    nt = nb * (rows // SUB)
    assert nx % nt == 0
    vmem = pltpu.VMEM
    return pl.pallas_call(
        functools.partial(allreduce_kernel, nx, ny, orthonormalize, divisor, patterns),
        out_shape=[jax.ShapeDtypeStruct(x.shape, jnp.float32)] + [
            jax.ShapeDtypeStruct((nb, len(p) * rows, cols), jnp.bfloat16) for p in patterns],
        in_specs=[pl.BlockSpec(memory_space=vmem)],
        out_specs=[pl.BlockSpec(memory_space=vmem)] * (1 + len(patterns)),
        scratch_shapes=[
            vmem((ny, nb, rows, LANES), jnp.float32),
            vmem((nt, SUB, LANES), jnp.float32),
            vmem((nx, SUB, LANES), jnp.float32),
            vmem((nt, SUB, LANES), jnp.float32),
            vmem((ny, nb, rows, LANES), jnp.float32),
            pltpu.SemaphoreType.DMA((ny,)),
            pltpu.SemaphoreType.DMA((ny,)),
            pltpu.SemaphoreType.DMA((nx,)),
            pltpu.SemaphoreType.DMA((nx,)),
            pltpu.SemaphoreType.DMA((nt,)),
            pltpu.SemaphoreType.DMA((nt,)),
            pltpu.SemaphoreType.DMA((ny,)),
            pltpu.SemaphoreType.DMA((ny,)),
        ],
        compiler_params=pltpu.CompilerParams(
            collective_id=collective_id, has_side_effects=True,
            vmem_limit_bytes=8 * 1024 * 1024,
        ),
    )(x)


def gram_of(factor_rows):
    return jnp.einsum("bki,bli->bkl", factor_rows, factor_rows, precision=HIGHEST)


def solve_rows(gram_matrix, factor_rows):
    width = gram_matrix.shape[-1]
    identity = jnp.eye(width, dtype=jnp.float32)
    trace_value = jnp.trace(gram_matrix, axis1=1, axis2=2)
    shift_value = 1e-06 * (trace_value / width + 1.0)
    lower_factor = jnp.linalg.cholesky(gram_matrix + shift_value[:, None, None] * identity)
    return lax.linalg.triangular_solve(lower_factor, factor_rows, left_side=True, lower=True)


def on_device(nx, ny, normed, grad_query, grad_key, error, start_factor):
    replicas = nx * ny
    query_grad = lax.dot_general(normed, grad_query, CONTRACT, preferred_element_type=jnp.float32)
    key_grad = lax.dot_general(normed, grad_key, CONTRACT, preferred_element_type=jnp.float32)
    query_merged = query_grad + error[0].astype(jnp.float32)
    key_merged = key_grad + error[1].astype(jnp.float32)
    merged = jnp.stack([query_merged, key_merged])
    m_hi, m_mid, m_lo = split3(merged)
    s_hi, s_mid, s_lo = split3(start_factor)
    left_local = combine6(*rows_times(
        [[s_hi, s_mid, s_lo], [s_hi, s_mid], [s_hi]], [m_hi, m_mid, m_lo], "bkj,bij->bki"))
    left_rows, lefts, right_rows, rights = factors(
        left_local, query_merged, key_merged, nx, ny, float(replicas))
    approx = jnp.einsum("bki,bkj->bij", lefts, rights, preferred_element_type=jnp.float32)
    return ((merged - approx).astype(jnp.bfloat16), left_rows, right_rows)


def split3(x):
    hi = lax.reduce_precision(x, exponent_bits=8, mantissa_bits=7)
    rest = x - hi
    mid = lax.reduce_precision(rest, exponent_bits=8, mantissa_bits=7)
    lo = rest - mid
    return (hi.astype(jnp.bfloat16), mid.astype(jnp.bfloat16), lo.astype(jnp.bfloat16))


def rows_times(row_groups, big_pieces, spec):
    out = []
    for group, big in zip(row_groups, big_pieces):
        k = group[0].shape[1]
        prod = jnp.einsum(spec, jnp.concatenate(group, axis=1), big,
                          preferred_element_type=jnp.float32)
        out.append([prod[:, g * k:(g + 1) * k] for g in range(len(group))])
    return out


def combine6(first, second, third):
    small = (first[2] + second[1]) + third[0]
    return first[0] + ((first[1] + second[0]) + small)


def solution(mesh):
    nx, ny = mesh.shape["gx"], mesh.shape["gy"]
    placed = (
        P(("gx", "gy"), None),
        P(("gx", "gy"), None),
        P(("gx", "gy"), None),
        P(("gx", "gy"), None, None),
        P(),
    )
    return jax.shard_map(
        functools.partial(on_device, nx, ny),
        mesh=mesh,
        in_specs=placed,
        out_specs=(P(("gx", "gy"), None, None), P(), P()),
        check_vma=False,
    )
```

```python
import functools

import jax
import jax.numpy as jnp
from jax import lax
from jax.experimental import pallas as pl
from jax.experimental.pallas import tpu as pltpu
from jax.sharding import PartitionSpec as P

HIGHEST = lax.Precision.HIGHEST
HIGH = lax.Precision.HIGH
CONTRACT = (((0,), (0,)), ((), ()))
MESH_ID = pl.DeviceIdType.MESH
LANES = 128
SUB = 8


def allreduce_kernel(nx, ny, orthonormalize, divisor, patterns, x_ref, o_ref, *refs):
    stacked = refs[:len(patterns)]
    allreduce_body(nx, ny, orthonormalize, divisor, x_ref, o_ref, *refs[len(patterns):])
    for b in range(o_ref.shape[0]):
        value = o_ref[b]
        k = value.shape[0]
        hi = value.astype(jnp.bfloat16)
        rest = value - hi.astype(jnp.float32)
        mid = rest.astype(jnp.bfloat16)
        lo = (rest - mid.astype(jnp.float32)).astype(jnp.bfloat16)
        parts = (hi, mid, lo)
        for pattern, out_ref in zip(patterns, stacked):
            for g, piece in enumerate(pattern):
                out_ref[b, g * k:(g + 1) * k, :] = parts[piece]


def allreduce_body(nx, ny, orthonormalize, divisor, x_ref, o_ref, recv_a, p_t, recv_b, recv_c, recv_d,
                     sa, ra, sb, rb, sc, rc, sd, rd, with_barrier=True):
    h = lax.axis_index("gx")
    a = lax.axis_index("gy")
    nb, rows = x_ref.shape[0], x_ref.shape[1]
    kb = rows // SUB
    nt = nb * kb

    barrier = pltpu.get_barrier_semaphore()

    def signal_y(j, carry):
        pl.semaphore_signal(barrier, 1, device_id=(h, lax.rem(a + j, ny)),
                            device_id_type=MESH_ID)
        return carry

    def signal_x(j, carry):
        pl.semaphore_signal(barrier, 1, device_id=(lax.rem(h + j, nx), a),
                            device_id_type=MESH_ID)
        return carry

    if with_barrier:
        lax.fori_loop(1, ny, signal_y, 0)
        lax.fori_loop(1, nx, signal_x, 0)
        pl.semaphore_wait(barrier, (ny - 1) + (nx - 1))

    def copy_a(peer, slot_src):
        return pltpu.make_async_remote_copy(
            src_ref=x_ref.at[:, :, pl.ds(pl.multiple_of(peer * LANES, LANES), LANES)],
            dst_ref=recv_a.at[slot_src],
            send_sem=sa.at[peer],
            recv_sem=ra.at[slot_src],
            device_id=(h, peer),
            device_id_type=MESH_ID,
        )

    def start_a(j, carry):
        copy_a(lax.rem(a + j, ny), a).start()
        return carry

    lax.fori_loop(1, ny, start_a, 0)
    recv_a[a] = x_ref[:, :, pl.ds(pl.multiple_of(a * LANES, LANES), LANES)]

    def wait_a(j, carry):
        copy_a(lax.rem(a + j, ny), a).wait_send()
        copy_a(a, lax.rem(a + j, ny)).wait_recv()
        return carry

    lax.fori_loop(1, ny, wait_a, 0)
    part = jnp.sum(recv_a[...], axis=0)
    for u in range(nt):
        p_t[u] = part[u // kb, (u % kb) * SUB:(u % kb + 1) * SUB, :]

    def copy_b(peer, slot_src, tile):
        return pltpu.make_async_remote_copy(
            src_ref=p_t.at[tile],
            dst_ref=recv_b.at[slot_src],
            send_sem=sb.at[peer],
            recv_sem=rb.at[slot_src],
            device_id=(peer, a),
            device_id_type=MESH_ID,
        )

    def start_b(j, carry):
        peer = lax.rem(h + j, nx)
        copy_b(peer, h, lax.rem(peer, nt)).start()
        return carry

    lax.fori_loop(1, nx, start_b, 0)
    own = lax.rem(h, nt)
    recv_b[h] = p_t[own]

    def wait_b(j, carry):
        peer = lax.rem(h + j, nx)
        copy_b(peer, h, lax.rem(peer, nt)).wait_send()
        copy_b(h, peer, own).wait_recv()
        return carry

    lax.fori_loop(1, nx, wait_b, 0)
    recv_c[own] = jnp.sum(recv_b[...], axis=0)

    base = h - own

    def copy_c(peer_tile, slot_tile):
        return pltpu.make_async_remote_copy(
            src_ref=recv_c.at[slot_tile],
            dst_ref=recv_c.at[slot_tile],
            send_sem=sc.at[peer_tile],
            recv_sem=rc.at[slot_tile],
            device_id=(base + peer_tile, a),
            device_id_type=MESH_ID,
        )

    def start_c(j, carry):
        copy_c(lax.rem(own + j, nt), own).start()
        return carry

    def copy_d_tile(peer, tile):
        row0 = pl.multiple_of(lax.rem(tile, kb) * SUB, SUB)
        return pltpu.make_async_remote_copy(
            src_ref=recv_c.at[tile],
            dst_ref=recv_d.at[a, tile // kb, pl.ds(row0, SUB), :],
            send_sem=sd.at[peer],
            recv_sem=rd.at[a],
            device_id=(h, peer),
            device_id_type=MESH_ID,
        )

    def copy_d(peer, slot_src):
        return pltpu.make_async_remote_copy(
            src_ref=recv_d.at[slot_src],
            dst_ref=recv_d.at[slot_src],
            send_sem=sd.at[peer],
            recv_sem=rd.at[slot_src],
            device_id=(h, peer),
            device_id_type=MESH_ID,
        )

    def forward(tile):
        def start_d(j, carry):
            copy_d_tile(lax.rem(a + j, ny), tile).start()
            return carry

        lax.fori_loop(1, ny, start_d, 0)

    lax.fori_loop(1, nt, start_c, 0)
    forward(own)

    def wait_c(j, carry):
        other = lax.rem(own + j, nt)
        copy_c(own, other).wait_recv()
        forward(other)
        return carry

    lax.fori_loop(1, nt, wait_c, 0)

    def wait_c_send(j, carry):
        copy_c(lax.rem(own + j, nt), own).wait_send()
        return carry

    lax.fori_loop(1, nt, wait_c_send, 0)

    def wait_d(j, carry):
        copy_d(lax.rem(a + j, ny), a).wait_send()
        copy_d(a, lax.rem(a + j, ny)).wait_recv()
        return carry

    lax.fori_loop(1, ny, wait_d, 0)
    for u in range(nt):
        recv_d[a, u // kb, (u % kb) * SUB:(u % kb + 1) * SUB, :] = recv_c[u]
    for s in range(ny):
        block = recv_d[s]
        if divisor is not None:
            block = block / divisor
        o_ref[:, :, s * LANES:(s + 1) * LANES] = block
    if orthonormalize:
        orthonormal_rows(o_ref)


def orthonormal_rows(rows_ref):
    nb, k = rows_ref.shape[0], rows_ref.shape[1]
    gram = jnp.stack([
        lax.dot_general(rows_ref[b], rows_ref[b], (((1,), (1,)), ((), ())),
                        precision=HIGHEST, preferred_element_type=jnp.float32)
        for b in range(nb)
    ])
    r_idx = lax.broadcasted_iota(jnp.int32, (nb, k, k), 1)
    c_idx = lax.broadcasted_iota(jnp.int32, (nb, k, k), 2)
    diag = r_idx == c_idx
    trace_value = jnp.sum(jnp.sum(jnp.where(diag, gram, 0.0), axis=2, keepdims=True),
                          axis=1, keepdims=True)
    shift_value = 1e-06 * (trace_value / k + 1.0)
    work = gram + jnp.where(diag, shift_value, 0.0)
    sub_idx = r_idx[:, :, :1]
    lane_idx = c_idx[:, :1, :]
    inverse = jnp.where(diag, 1.0, 0.0)
    for j in range(k):
        row = work[:, j:j + 1, :]
        inv_root = lax.rsqrt(row[:, :, j:j + 1])
        col = jnp.where(sub_idx >= j, work[:, :, j:j + 1] * inv_root, 0.0)
        row = jnp.where(lane_idx >= j, row * inv_root, 0.0)
        work = work - col * row
        solved = inverse[:, j:j + 1, :] * inv_root
        below = jnp.where(sub_idx > j, col, 0.0)
        inverse = jnp.where(sub_idx == j, solved, inverse - below * solved)
    for b in range(nb):
        rows_ref[b] = jnp.dot(inverse[b], rows_ref[b], precision=HIGHEST,
                              preferred_element_type=jnp.float32)


def write_pieces(value_ref, patterns, stacked):
    for b in range(value_ref.shape[0]):
        value = value_ref[b]
        k = value.shape[0]
        hi = value.astype(jnp.bfloat16)
        rest = value - hi.astype(jnp.float32)
        mid = rest.astype(jnp.bfloat16)
        lo = (rest - mid.astype(jnp.float32)).astype(jnp.bfloat16)
        parts = (hi, mid, lo)
        for pattern, out_ref in zip(patterns, stacked):
            for g, piece in enumerate(pattern):
                out_ref[b, g * k:(g + 1) * k, :] = parts[piece]


def factors_kernel(nx, ny, divisor, x_ref, mq_ref, mk_ref, left_ref, lefts_ref, right_ref,
                   rights_ref, pair_ref, local_ref, *scratch):
    first, second = scratch[:13], scratch[13:]
    allreduce_body(nx, ny, True, None, x_ref, left_ref, *first)
    write_pieces(left_ref, ((0, 0, 1, 0, 1, 2), (0, 1)), (lefts_ref, pair_ref))
    k = left_ref.shape[1]
    width = 256
    for b, m_ref in enumerate((mq_ref, mk_ref)):
        pair = pair_ref[b]
        top = lefts_ref[b, :k, :]
        for c in range(m_ref.shape[1] // width):
            block = m_ref[:, c * width:(c + 1) * width]
            hi = block.astype(jnp.bfloat16)
            mid = (block - hi.astype(jnp.float32)).astype(jnp.bfloat16)
            both = jnp.dot(pair, hi, preferred_element_type=jnp.float32)
            cross = jnp.dot(top, mid, preferred_element_type=jnp.float32)
            local_ref[b, :, c * width:(c + 1) * width] = both[:k] + (both[k:] + cross)
    allreduce_body(nx, ny, False, divisor, local_ref, right_ref, *second, with_barrier=False)
    write_pieces(right_ref, ((0, 1, 0, 2, 1, 0),), (rights_ref,))


def allreduce_scratch(nx, ny, nb, rows):
    vmem = pltpu.VMEM
    nt = nb * (rows // SUB)
    return [
        vmem((ny, nb, rows, LANES), jnp.float32),
        vmem((nt, SUB, LANES), jnp.float32),
        vmem((nx, SUB, LANES), jnp.float32),
        vmem((nt, SUB, LANES), jnp.float32),
        vmem((ny, nb, rows, LANES), jnp.float32),
        pltpu.SemaphoreType.DMA((ny,)),
        pltpu.SemaphoreType.DMA((ny,)),
        pltpu.SemaphoreType.DMA((nx,)),
        pltpu.SemaphoreType.DMA((nx,)),
        pltpu.SemaphoreType.DMA((nt,)),
        pltpu.SemaphoreType.DMA((nt,)),
        pltpu.SemaphoreType.DMA((ny,)),
        pltpu.SemaphoreType.DMA((ny,)),
    ]


def factors(x, query_merged, key_merged, nx, ny, divisor):
    nb, rows, cols = x.shape
    assert cols == ny * LANES and rows % SUB == 0
    assert nx % (nb * (rows // SUB)) == 0
    vmem = pltpu.VMEM
    f32, bf16 = jnp.float32, jnp.bfloat16
    return pl.pallas_call(
        functools.partial(factors_kernel, nx, ny, divisor),
        out_shape=[
            jax.ShapeDtypeStruct(x.shape, f32),
            jax.ShapeDtypeStruct((nb, 6 * rows, cols), bf16),
            jax.ShapeDtypeStruct(x.shape, f32),
            jax.ShapeDtypeStruct((nb, 6 * rows, cols), bf16),
        ],
        in_specs=[pl.BlockSpec(memory_space=vmem)] * 3,
        out_specs=[pl.BlockSpec(memory_space=vmem)] * 4,
        scratch_shapes=[vmem((nb, 2 * rows, cols), bf16), vmem(x.shape, f32)]
        + allreduce_scratch(nx, ny, nb, rows) + allreduce_scratch(nx, ny, nb, rows),
        compiler_params=pltpu.CompilerParams(
            collective_id=0, has_side_effects=True,
            vmem_limit_bytes=24 * 1024 * 1024,
        ),
    )(x, query_merged, key_merged)


def allreduce(x, nx, ny, collective_id, orthonormalize=False, divisor=None, patterns=()):
    nb, rows, cols = x.shape
    assert cols == ny * LANES and rows % SUB == 0
    nt = nb * (rows // SUB)
    assert nx % nt == 0
    vmem = pltpu.VMEM
    return pl.pallas_call(
        functools.partial(allreduce_kernel, nx, ny, orthonormalize, divisor, patterns),
        out_shape=[jax.ShapeDtypeStruct(x.shape, jnp.float32)] + [
            jax.ShapeDtypeStruct((nb, len(p) * rows, cols), jnp.bfloat16) for p in patterns],
        in_specs=[pl.BlockSpec(memory_space=vmem)],
        out_specs=[pl.BlockSpec(memory_space=vmem)] * (1 + len(patterns)),
        scratch_shapes=[
            vmem((ny, nb, rows, LANES), jnp.float32),
            vmem((nt, SUB, LANES), jnp.float32),
            vmem((nx, SUB, LANES), jnp.float32),
            vmem((nt, SUB, LANES), jnp.float32),
            vmem((ny, nb, rows, LANES), jnp.float32),
            pltpu.SemaphoreType.DMA((ny,)),
            pltpu.SemaphoreType.DMA((ny,)),
            pltpu.SemaphoreType.DMA((nx,)),
            pltpu.SemaphoreType.DMA((nx,)),
            pltpu.SemaphoreType.DMA((nt,)),
            pltpu.SemaphoreType.DMA((nt,)),
            pltpu.SemaphoreType.DMA((ny,)),
            pltpu.SemaphoreType.DMA((ny,)),
        ],
        compiler_params=pltpu.CompilerParams(
            collective_id=collective_id, has_side_effects=True,
            vmem_limit_bytes=8 * 1024 * 1024,
        ),
    )(x)


def gram_of(factor_rows):
    return jnp.einsum("bki,bli->bkl", factor_rows, factor_rows, precision=HIGHEST)


def solve_rows(gram_matrix, factor_rows):
    width = gram_matrix.shape[-1]
    identity = jnp.eye(width, dtype=jnp.float32)
    trace_value = jnp.trace(gram_matrix, axis1=1, axis2=2)
    shift_value = 1e-06 * (trace_value / width + 1.0)
    lower_factor = jnp.linalg.cholesky(gram_matrix + shift_value[:, None, None] * identity)
    return lax.linalg.triangular_solve(lower_factor, factor_rows, left_side=True, lower=True)


def on_device(nx, ny, normed, grad_query, grad_key, error, start_factor):
    replicas = nx * ny
    query_grad = lax.dot_general(normed, grad_query, CONTRACT, preferred_element_type=jnp.float32)
    key_grad = lax.dot_general(normed, grad_key, CONTRACT, preferred_element_type=jnp.float32)
    query_merged = query_grad + error[0].astype(jnp.float32)
    key_merged = key_grad + error[1].astype(jnp.float32)
    merged = jnp.stack([query_merged, key_merged])
    m_hi, m_mid, m_lo = split3(merged)
    s_hi, s_mid, s_lo = split3(start_factor)
    left_local = combine6(*rows_times(
        [[s_hi, s_mid, s_lo], [s_hi, s_mid], [s_hi]], [m_hi, m_mid, m_lo], "bkj,bij->bki"))
    left_rows, lefts, right_rows, rights = factors(
        left_local, query_merged, key_merged, nx, ny, float(replicas))
    approx = jnp.einsum("bki,bkj->bij", lefts, rights, preferred_element_type=jnp.float32)
    return ((merged - approx).astype(jnp.bfloat16), left_rows, right_rows)


def split3(x):
    hi = lax.reduce_precision(x, exponent_bits=8, mantissa_bits=7)
    rest = x - hi
    mid = lax.reduce_precision(rest, exponent_bits=8, mantissa_bits=7)
    lo = rest - mid
    return (hi.astype(jnp.bfloat16), mid.astype(jnp.bfloat16), lo.astype(jnp.bfloat16))


def rows_times(row_groups, big_pieces, spec):
    out = []
    for group, big in zip(row_groups, big_pieces):
        k = group[0].shape[1]
        prod = jnp.einsum(spec, jnp.concatenate(group, axis=1), big,
                          preferred_element_type=jnp.float32)
        out.append([prod[:, g * k:(g + 1) * k] for g in range(len(group))])
    return out


def combine6(first, second, third):
    small = (first[2] + second[1]) + third[0]
    return first[0] + ((first[1] + second[0]) + small)


def solution(mesh):
    nx, ny = mesh.shape["gx"], mesh.shape["gy"]
    placed = (
        P(("gx", "gy"), None),
        P(("gx", "gy"), None),
        P(("gx", "gy"), None),
        P(("gx", "gy"), None, None),
        P(),
    )
    return jax.shard_map(
        functools.partial(on_device, nx, ny),
        mesh=mesh,
        in_specs=placed,
        out_specs=(P(("gx", "gy"), None, None), P(), P()),
        check_vma=False,
    )
```

```python
import functools

import jax
import jax.numpy as jnp
from jax import lax
from jax.experimental import pallas as pl
from jax.experimental.pallas import tpu as pltpu
from jax.sharding import PartitionSpec as P

HIGHEST = lax.Precision.HIGHEST
HIGH = lax.Precision.HIGH
CONTRACT = (((0,), (0,)), ((), ()))
MESH_ID = pl.DeviceIdType.MESH
LANES = 128
SUB = 8


def allreduce_kernel(nx, ny, orthonormalize, divisor, patterns, x_ref, o_ref, *refs):
    stacked = refs[:len(patterns)]
    allreduce_body(nx, ny, orthonormalize, divisor, x_ref, o_ref, *refs[len(patterns):])
    for b in range(o_ref.shape[0]):
        value = o_ref[b]
        k = value.shape[0]
        hi = value.astype(jnp.bfloat16)
        rest = value - hi.astype(jnp.float32)
        mid = rest.astype(jnp.bfloat16)
        lo = (rest - mid.astype(jnp.float32)).astype(jnp.bfloat16)
        parts = (hi, mid, lo)
        for pattern, out_ref in zip(patterns, stacked):
            for g, piece in enumerate(pattern):
                out_ref[b, g * k:(g + 1) * k, :] = parts[piece]


def allreduce_body(nx, ny, orthonormalize, divisor, x_ref, o_ref, recv_a, p_t, recv_b, recv_c, recv_d,
                     sa, ra, sb, rb, sc, rc, sd, rd, with_barrier=True, idle_work=None):
    h = lax.axis_index("gx")
    a = lax.axis_index("gy")
    nb, rows = x_ref.shape[0], x_ref.shape[1]
    kb = rows // SUB
    nt = nb * kb

    barrier = pltpu.get_barrier_semaphore()

    def signal_y(j, carry):
        pl.semaphore_signal(barrier, 1, device_id=(h, lax.rem(a + j, ny)),
                            device_id_type=MESH_ID)
        return carry

    def signal_x(j, carry):
        pl.semaphore_signal(barrier, 1, device_id=(lax.rem(h + j, nx), a),
                            device_id_type=MESH_ID)
        return carry

    if with_barrier:
        lax.fori_loop(1, ny, signal_y, 0)
        lax.fori_loop(1, nx, signal_x, 0)
        pl.semaphore_wait(barrier, (ny - 1) + (nx - 1))

    def copy_a(peer, slot_src):
        return pltpu.make_async_remote_copy(
            src_ref=x_ref.at[:, :, pl.ds(pl.multiple_of(peer * LANES, LANES), LANES)],
            dst_ref=recv_a.at[slot_src],
            send_sem=sa.at[peer],
            recv_sem=ra.at[slot_src],
            device_id=(h, peer),
            device_id_type=MESH_ID,
        )

    def start_a(j, carry):
        copy_a(lax.rem(a + j, ny), a).start()
        return carry

    lax.fori_loop(1, ny, start_a, 0)
    recv_a[a] = x_ref[:, :, pl.ds(pl.multiple_of(a * LANES, LANES), LANES)]
    if idle_work is not None:
        idle_work()

    def wait_a(j, carry):
        copy_a(lax.rem(a + j, ny), a).wait_send()
        copy_a(a, lax.rem(a + j, ny)).wait_recv()
        return carry

    lax.fori_loop(1, ny, wait_a, 0)
    part = jnp.sum(recv_a[...], axis=0)
    for u in range(nt):
        p_t[u] = part[u // kb, (u % kb) * SUB:(u % kb + 1) * SUB, :]

    def copy_b(peer, slot_src, tile):
        return pltpu.make_async_remote_copy(
            src_ref=p_t.at[tile],
            dst_ref=recv_b.at[slot_src],
            send_sem=sb.at[peer],
            recv_sem=rb.at[slot_src],
            device_id=(peer, a),
            device_id_type=MESH_ID,
        )

    def start_b(j, carry):
        peer = lax.rem(h + j, nx)
        copy_b(peer, h, lax.rem(peer, nt)).start()
        return carry

    lax.fori_loop(1, nx, start_b, 0)
    own = lax.rem(h, nt)
    recv_b[h] = p_t[own]

    def wait_b(j, carry):
        peer = lax.rem(h + j, nx)
        copy_b(peer, h, lax.rem(peer, nt)).wait_send()
        copy_b(h, peer, own).wait_recv()
        return carry

    lax.fori_loop(1, nx, wait_b, 0)
    recv_c[own] = jnp.sum(recv_b[...], axis=0)

    base = h - own

    def copy_c(peer_tile, slot_tile):
        return pltpu.make_async_remote_copy(
            src_ref=recv_c.at[slot_tile],
            dst_ref=recv_c.at[slot_tile],
            send_sem=sc.at[peer_tile],
            recv_sem=rc.at[slot_tile],
            device_id=(base + peer_tile, a),
            device_id_type=MESH_ID,
        )

    def start_c(j, carry):
        copy_c(lax.rem(own + j, nt), own).start()
        return carry

    def copy_d_tile(peer, tile):
        row0 = pl.multiple_of(lax.rem(tile, kb) * SUB, SUB)
        return pltpu.make_async_remote_copy(
            src_ref=recv_c.at[tile],
            dst_ref=recv_d.at[a, tile // kb, pl.ds(row0, SUB), :],
            send_sem=sd.at[peer],
            recv_sem=rd.at[a],
            device_id=(h, peer),
            device_id_type=MESH_ID,
        )

    def copy_d(peer, slot_src):
        return pltpu.make_async_remote_copy(
            src_ref=recv_d.at[slot_src],
            dst_ref=recv_d.at[slot_src],
            send_sem=sd.at[peer],
            recv_sem=rd.at[slot_src],
            device_id=(h, peer),
            device_id_type=MESH_ID,
        )

    def forward(tile):
        def start_d(j, carry):
            copy_d_tile(lax.rem(a + j, ny), tile).start()
            return carry

        lax.fori_loop(1, ny, start_d, 0)

    lax.fori_loop(1, nt, start_c, 0)
    forward(own)

    def wait_c(j, carry):
        other = lax.rem(own + j, nt)
        copy_c(own, other).wait_recv()
        forward(other)
        return carry

    lax.fori_loop(1, nt, wait_c, 0)

    def wait_c_send(j, carry):
        copy_c(lax.rem(own + j, nt), own).wait_send()
        return carry

    lax.fori_loop(1, nt, wait_c_send, 0)

    def wait_d(j, carry):
        copy_d(lax.rem(a + j, ny), a).wait_send()
        copy_d(a, lax.rem(a + j, ny)).wait_recv()
        return carry

    lax.fori_loop(1, ny, wait_d, 0)
    for u in range(nt):
        recv_d[a, u // kb, (u % kb) * SUB:(u % kb + 1) * SUB, :] = recv_c[u]
    for s in range(ny):
        block = recv_d[s]
        if divisor is not None:
            block = block / divisor
        o_ref[:, :, s * LANES:(s + 1) * LANES] = block
    if orthonormalize:
        orthonormal_rows(o_ref)


def orthonormal_rows(rows_ref):
    nb, k = rows_ref.shape[0], rows_ref.shape[1]
    gram = jnp.stack([
        lax.dot_general(rows_ref[b], rows_ref[b], (((1,), (1,)), ((), ())),
                        precision=HIGHEST, preferred_element_type=jnp.float32)
        for b in range(nb)
    ])
    r_idx = lax.broadcasted_iota(jnp.int32, (nb, k, k), 1)
    c_idx = lax.broadcasted_iota(jnp.int32, (nb, k, k), 2)
    diag = r_idx == c_idx
    trace_value = jnp.sum(jnp.sum(jnp.where(diag, gram, 0.0), axis=2, keepdims=True),
                          axis=1, keepdims=True)
    shift_value = 1e-06 * (trace_value / k + 1.0)
    work = gram + jnp.where(diag, shift_value, 0.0)
    sub_idx = r_idx[:, :, :1]
    lane_idx = c_idx[:, :1, :]
    inverse = jnp.where(diag, 1.0, 0.0)
    for j in range(k):
        row = work[:, j:j + 1, :]
        inv_root = lax.rsqrt(row[:, :, j:j + 1])
        col = jnp.where(sub_idx >= j, work[:, :, j:j + 1] * inv_root, 0.0)
        row = jnp.where(lane_idx >= j, row * inv_root, 0.0)
        work = work - col * row
        solved = inverse[:, j:j + 1, :] * inv_root
        below = jnp.where(sub_idx > j, col, 0.0)
        inverse = jnp.where(sub_idx == j, solved, inverse - below * solved)
    for b in range(nb):
        rows_ref[b] = jnp.dot(inverse[b], rows_ref[b], precision=HIGHEST,
                              preferred_element_type=jnp.float32)


def write_pieces(value_ref, patterns, stacked):
    for b in range(value_ref.shape[0]):
        value = value_ref[b]
        k = value.shape[0]
        hi = value.astype(jnp.bfloat16)
        rest = value - hi.astype(jnp.float32)
        mid = rest.astype(jnp.bfloat16)
        lo = (rest - mid.astype(jnp.float32)).astype(jnp.bfloat16)
        parts = (hi, mid, lo)
        for pattern, out_ref in zip(patterns, stacked):
            for g, piece in enumerate(pattern):
                out_ref[b, g * k:(g + 1) * k, :] = parts[piece]


def factors_kernel(nx, ny, divisor, x_ref, mq_ref, mk_ref, left_ref, lefts_ref, right_ref,
                   rights_ref, pair_ref, local_ref, m_hi_ref, m_mid_ref, *scratch):
    first, second = scratch[:13], scratch[13:]
    width = 256
    merged_refs = (mq_ref, mk_ref)

    def split_merged():
        for b, m_ref in enumerate(merged_refs):
            for c in range(m_ref.shape[1] // width):
                block = m_ref[:, c * width:(c + 1) * width]
                hi = block.astype(jnp.bfloat16)
                m_hi_ref[b, :, c * width:(c + 1) * width] = hi
                m_mid_ref[b, :, c * width:(c + 1) * width] = (
                    block - hi.astype(jnp.float32)).astype(jnp.bfloat16)

    allreduce_body(nx, ny, True, None, x_ref, left_ref, *first, idle_work=split_merged)
    write_pieces(left_ref, ((0, 0, 1, 0, 1, 2), (0, 1)), (lefts_ref, pair_ref))
    k = left_ref.shape[1]
    for b in range(len(merged_refs)):
        both = jnp.dot(pair_ref[b], m_hi_ref[b], preferred_element_type=jnp.float32)
        cross = jnp.dot(lefts_ref[b, :k, :], m_mid_ref[b], preferred_element_type=jnp.float32)
        local_ref[b] = both[:k] + (both[k:] + cross)
    allreduce_body(nx, ny, False, divisor, local_ref, right_ref, *second, with_barrier=False)
    write_pieces(right_ref, ((0, 1, 0, 2, 1, 0),), (rights_ref,))


def allreduce_scratch(nx, ny, nb, rows):
    vmem = pltpu.VMEM
    nt = nb * (rows // SUB)
    return [
        vmem((ny, nb, rows, LANES), jnp.float32),
        vmem((nt, SUB, LANES), jnp.float32),
        vmem((nx, SUB, LANES), jnp.float32),
        vmem((nt, SUB, LANES), jnp.float32),
        vmem((ny, nb, rows, LANES), jnp.float32),
        pltpu.SemaphoreType.DMA((ny,)),
        pltpu.SemaphoreType.DMA((ny,)),
        pltpu.SemaphoreType.DMA((nx,)),
        pltpu.SemaphoreType.DMA((nx,)),
        pltpu.SemaphoreType.DMA((nt,)),
        pltpu.SemaphoreType.DMA((nt,)),
        pltpu.SemaphoreType.DMA((ny,)),
        pltpu.SemaphoreType.DMA((ny,)),
    ]


def factors(x, query_merged, key_merged, nx, ny, divisor):
    nb, rows, cols = x.shape
    assert cols == ny * LANES and rows % SUB == 0
    assert nx % (nb * (rows // SUB)) == 0
    vmem = pltpu.VMEM
    f32, bf16 = jnp.float32, jnp.bfloat16
    return pl.pallas_call(
        functools.partial(factors_kernel, nx, ny, divisor),
        out_shape=[
            jax.ShapeDtypeStruct(x.shape, f32),
            jax.ShapeDtypeStruct((nb, 6 * rows, cols), bf16),
            jax.ShapeDtypeStruct(x.shape, f32),
            jax.ShapeDtypeStruct((nb, 6 * rows, cols), bf16),
        ],
        in_specs=[pl.BlockSpec(memory_space=vmem)] * 3,
        out_specs=[pl.BlockSpec(memory_space=vmem)] * 4,
        scratch_shapes=[vmem((nb, 2 * rows, cols), bf16), vmem(x.shape, f32),
                        vmem((2,) + query_merged.shape, bf16), vmem((2,) + query_merged.shape, bf16)]
        + allreduce_scratch(nx, ny, nb, rows) + allreduce_scratch(nx, ny, nb, rows),
        compiler_params=pltpu.CompilerParams(
            collective_id=0, has_side_effects=True,
            vmem_limit_bytes=24 * 1024 * 1024,
        ),
    )(x, query_merged, key_merged)


def allreduce(x, nx, ny, collective_id, orthonormalize=False, divisor=None, patterns=()):
    nb, rows, cols = x.shape
    assert cols == ny * LANES and rows % SUB == 0
    nt = nb * (rows // SUB)
    assert nx % nt == 0
    vmem = pltpu.VMEM
    return pl.pallas_call(
        functools.partial(allreduce_kernel, nx, ny, orthonormalize, divisor, patterns),
        out_shape=[jax.ShapeDtypeStruct(x.shape, jnp.float32)] + [
            jax.ShapeDtypeStruct((nb, len(p) * rows, cols), jnp.bfloat16) for p in patterns],
        in_specs=[pl.BlockSpec(memory_space=vmem)],
        out_specs=[pl.BlockSpec(memory_space=vmem)] * (1 + len(patterns)),
        scratch_shapes=[
            vmem((ny, nb, rows, LANES), jnp.float32),
            vmem((nt, SUB, LANES), jnp.float32),
            vmem((nx, SUB, LANES), jnp.float32),
            vmem((nt, SUB, LANES), jnp.float32),
            vmem((ny, nb, rows, LANES), jnp.float32),
            pltpu.SemaphoreType.DMA((ny,)),
            pltpu.SemaphoreType.DMA((ny,)),
            pltpu.SemaphoreType.DMA((nx,)),
            pltpu.SemaphoreType.DMA((nx,)),
            pltpu.SemaphoreType.DMA((nt,)),
            pltpu.SemaphoreType.DMA((nt,)),
            pltpu.SemaphoreType.DMA((ny,)),
            pltpu.SemaphoreType.DMA((ny,)),
        ],
        compiler_params=pltpu.CompilerParams(
            collective_id=collective_id, has_side_effects=True,
            vmem_limit_bytes=8 * 1024 * 1024,
        ),
    )(x)


def gram_of(factor_rows):
    return jnp.einsum("bki,bli->bkl", factor_rows, factor_rows, precision=HIGHEST)


def solve_rows(gram_matrix, factor_rows):
    width = gram_matrix.shape[-1]
    identity = jnp.eye(width, dtype=jnp.float32)
    trace_value = jnp.trace(gram_matrix, axis1=1, axis2=2)
    shift_value = 1e-06 * (trace_value / width + 1.0)
    lower_factor = jnp.linalg.cholesky(gram_matrix + shift_value[:, None, None] * identity)
    return lax.linalg.triangular_solve(lower_factor, factor_rows, left_side=True, lower=True)


def on_device(nx, ny, normed, grad_query, grad_key, error, start_factor):
    replicas = nx * ny
    query_grad = lax.dot_general(normed, grad_query, CONTRACT, preferred_element_type=jnp.float32)
    key_grad = lax.dot_general(normed, grad_key, CONTRACT, preferred_element_type=jnp.float32)
    query_merged = query_grad + error[0].astype(jnp.float32)
    key_merged = key_grad + error[1].astype(jnp.float32)
    merged = jnp.stack([query_merged, key_merged])
    m_hi, m_mid, m_lo = split3(merged)
    s_hi, s_mid, s_lo = split3(start_factor)
    left_local = combine6(*rows_times(
        [[s_hi, s_mid, s_lo], [s_hi, s_mid], [s_hi]], [m_hi, m_mid, m_lo], "bkj,bij->bki"))
    left_rows, lefts, right_rows, rights = factors(
        left_local, query_merged, key_merged, nx, ny, float(replicas))
    approx = jnp.einsum("bki,bkj->bij", lefts, rights, preferred_element_type=jnp.float32)
    return ((merged - approx).astype(jnp.bfloat16), left_rows, right_rows)


def split3(x):
    hi = lax.reduce_precision(x, exponent_bits=8, mantissa_bits=7)
    rest = x - hi
    mid = lax.reduce_precision(rest, exponent_bits=8, mantissa_bits=7)
    lo = rest - mid
    return (hi.astype(jnp.bfloat16), mid.astype(jnp.bfloat16), lo.astype(jnp.bfloat16))


def rows_times(row_groups, big_pieces, spec):
    out = []
    for group, big in zip(row_groups, big_pieces):
        k = group[0].shape[1]
        prod = jnp.einsum(spec, jnp.concatenate(group, axis=1), big,
                          preferred_element_type=jnp.float32)
        out.append([prod[:, g * k:(g + 1) * k] for g in range(len(group))])
    return out


def combine6(first, second, third):
    small = (first[2] + second[1]) + third[0]
    return first[0] + ((first[1] + second[0]) + small)


def solution(mesh):
    nx, ny = mesh.shape["gx"], mesh.shape["gy"]
    placed = (
        P(("gx", "gy"), None),
        P(("gx", "gy"), None),
        P(("gx", "gy"), None),
        P(("gx", "gy"), None, None),
        P(),
    )
    return jax.shard_map(
        functools.partial(on_device, nx, ny),
        mesh=mesh,
        in_specs=placed,
        out_specs=(P(("gx", "gy"), None, None), P(), P()),
        check_vma=False,
    )
```

```python
import functools

import jax
import jax.numpy as jnp
from jax import lax
from jax.experimental import pallas as pl
from jax.experimental.pallas import tpu as pltpu
from jax.sharding import PartitionSpec as P

HIGHEST = lax.Precision.HIGHEST
HIGH = lax.Precision.HIGH
CONTRACT = (((0,), (0,)), ((), ()))
MESH_ID = pl.DeviceIdType.MESH
LANES = 128
SUB = 8


def allreduce_kernel(nx, ny, orthonormalize, divisor, patterns, x_ref, o_ref, *refs):
    stacked = refs[:len(patterns)]
    allreduce_body(nx, ny, orthonormalize, divisor, x_ref, o_ref, *refs[len(patterns):])
    for b in range(o_ref.shape[0]):
        value = o_ref[b]
        k = value.shape[0]
        hi = value.astype(jnp.bfloat16)
        rest = value - hi.astype(jnp.float32)
        mid = rest.astype(jnp.bfloat16)
        lo = (rest - mid.astype(jnp.float32)).astype(jnp.bfloat16)
        parts = (hi, mid, lo)
        for pattern, out_ref in zip(patterns, stacked):
            for g, piece in enumerate(pattern):
                out_ref[b, g * k:(g + 1) * k, :] = parts[piece]


def allreduce_body(nx, ny, orthonormalize, divisor, x_ref, o_ref, recv_a, p_t, recv_b, recv_c, recv_d,
                     sa, ra, sb, rb, sc, rc, sd, rd, with_barrier=True, idle_work=None):
    h = lax.axis_index("gx")
    a = lax.axis_index("gy")
    nb, rows = x_ref.shape[0], x_ref.shape[1]
    kb = rows // SUB
    nt = nb * kb

    barrier = pltpu.get_barrier_semaphore()

    def signal_y(j, carry):
        pl.semaphore_signal(barrier, 1, device_id=(h, lax.rem(a + j, ny)),
                            device_id_type=MESH_ID)
        return carry

    def signal_x(j, carry):
        pl.semaphore_signal(barrier, 1, device_id=(lax.rem(h + j, nx), a),
                            device_id_type=MESH_ID)
        return carry

    if with_barrier:
        lax.fori_loop(1, ny, signal_y, 0)
        lax.fori_loop(1, nx, signal_x, 0)
        pl.semaphore_wait(barrier, (ny - 1) + (nx - 1))

    def copy_a(peer, slot_src):
        return pltpu.make_async_remote_copy(
            src_ref=x_ref.at[:, :, pl.ds(pl.multiple_of(peer * LANES, LANES), LANES)],
            dst_ref=recv_a.at[slot_src],
            send_sem=sa.at[peer],
            recv_sem=ra.at[slot_src],
            device_id=(h, peer),
            device_id_type=MESH_ID,
        )

    def start_a(j, carry):
        copy_a(lax.rem(a + j, ny), a).start()
        return carry

    lax.fori_loop(1, ny, start_a, 0)
    recv_a[a] = x_ref[:, :, pl.ds(pl.multiple_of(a * LANES, LANES), LANES)]
    if idle_work is not None:
        idle_work()

    def wait_a(j, carry):
        copy_a(lax.rem(a + j, ny), a).wait_send()
        copy_a(a, lax.rem(a + j, ny)).wait_recv()
        return carry

    lax.fori_loop(1, ny, wait_a, 0)
    part = jnp.sum(recv_a[...], axis=0)
    for u in range(nt):
        p_t[u] = part[u // kb, (u % kb) * SUB:(u % kb + 1) * SUB, :]

    def copy_b(peer, slot_src, tile):
        return pltpu.make_async_remote_copy(
            src_ref=p_t.at[tile],
            dst_ref=recv_b.at[slot_src],
            send_sem=sb.at[peer],
            recv_sem=rb.at[slot_src],
            device_id=(peer, a),
            device_id_type=MESH_ID,
        )

    def start_b(j, carry):
        peer = lax.rem(h + j, nx)
        copy_b(peer, h, lax.rem(peer, nt)).start()
        return carry

    lax.fori_loop(1, nx, start_b, 0)
    own = lax.rem(h, nt)
    recv_b[h] = p_t[own]

    def wait_b(j, carry):
        peer = lax.rem(h + j, nx)
        copy_b(peer, h, lax.rem(peer, nt)).wait_send()
        copy_b(h, peer, own).wait_recv()
        return carry

    lax.fori_loop(1, nx, wait_b, 0)
    recv_c[own] = jnp.sum(recv_b[...], axis=0)

    base = h - own

    def copy_c(peer_tile, slot_tile):
        return pltpu.make_async_remote_copy(
            src_ref=recv_c.at[slot_tile],
            dst_ref=recv_c.at[slot_tile],
            send_sem=sc.at[peer_tile],
            recv_sem=rc.at[slot_tile],
            device_id=(base + peer_tile, a),
            device_id_type=MESH_ID,
        )

    def start_c(j, carry):
        copy_c(lax.rem(own + j, nt), own).start()
        return carry

    def copy_d_tile(peer, tile):
        row0 = pl.multiple_of(lax.rem(tile, kb) * SUB, SUB)
        return pltpu.make_async_remote_copy(
            src_ref=recv_c.at[tile],
            dst_ref=recv_d.at[a, tile // kb, pl.ds(row0, SUB), :],
            send_sem=sd.at[peer],
            recv_sem=rd.at[a],
            device_id=(h, peer),
            device_id_type=MESH_ID,
        )

    def copy_d(peer, slot_src):
        return pltpu.make_async_remote_copy(
            src_ref=recv_d.at[slot_src],
            dst_ref=recv_d.at[slot_src],
            send_sem=sd.at[peer],
            recv_sem=rd.at[slot_src],
            device_id=(h, peer),
            device_id_type=MESH_ID,
        )

    def forward(tile):
        def start_d(j, carry):
            copy_d_tile(lax.rem(a + j, ny), tile).start()
            return carry

        lax.fori_loop(1, ny, start_d, 0)

    lax.fori_loop(1, nt, start_c, 0)
    forward(own)

    def wait_c(j, carry):
        other = lax.rem(own + j, nt)
        copy_c(own, other).wait_recv()
        forward(other)
        return carry

    lax.fori_loop(1, nt, wait_c, 0)

    def wait_c_send(j, carry):
        copy_c(lax.rem(own + j, nt), own).wait_send()
        return carry

    lax.fori_loop(1, nt, wait_c_send, 0)

    def wait_d(j, carry):
        copy_d(lax.rem(a + j, ny), a).wait_send()
        copy_d(a, lax.rem(a + j, ny)).wait_recv()
        return carry

    lax.fori_loop(1, ny, wait_d, 0)
    for u in range(nt):
        recv_d[a, u // kb, (u % kb) * SUB:(u % kb + 1) * SUB, :] = recv_c[u]
    for s in range(ny):
        block = recv_d[s]
        if divisor is not None:
            block = block / divisor
        o_ref[:, :, s * LANES:(s + 1) * LANES] = block
    if orthonormalize:
        orthonormal_rows(o_ref)


def orthonormal_rows(rows_ref):
    nb, k = rows_ref.shape[0], rows_ref.shape[1]
    gram = jnp.stack([
        lax.dot_general(rows_ref[b], rows_ref[b], (((1,), (1,)), ((), ())),
                        precision=HIGHEST, preferred_element_type=jnp.float32)
        for b in range(nb)
    ])
    r_idx = lax.broadcasted_iota(jnp.int32, (nb, k, k), 1)
    c_idx = lax.broadcasted_iota(jnp.int32, (nb, k, k), 2)
    diag = r_idx == c_idx
    trace_value = jnp.sum(jnp.sum(jnp.where(diag, gram, 0.0), axis=2, keepdims=True),
                          axis=1, keepdims=True)
    shift_value = 1e-06 * (trace_value / k + 1.0)
    work = gram + jnp.where(diag, shift_value, 0.0)
    sub_idx = r_idx[:, :, :1]
    lane_idx = c_idx[:, :1, :]
    inverse = jnp.where(diag, 1.0, 0.0)
    for j in range(k):
        row = work[:, j:j + 1, :]
        inv_root = lax.rsqrt(row[:, :, j:j + 1])
        col = jnp.where(sub_idx >= j, work[:, :, j:j + 1] * inv_root, 0.0)
        row = jnp.where(lane_idx >= j, row * inv_root, 0.0)
        work = work - col * row
        solved = inverse[:, j:j + 1, :] * inv_root
        below = jnp.where(sub_idx > j, col, 0.0)
        inverse = jnp.where(sub_idx == j, solved, inverse - below * solved)
    for b in range(nb):
        rows_ref[b] = jnp.dot(inverse[b], rows_ref[b], precision=HIGHEST,
                              preferred_element_type=jnp.float32)


def write_pieces(value_ref, patterns, stacked):
    for b in range(value_ref.shape[0]):
        value = value_ref[b]
        k = value.shape[0]
        hi = value.astype(jnp.bfloat16)
        rest = value - hi.astype(jnp.float32)
        mid = rest.astype(jnp.bfloat16)
        lo = (rest - mid.astype(jnp.float32)).astype(jnp.bfloat16)
        parts = (hi, mid, lo)
        for pattern, out_ref in zip(patterns, stacked):
            for g, piece in enumerate(pattern):
                out_ref[b, g * k:(g + 1) * k, :] = parts[piece]


def factors_kernel(nx, ny, divisor, x_ref, mq_ref, mk_ref, left_ref, lefts_ref, right_ref,
                   rights_ref, pair_ref, local_ref, m_hi_ref, m_mid_ref, *scratch):
    first, second = scratch[:13], scratch[13:]
    width = 256
    merged_refs = (mq_ref, mk_ref)

    def split_merged():
        for b, m_ref in enumerate(merged_refs):
            for c in range(m_ref.shape[1] // width):
                block = m_ref[:, c * width:(c + 1) * width]
                hi = block.astype(jnp.bfloat16)
                m_hi_ref[b, :, c * width:(c + 1) * width] = hi
                m_mid_ref[b, :, c * width:(c + 1) * width] = (
                    block - hi.astype(jnp.float32)).astype(jnp.bfloat16)

    allreduce_body(nx, ny, True, None, x_ref, left_ref, *first, idle_work=split_merged)
    write_pieces(left_ref, ((0, 0, 1, 0, 1, 2), (0, 1)), (lefts_ref, pair_ref))
    k = left_ref.shape[1]
    for b in range(len(merged_refs)):
        both = jnp.dot(pair_ref[b], m_hi_ref[b], preferred_element_type=jnp.float32)
        cross = jnp.dot(lefts_ref[b, :k, :], m_mid_ref[b], preferred_element_type=jnp.float32)
        local_ref[b] = both[:k] + (both[k:] + cross)
    allreduce_body(nx, ny, False, divisor, local_ref, right_ref, *second, with_barrier=False)
    write_pieces(right_ref, ((0, 1, 0, 2, 1, 0),), (rights_ref,))


def allreduce_scratch(nx, ny, nb, rows):
    vmem = pltpu.VMEM
    nt = nb * (rows // SUB)
    return [
        vmem((ny, nb, rows, LANES), jnp.float32),
        vmem((nt, SUB, LANES), jnp.float32),
        vmem((nx, SUB, LANES), jnp.float32),
        vmem((nt, SUB, LANES), jnp.float32),
        vmem((ny, nb, rows, LANES), jnp.float32),
        pltpu.SemaphoreType.DMA((ny,)),
        pltpu.SemaphoreType.DMA((ny,)),
        pltpu.SemaphoreType.DMA((nx,)),
        pltpu.SemaphoreType.DMA((nx,)),
        pltpu.SemaphoreType.DMA((nt,)),
        pltpu.SemaphoreType.DMA((nt,)),
        pltpu.SemaphoreType.DMA((ny,)),
        pltpu.SemaphoreType.DMA((ny,)),
    ]


def factors(x, query_merged, key_merged, nx, ny, divisor):
    nb, rows, cols = x.shape
    assert cols == ny * LANES and rows % SUB == 0
    assert nx % (nb * (rows // SUB)) == 0
    vmem = pltpu.VMEM
    f32, bf16 = jnp.float32, jnp.bfloat16
    return pl.pallas_call(
        functools.partial(factors_kernel, nx, ny, divisor),
        out_shape=[
            jax.ShapeDtypeStruct(x.shape, f32),
            jax.ShapeDtypeStruct((nb, 6 * rows, cols), bf16),
            jax.ShapeDtypeStruct(x.shape, f32),
            jax.ShapeDtypeStruct((nb, 6 * rows, cols), bf16),
        ],
        in_specs=[pl.BlockSpec(memory_space=vmem)] * 3,
        out_specs=[pl.BlockSpec(memory_space=vmem)] * 4,
        scratch_shapes=[vmem((nb, 2 * rows, cols), bf16), vmem(x.shape, f32),
                        vmem((2,) + query_merged.shape, bf16), vmem((2,) + query_merged.shape, bf16)]
        + allreduce_scratch(nx, ny, nb, rows) + allreduce_scratch(nx, ny, nb, rows),
        compiler_params=pltpu.CompilerParams(
            collective_id=0, has_side_effects=True,
            vmem_limit_bytes=24 * 1024 * 1024,
        ),
    )(x, query_merged, key_merged)


def allreduce(x, nx, ny, collective_id, orthonormalize=False, divisor=None, patterns=()):
    nb, rows, cols = x.shape
    assert cols == ny * LANES and rows % SUB == 0
    nt = nb * (rows // SUB)
    assert nx % nt == 0
    vmem = pltpu.VMEM
    return pl.pallas_call(
        functools.partial(allreduce_kernel, nx, ny, orthonormalize, divisor, patterns),
        out_shape=[jax.ShapeDtypeStruct(x.shape, jnp.float32)] + [
            jax.ShapeDtypeStruct((nb, len(p) * rows, cols), jnp.bfloat16) for p in patterns],
        in_specs=[pl.BlockSpec(memory_space=vmem)],
        out_specs=[pl.BlockSpec(memory_space=vmem)] * (1 + len(patterns)),
        scratch_shapes=[
            vmem((ny, nb, rows, LANES), jnp.float32),
            vmem((nt, SUB, LANES), jnp.float32),
            vmem((nx, SUB, LANES), jnp.float32),
            vmem((nt, SUB, LANES), jnp.float32),
            vmem((ny, nb, rows, LANES), jnp.float32),
            pltpu.SemaphoreType.DMA((ny,)),
            pltpu.SemaphoreType.DMA((ny,)),
            pltpu.SemaphoreType.DMA((nx,)),
            pltpu.SemaphoreType.DMA((nx,)),
            pltpu.SemaphoreType.DMA((nt,)),
            pltpu.SemaphoreType.DMA((nt,)),
            pltpu.SemaphoreType.DMA((ny,)),
            pltpu.SemaphoreType.DMA((ny,)),
        ],
        compiler_params=pltpu.CompilerParams(
            collective_id=collective_id, has_side_effects=True,
            vmem_limit_bytes=8 * 1024 * 1024,
        ),
    )(x)


def gram_of(factor_rows):
    return jnp.einsum("bki,bli->bkl", factor_rows, factor_rows, precision=HIGHEST)


def solve_rows(gram_matrix, factor_rows):
    width = gram_matrix.shape[-1]
    identity = jnp.eye(width, dtype=jnp.float32)
    trace_value = jnp.trace(gram_matrix, axis1=1, axis2=2)
    shift_value = 1e-06 * (trace_value / width + 1.0)
    lower_factor = jnp.linalg.cholesky(gram_matrix + shift_value[:, None, None] * identity)
    return lax.linalg.triangular_solve(lower_factor, factor_rows, left_side=True, lower=True)


def on_device(nx, ny, normed, grad_query, grad_key, error, start_factor):
    replicas = nx * ny
    query_grad = lax.dot_general(normed, grad_query, CONTRACT, preferred_element_type=jnp.float32)
    key_grad = lax.dot_general(normed, grad_key, CONTRACT, preferred_element_type=jnp.float32)
    query_merged = query_grad + error[0].astype(jnp.float32)
    key_merged = key_grad + error[1].astype(jnp.float32)
    merged = jnp.stack([query_merged, key_merged])
    m_hi, m_mid, m_lo = split3(merged)
    s_hi, s_mid, s_lo = split3(start_factor)
    left_local = combine6(*rows_times(
        [[s_hi, s_mid, s_lo], [s_hi, s_mid], [s_hi]], [m_hi, m_mid, m_lo], "bkj,bij->bki"))
    left_rows, lefts, right_rows, rights = factors(
        left_local, query_merged, key_merged, nx, ny, float(replicas))
    approx = jnp.einsum("bki,bkj->bij", lefts, rights, preferred_element_type=jnp.float32)
    k = left_rows.shape[1]
    left_out = exact_sum(lefts[:, :k], lefts[:, 2 * k:3 * k], lefts[:, 5 * k:])
    right_out = exact_sum(rights[:, :k], rights[:, k:2 * k], rights[:, 3 * k:4 * k])
    return ((merged - approx).astype(jnp.bfloat16), left_out, right_out)


def exact_sum(hi, mid, lo):
    f32 = jnp.float32
    return (hi.astype(f32) + mid.astype(f32)) + lo.astype(f32)


def split3(x):
    hi = lax.reduce_precision(x, exponent_bits=8, mantissa_bits=7)
    rest = x - hi
    mid = lax.reduce_precision(rest, exponent_bits=8, mantissa_bits=7)
    lo = rest - mid
    return (hi.astype(jnp.bfloat16), mid.astype(jnp.bfloat16), lo.astype(jnp.bfloat16))


def rows_times(row_groups, big_pieces, spec):
    out = []
    for group, big in zip(row_groups, big_pieces):
        k = group[0].shape[1]
        prod = jnp.einsum(spec, jnp.concatenate(group, axis=1), big,
                          preferred_element_type=jnp.float32)
        out.append([prod[:, g * k:(g + 1) * k] for g in range(len(group))])
    return out


def combine6(first, second, third):
    small = (first[2] + second[1]) + third[0]
    return first[0] + ((first[1] + second[0]) + small)


def solution(mesh):
    nx, ny = mesh.shape["gx"], mesh.shape["gy"]
    placed = (
        P(("gx", "gy"), None),
        P(("gx", "gy"), None),
        P(("gx", "gy"), None),
        P(("gx", "gy"), None, None),
        P(),
    )
    return jax.shard_map(
        functools.partial(on_device, nx, ny),
        mesh=mesh,
        in_specs=placed,
        out_specs=(P(("gx", "gy"), None, None), P(), P()),
        check_vma=False,
    )
```

```python
import functools

import jax
import jax.numpy as jnp
from jax import lax
from jax.experimental import pallas as pl
from jax.experimental.pallas import tpu as pltpu
from jax.sharding import PartitionSpec as P

HIGHEST = lax.Precision.HIGHEST
HIGH = lax.Precision.HIGH
CONTRACT = (((0,), (0,)), ((), ()))
MESH_ID = pl.DeviceIdType.MESH
LANES = 128
SUB = 8


def allreduce_kernel(nx, ny, orthonormalize, divisor, patterns, x_ref, o_ref, *refs):
    stacked = refs[:len(patterns)]
    allreduce_body(nx, ny, orthonormalize, divisor, x_ref, o_ref, *refs[len(patterns):])
    for b in range(o_ref.shape[0]):
        value = o_ref[b]
        k = value.shape[0]
        hi = value.astype(jnp.bfloat16)
        rest = value - hi.astype(jnp.float32)
        mid = rest.astype(jnp.bfloat16)
        lo = (rest - mid.astype(jnp.float32)).astype(jnp.bfloat16)
        parts = (hi, mid, lo)
        for pattern, out_ref in zip(patterns, stacked):
            for g, piece in enumerate(pattern):
                out_ref[b, g * k:(g + 1) * k, :] = parts[piece]


def allreduce_body(nx, ny, orthonormalize, divisor, x_ref, o_ref, recv_a, p_t, recv_b, recv_c, recv_d,
                     sa, ra, sb, rb, sc, rc, sd, rd, with_barrier=True, idle_work=None,
                     produce=None):
    h = lax.axis_index("gx")
    a = lax.axis_index("gy")
    nb, rows = x_ref.shape[0], x_ref.shape[1]
    kb = rows // SUB
    nt = nb * kb

    barrier = pltpu.get_barrier_semaphore()

    def signal_y(j, carry):
        pl.semaphore_signal(barrier, 1, device_id=(h, lax.rem(a + j, ny)),
                            device_id_type=MESH_ID)
        return carry

    def signal_x(j, carry):
        pl.semaphore_signal(barrier, 1, device_id=(lax.rem(h + j, nx), a),
                            device_id_type=MESH_ID)
        return carry

    if with_barrier:
        lax.fori_loop(1, ny, signal_y, 0)
        lax.fori_loop(1, nx, signal_x, 0)
        pl.semaphore_wait(barrier, (ny - 1) + (nx - 1))

    def copy_a(peer, slot_src):
        return pltpu.make_async_remote_copy(
            src_ref=x_ref.at[:, :, pl.ds(pl.multiple_of(peer * LANES, LANES), LANES)],
            dst_ref=recv_a.at[slot_src],
            send_sem=sa.at[peer],
            recv_sem=ra.at[slot_src],
            device_id=(h, peer),
            device_id_type=MESH_ID,
        )

    def start_a(j, carry):
        copy_a(lax.rem(a + j, ny), a).start()
        return carry

    def start_part(b):
        def start_one(j, carry):
            peer = lax.rem(a + j, ny)
            pltpu.make_async_remote_copy(
                src_ref=x_ref.at[b, :, pl.ds(pl.multiple_of(peer * LANES, LANES), LANES)],
                dst_ref=recv_a.at[a, b],
                send_sem=sa.at[peer],
                recv_sem=ra.at[a],
                device_id=(h, peer),
                device_id_type=MESH_ID,
            ).start()
            return carry

        lax.fori_loop(1, ny, start_one, 0)

    if produce is None:
        lax.fori_loop(1, ny, start_a, 0)
    else:
        for b in range(nb):
            produce(b)
            start_part(b)
    recv_a[a] = x_ref[:, :, pl.ds(pl.multiple_of(a * LANES, LANES), LANES)]
    if idle_work is not None:
        idle_work()

    def wait_a(j, carry):
        copy_a(lax.rem(a + j, ny), a).wait_send()
        copy_a(a, lax.rem(a + j, ny)).wait_recv()
        return carry

    lax.fori_loop(1, ny, wait_a, 0)
    part = jnp.sum(recv_a[...], axis=0)
    for u in range(nt):
        p_t[u] = part[u // kb, (u % kb) * SUB:(u % kb + 1) * SUB, :]

    def copy_b(peer, slot_src, tile):
        return pltpu.make_async_remote_copy(
            src_ref=p_t.at[tile],
            dst_ref=recv_b.at[slot_src],
            send_sem=sb.at[peer],
            recv_sem=rb.at[slot_src],
            device_id=(peer, a),
            device_id_type=MESH_ID,
        )

    def start_b(j, carry):
        peer = lax.rem(h + j, nx)
        copy_b(peer, h, lax.rem(peer, nt)).start()
        return carry

    lax.fori_loop(1, nx, start_b, 0)
    own = lax.rem(h, nt)
    recv_b[h] = p_t[own]

    def wait_b(j, carry):
        peer = lax.rem(h + j, nx)
        copy_b(peer, h, lax.rem(peer, nt)).wait_send()
        copy_b(h, peer, own).wait_recv()
        return carry

    lax.fori_loop(1, nx, wait_b, 0)
    recv_c[own] = jnp.sum(recv_b[...], axis=0)

    base = h - own

    def copy_c(peer_tile, slot_tile):
        return pltpu.make_async_remote_copy(
            src_ref=recv_c.at[slot_tile],
            dst_ref=recv_c.at[slot_tile],
            send_sem=sc.at[peer_tile],
            recv_sem=rc.at[slot_tile],
            device_id=(base + peer_tile, a),
            device_id_type=MESH_ID,
        )

    def start_c(j, carry):
        copy_c(lax.rem(own + j, nt), own).start()
        return carry

    def copy_d_tile(peer, tile):
        row0 = pl.multiple_of(lax.rem(tile, kb) * SUB, SUB)
        return pltpu.make_async_remote_copy(
            src_ref=recv_c.at[tile],
            dst_ref=recv_d.at[a, tile // kb, pl.ds(row0, SUB), :],
            send_sem=sd.at[peer],
            recv_sem=rd.at[a],
            device_id=(h, peer),
            device_id_type=MESH_ID,
        )

    def copy_d(peer, slot_src):
        return pltpu.make_async_remote_copy(
            src_ref=recv_d.at[slot_src],
            dst_ref=recv_d.at[slot_src],
            send_sem=sd.at[peer],
            recv_sem=rd.at[slot_src],
            device_id=(h, peer),
            device_id_type=MESH_ID,
        )

    def forward(tile):
        def start_d(j, carry):
            copy_d_tile(lax.rem(a + j, ny), tile).start()
            return carry

        lax.fori_loop(1, ny, start_d, 0)

    lax.fori_loop(1, nt, start_c, 0)
    forward(own)

    def wait_c(j, carry):
        other = lax.rem(own + j, nt)
        copy_c(own, other).wait_recv()
        forward(other)
        return carry

    lax.fori_loop(1, nt, wait_c, 0)

    def wait_c_send(j, carry):
        copy_c(lax.rem(own + j, nt), own).wait_send()
        return carry

    lax.fori_loop(1, nt, wait_c_send, 0)

    def wait_d(j, carry):
        copy_d(lax.rem(a + j, ny), a).wait_send()
        copy_d(a, lax.rem(a + j, ny)).wait_recv()
        return carry

    lax.fori_loop(1, ny, wait_d, 0)
    for u in range(nt):
        recv_d[a, u // kb, (u % kb) * SUB:(u % kb + 1) * SUB, :] = recv_c[u]
    for s in range(ny):
        block = recv_d[s]
        if divisor is not None:
            block = block / divisor
        o_ref[:, :, s * LANES:(s + 1) * LANES] = block
    if orthonormalize:
        orthonormal_rows(o_ref)


def orthonormal_rows(rows_ref):
    nb, k = rows_ref.shape[0], rows_ref.shape[1]
    gram = jnp.stack([
        lax.dot_general(rows_ref[b], rows_ref[b], (((1,), (1,)), ((), ())),
                        precision=HIGHEST, preferred_element_type=jnp.float32)
        for b in range(nb)
    ])
    r_idx = lax.broadcasted_iota(jnp.int32, (nb, k, k), 1)
    c_idx = lax.broadcasted_iota(jnp.int32, (nb, k, k), 2)
    diag = r_idx == c_idx
    trace_value = jnp.sum(jnp.sum(jnp.where(diag, gram, 0.0), axis=2, keepdims=True),
                          axis=1, keepdims=True)
    shift_value = 1e-06 * (trace_value / k + 1.0)
    work = gram + jnp.where(diag, shift_value, 0.0)
    sub_idx = r_idx[:, :, :1]
    lane_idx = c_idx[:, :1, :]
    inverse = jnp.where(diag, 1.0, 0.0)
    for j in range(k):
        row = work[:, j:j + 1, :]
        inv_root = lax.rsqrt(row[:, :, j:j + 1])
        col = jnp.where(sub_idx >= j, work[:, :, j:j + 1] * inv_root, 0.0)
        row = jnp.where(lane_idx >= j, row * inv_root, 0.0)
        work = work - col * row
        solved = inverse[:, j:j + 1, :] * inv_root
        below = jnp.where(sub_idx > j, col, 0.0)
        inverse = jnp.where(sub_idx == j, solved, inverse - below * solved)
    for b in range(nb):
        rows_ref[b] = jnp.dot(inverse[b], rows_ref[b], precision=HIGHEST,
                              preferred_element_type=jnp.float32)


def write_pieces(value_ref, patterns, stacked):
    for b in range(value_ref.shape[0]):
        value = value_ref[b]
        k = value.shape[0]
        hi = value.astype(jnp.bfloat16)
        rest = value - hi.astype(jnp.float32)
        mid = rest.astype(jnp.bfloat16)
        lo = (rest - mid.astype(jnp.float32)).astype(jnp.bfloat16)
        parts = (hi, mid, lo)
        for pattern, out_ref in zip(patterns, stacked):
            for g, piece in enumerate(pattern):
                out_ref[b, g * k:(g + 1) * k, :] = parts[piece]


def factors_kernel(nx, ny, divisor, x_ref, mq_ref, mk_ref, left_ref, lefts_ref, right_ref,
                   rights_ref, pair_ref, local_ref, m_hi_ref, m_mid_ref, *scratch):
    first, second = scratch[:13], scratch[13:]
    width = 256
    merged_refs = (mq_ref, mk_ref)

    def split_merged():
        for b, m_ref in enumerate(merged_refs):
            for c in range(m_ref.shape[1] // width):
                block = m_ref[:, c * width:(c + 1) * width]
                hi = block.astype(jnp.bfloat16)
                m_hi_ref[b, :, c * width:(c + 1) * width] = hi
                m_mid_ref[b, :, c * width:(c + 1) * width] = (
                    block - hi.astype(jnp.float32)).astype(jnp.bfloat16)

    allreduce_body(nx, ny, True, None, x_ref, left_ref, *first, idle_work=split_merged)
    write_pieces(left_ref, ((0, 0, 1, 0, 1, 2), (0, 1)), (lefts_ref, pair_ref))
    k = left_ref.shape[1]
    def right_product(b):
        both = jnp.dot(pair_ref[b], m_hi_ref[b], preferred_element_type=jnp.float32)
        cross = jnp.dot(lefts_ref[b, :k, :], m_mid_ref[b], preferred_element_type=jnp.float32)
        local_ref[b] = both[:k] + (both[k:] + cross)

    allreduce_body(nx, ny, False, divisor, local_ref, right_ref, *second, with_barrier=False,
                   produce=right_product)
    write_pieces(right_ref, ((0, 1, 0, 2, 1, 0),), (rights_ref,))


def allreduce_scratch(nx, ny, nb, rows):
    vmem = pltpu.VMEM
    nt = nb * (rows // SUB)
    return [
        vmem((ny, nb, rows, LANES), jnp.float32),
        vmem((nt, SUB, LANES), jnp.float32),
        vmem((nx, SUB, LANES), jnp.float32),
        vmem((nt, SUB, LANES), jnp.float32),
        vmem((ny, nb, rows, LANES), jnp.float32),
        pltpu.SemaphoreType.DMA((ny,)),
        pltpu.SemaphoreType.DMA((ny,)),
        pltpu.SemaphoreType.DMA((nx,)),
        pltpu.SemaphoreType.DMA((nx,)),
        pltpu.SemaphoreType.DMA((nt,)),
        pltpu.SemaphoreType.DMA((nt,)),
        pltpu.SemaphoreType.DMA((ny,)),
        pltpu.SemaphoreType.DMA((ny,)),
    ]


def factors(x, query_merged, key_merged, nx, ny, divisor):
    nb, rows, cols = x.shape
    assert cols == ny * LANES and rows % SUB == 0
    assert nx % (nb * (rows // SUB)) == 0
    vmem = pltpu.VMEM
    f32, bf16 = jnp.float32, jnp.bfloat16
    return pl.pallas_call(
        functools.partial(factors_kernel, nx, ny, divisor),
        out_shape=[
            jax.ShapeDtypeStruct(x.shape, f32),
            jax.ShapeDtypeStruct((nb, 6 * rows, cols), bf16),
            jax.ShapeDtypeStruct(x.shape, f32),
            jax.ShapeDtypeStruct((nb, 6 * rows, cols), bf16),
        ],
        in_specs=[pl.BlockSpec(memory_space=vmem)] * 3,
        out_specs=[pl.BlockSpec(memory_space=vmem)] * 4,
        scratch_shapes=[vmem((nb, 2 * rows, cols), bf16), vmem(x.shape, f32),
                        vmem((2,) + query_merged.shape, bf16), vmem((2,) + query_merged.shape, bf16)]
        + allreduce_scratch(nx, ny, nb, rows) + allreduce_scratch(nx, ny, nb, rows),
        compiler_params=pltpu.CompilerParams(
            collective_id=0, has_side_effects=True,
            vmem_limit_bytes=24 * 1024 * 1024,
        ),
    )(x, query_merged, key_merged)


def allreduce(x, nx, ny, collective_id, orthonormalize=False, divisor=None, patterns=()):
    nb, rows, cols = x.shape
    assert cols == ny * LANES and rows % SUB == 0
    nt = nb * (rows // SUB)
    assert nx % nt == 0
    vmem = pltpu.VMEM
    return pl.pallas_call(
        functools.partial(allreduce_kernel, nx, ny, orthonormalize, divisor, patterns),
        out_shape=[jax.ShapeDtypeStruct(x.shape, jnp.float32)] + [
            jax.ShapeDtypeStruct((nb, len(p) * rows, cols), jnp.bfloat16) for p in patterns],
        in_specs=[pl.BlockSpec(memory_space=vmem)],
        out_specs=[pl.BlockSpec(memory_space=vmem)] * (1 + len(patterns)),
        scratch_shapes=[
            vmem((ny, nb, rows, LANES), jnp.float32),
            vmem((nt, SUB, LANES), jnp.float32),
            vmem((nx, SUB, LANES), jnp.float32),
            vmem((nt, SUB, LANES), jnp.float32),
            vmem((ny, nb, rows, LANES), jnp.float32),
            pltpu.SemaphoreType.DMA((ny,)),
            pltpu.SemaphoreType.DMA((ny,)),
            pltpu.SemaphoreType.DMA((nx,)),
            pltpu.SemaphoreType.DMA((nx,)),
            pltpu.SemaphoreType.DMA((nt,)),
            pltpu.SemaphoreType.DMA((nt,)),
            pltpu.SemaphoreType.DMA((ny,)),
            pltpu.SemaphoreType.DMA((ny,)),
        ],
        compiler_params=pltpu.CompilerParams(
            collective_id=collective_id, has_side_effects=True,
            vmem_limit_bytes=8 * 1024 * 1024,
        ),
    )(x)


def gram_of(factor_rows):
    return jnp.einsum("bki,bli->bkl", factor_rows, factor_rows, precision=HIGHEST)


def solve_rows(gram_matrix, factor_rows):
    width = gram_matrix.shape[-1]
    identity = jnp.eye(width, dtype=jnp.float32)
    trace_value = jnp.trace(gram_matrix, axis1=1, axis2=2)
    shift_value = 1e-06 * (trace_value / width + 1.0)
    lower_factor = jnp.linalg.cholesky(gram_matrix + shift_value[:, None, None] * identity)
    return lax.linalg.triangular_solve(lower_factor, factor_rows, left_side=True, lower=True)


def on_device(nx, ny, normed, grad_query, grad_key, error, start_factor):
    replicas = nx * ny
    query_grad = lax.dot_general(normed, grad_query, CONTRACT, preferred_element_type=jnp.float32)
    key_grad = lax.dot_general(normed, grad_key, CONTRACT, preferred_element_type=jnp.float32)
    query_merged = query_grad + error[0].astype(jnp.float32)
    key_merged = key_grad + error[1].astype(jnp.float32)
    merged = jnp.stack([query_merged, key_merged])
    m_hi, m_mid, m_lo = split3(merged)
    s_hi, s_mid, s_lo = split3(start_factor)
    left_local = combine6(*rows_times(
        [[s_hi, s_mid, s_lo], [s_hi, s_mid], [s_hi]], [m_hi, m_mid, m_lo], "bkj,bij->bki"))
    left_rows, lefts, right_rows, rights = factors(
        left_local, query_merged, key_merged, nx, ny, float(replicas))
    approx = jnp.einsum("bki,bkj->bij", lefts, rights, preferred_element_type=jnp.float32)
    k = left_rows.shape[1]
    left_out = exact_sum(lefts[:, :k], lefts[:, 2 * k:3 * k], lefts[:, 5 * k:])
    right_out = exact_sum(rights[:, :k], rights[:, k:2 * k], rights[:, 3 * k:4 * k])
    return ((merged - approx).astype(jnp.bfloat16), left_out, right_out)


def exact_sum(hi, mid, lo):
    f32 = jnp.float32
    return (hi.astype(f32) + mid.astype(f32)) + lo.astype(f32)


def split3(x):
    hi = lax.reduce_precision(x, exponent_bits=8, mantissa_bits=7)
    rest = x - hi
    mid = lax.reduce_precision(rest, exponent_bits=8, mantissa_bits=7)
    lo = rest - mid
    return (hi.astype(jnp.bfloat16), mid.astype(jnp.bfloat16), lo.astype(jnp.bfloat16))


def rows_times(row_groups, big_pieces, spec):
    out = []
    for group, big in zip(row_groups, big_pieces):
        k = group[0].shape[1]
        prod = jnp.einsum(spec, jnp.concatenate(group, axis=1), big,
                          preferred_element_type=jnp.float32)
        out.append([prod[:, g * k:(g + 1) * k] for g in range(len(group))])
    return out


def combine6(first, second, third):
    small = (first[2] + second[1]) + third[0]
    return first[0] + ((first[1] + second[0]) + small)


def solution(mesh):
    nx, ny = mesh.shape["gx"], mesh.shape["gy"]
    placed = (
        P(("gx", "gy"), None),
        P(("gx", "gy"), None),
        P(("gx", "gy"), None),
        P(("gx", "gy"), None, None),
        P(),
    )
    return jax.shard_map(
        functools.partial(on_device, nx, ny),
        mesh=mesh,
        in_specs=placed,
        out_specs=(P(("gx", "gy"), None, None), P(), P()),
        check_vma=False,
    )
```

```python
import functools

import jax
import jax.numpy as jnp
from jax import lax
from jax.experimental import pallas as pl
from jax.experimental.pallas import tpu as pltpu
from jax.sharding import PartitionSpec as P

HIGHEST = lax.Precision.HIGHEST
HIGH = lax.Precision.HIGH
CONTRACT = (((0,), (0,)), ((), ()))
MESH_ID = pl.DeviceIdType.MESH
LANES = 128
SUB = 8


def allreduce_kernel(nx, ny, orthonormalize, divisor, patterns, x_ref, o_ref, *refs):
    stacked = refs[:len(patterns)]
    allreduce_body(nx, ny, orthonormalize, divisor, x_ref, o_ref, *refs[len(patterns):])
    for b in range(o_ref.shape[0]):
        value = o_ref[b]
        k = value.shape[0]
        hi = value.astype(jnp.bfloat16)
        rest = value - hi.astype(jnp.float32)
        mid = rest.astype(jnp.bfloat16)
        lo = (rest - mid.astype(jnp.float32)).astype(jnp.bfloat16)
        parts = (hi, mid, lo)
        for pattern, out_ref in zip(patterns, stacked):
            for g, piece in enumerate(pattern):
                out_ref[b, g * k:(g + 1) * k, :] = parts[piece]


def allreduce_body(nx, ny, orthonormalize, divisor, x_ref, o_ref, recv_a, p_t, recv_b, recv_c, recv_d,
                     sa, ra, sb, rb, sc, rc, sd, rd, with_barrier=True, idle_work=None,
                     produce=None):
    h = lax.axis_index("gx")
    a = lax.axis_index("gy")
    nb, rows = x_ref.shape[0], x_ref.shape[1]
    kb = rows // SUB
    nt = nb * kb

    barrier = pltpu.get_barrier_semaphore()

    def signal_y(j, carry):
        pl.semaphore_signal(barrier, 1, device_id=(h, lax.rem(a + j, ny)),
                            device_id_type=MESH_ID)
        return carry

    def signal_x(j, carry):
        pl.semaphore_signal(barrier, 1, device_id=(lax.rem(h + j, nx), a),
                            device_id_type=MESH_ID)
        return carry

    if with_barrier:
        lax.fori_loop(1, ny, signal_y, 0)
        lax.fori_loop(1, nx, signal_x, 0)
        pl.semaphore_wait(barrier, (ny - 1) + (nx - 1))

    def copy_a(peer, slot_src):
        return pltpu.make_async_remote_copy(
            src_ref=x_ref.at[:, :, pl.ds(pl.multiple_of(peer * LANES, LANES), LANES)],
            dst_ref=recv_a.at[slot_src],
            send_sem=sa.at[peer],
            recv_sem=ra.at[slot_src],
            device_id=(h, peer),
            device_id_type=MESH_ID,
        )

    def start_a(j, carry):
        copy_a(lax.rem(a + j, ny), a).start()
        return carry

    def start_part(b):
        def start_one(j, carry):
            peer = lax.rem(a + j, ny)
            pltpu.make_async_remote_copy(
                src_ref=x_ref.at[b, :, pl.ds(pl.multiple_of(peer * LANES, LANES), LANES)],
                dst_ref=recv_a.at[a, b],
                send_sem=sa.at[peer],
                recv_sem=ra.at[a],
                device_id=(h, peer),
                device_id_type=MESH_ID,
            ).start()
            return carry

        lax.fori_loop(1, ny, start_one, 0)

    if produce is None:
        lax.fori_loop(1, ny, start_a, 0)
    else:
        for b in range(nb):
            produce(b)
            start_part(b)
    recv_a[a] = x_ref[:, :, pl.ds(pl.multiple_of(a * LANES, LANES), LANES)]

    def wait_a(j, carry):
        copy_a(lax.rem(a + j, ny), a).wait_send()
        copy_a(a, lax.rem(a + j, ny)).wait_recv()
        return carry

    lax.fori_loop(1, ny, wait_a, 0)
    part = jnp.sum(recv_a[...], axis=0)
    for u in range(nt):
        p_t[u] = part[u // kb, (u % kb) * SUB:(u % kb + 1) * SUB, :]

    def copy_b(peer, slot_src, tile):
        return pltpu.make_async_remote_copy(
            src_ref=p_t.at[tile],
            dst_ref=recv_b.at[slot_src],
            send_sem=sb.at[peer],
            recv_sem=rb.at[slot_src],
            device_id=(peer, a),
            device_id_type=MESH_ID,
        )

    def start_b(j, carry):
        peer = lax.rem(h + j, nx)
        copy_b(peer, h, lax.rem(peer, nt)).start()
        return carry

    lax.fori_loop(1, nx, start_b, 0)
    own = lax.rem(h, nt)
    recv_b[h] = p_t[own]
    if idle_work is not None:
        idle_work()

    def wait_b(j, carry):
        peer = lax.rem(h + j, nx)
        copy_b(peer, h, lax.rem(peer, nt)).wait_send()
        copy_b(h, peer, own).wait_recv()
        return carry

    lax.fori_loop(1, nx, wait_b, 0)
    recv_c[own] = jnp.sum(recv_b[...], axis=0)

    base = h - own

    def copy_c(peer_tile, slot_tile):
        return pltpu.make_async_remote_copy(
            src_ref=recv_c.at[slot_tile],
            dst_ref=recv_c.at[slot_tile],
            send_sem=sc.at[peer_tile],
            recv_sem=rc.at[slot_tile],
            device_id=(base + peer_tile, a),
            device_id_type=MESH_ID,
        )

    def start_c(j, carry):
        copy_c(lax.rem(own + j, nt), own).start()
        return carry

    def copy_d_tile(peer, tile):
        row0 = pl.multiple_of(lax.rem(tile, kb) * SUB, SUB)
        return pltpu.make_async_remote_copy(
            src_ref=recv_c.at[tile],
            dst_ref=recv_d.at[a, tile // kb, pl.ds(row0, SUB), :],
            send_sem=sd.at[peer],
            recv_sem=rd.at[a],
            device_id=(h, peer),
            device_id_type=MESH_ID,
        )

    def copy_d(peer, slot_src):
        return pltpu.make_async_remote_copy(
            src_ref=recv_d.at[slot_src],
            dst_ref=recv_d.at[slot_src],
            send_sem=sd.at[peer],
            recv_sem=rd.at[slot_src],
            device_id=(h, peer),
            device_id_type=MESH_ID,
        )

    def forward(tile):
        def start_d(j, carry):
            copy_d_tile(lax.rem(a + j, ny), tile).start()
            return carry

        lax.fori_loop(1, ny, start_d, 0)

    lax.fori_loop(1, nt, start_c, 0)
    forward(own)

    def wait_c(j, carry):
        other = lax.rem(own + j, nt)
        copy_c(own, other).wait_recv()
        forward(other)
        return carry

    lax.fori_loop(1, nt, wait_c, 0)

    def wait_c_send(j, carry):
        copy_c(lax.rem(own + j, nt), own).wait_send()
        return carry

    lax.fori_loop(1, nt, wait_c_send, 0)

    def wait_d(j, carry):
        copy_d(lax.rem(a + j, ny), a).wait_send()
        copy_d(a, lax.rem(a + j, ny)).wait_recv()
        return carry

    lax.fori_loop(1, ny, wait_d, 0)
    for u in range(nt):
        recv_d[a, u // kb, (u % kb) * SUB:(u % kb + 1) * SUB, :] = recv_c[u]
    for s in range(ny):
        block = recv_d[s]
        if divisor is not None:
            block = block / divisor
        o_ref[:, :, s * LANES:(s + 1) * LANES] = block
    if orthonormalize:
        orthonormal_rows(o_ref)


def orthonormal_rows(rows_ref):
    nb, k = rows_ref.shape[0], rows_ref.shape[1]
    gram = jnp.stack([
        lax.dot_general(rows_ref[b], rows_ref[b], (((1,), (1,)), ((), ())),
                        precision=HIGHEST, preferred_element_type=jnp.float32)
        for b in range(nb)
    ])
    r_idx = lax.broadcasted_iota(jnp.int32, (nb, k, k), 1)
    c_idx = lax.broadcasted_iota(jnp.int32, (nb, k, k), 2)
    diag = r_idx == c_idx
    trace_value = jnp.sum(jnp.sum(jnp.where(diag, gram, 0.0), axis=2, keepdims=True),
                          axis=1, keepdims=True)
    shift_value = 1e-06 * (trace_value / k + 1.0)
    work = gram + jnp.where(diag, shift_value, 0.0)
    sub_idx = r_idx[:, :, :1]
    lane_idx = c_idx[:, :1, :]
    inverse = jnp.where(diag, 1.0, 0.0)
    for j in range(k):
        row = work[:, j:j + 1, :]
        inv_root = lax.rsqrt(row[:, :, j:j + 1])
        col = jnp.where(sub_idx >= j, work[:, :, j:j + 1] * inv_root, 0.0)
        row = jnp.where(lane_idx >= j, row * inv_root, 0.0)
        work = work - col * row
        solved = inverse[:, j:j + 1, :] * inv_root
        below = jnp.where(sub_idx > j, col, 0.0)
        inverse = jnp.where(sub_idx == j, solved, inverse - below * solved)
    for b in range(nb):
        rows_ref[b] = jnp.dot(inverse[b], rows_ref[b], precision=HIGHEST,
                              preferred_element_type=jnp.float32)


def write_pieces(value_ref, patterns, stacked):
    for b in range(value_ref.shape[0]):
        value = value_ref[b]
        k = value.shape[0]
        hi = value.astype(jnp.bfloat16)
        rest = value - hi.astype(jnp.float32)
        mid = rest.astype(jnp.bfloat16)
        lo = (rest - mid.astype(jnp.float32)).astype(jnp.bfloat16)
        parts = (hi, mid, lo)
        for pattern, out_ref in zip(patterns, stacked):
            for g, piece in enumerate(pattern):
                out_ref[b, g * k:(g + 1) * k, :] = parts[piece]


def factors_kernel(nx, ny, divisor, x_ref, mq_ref, mk_ref, left_ref, lefts_ref, right_ref,
                   rights_ref, pair_ref, local_ref, m_hi_ref, m_mid_ref, *scratch):
    first, second = scratch[:13], scratch[13:]
    width = 256
    merged_refs = (mq_ref, mk_ref)

    def split_merged():
        for b, m_ref in enumerate(merged_refs):
            for c in range(m_ref.shape[1] // width):
                block = m_ref[:, c * width:(c + 1) * width]
                hi = block.astype(jnp.bfloat16)
                m_hi_ref[b, :, c * width:(c + 1) * width] = hi
                m_mid_ref[b, :, c * width:(c + 1) * width] = (
                    block - hi.astype(jnp.float32)).astype(jnp.bfloat16)

    allreduce_body(nx, ny, True, None, x_ref, left_ref, *first, idle_work=split_merged)
    write_pieces(left_ref, ((0, 0, 1, 0, 1, 2), (0, 1)), (lefts_ref, pair_ref))
    k = left_ref.shape[1]
    def right_product(b):
        both = jnp.dot(pair_ref[b], m_hi_ref[b], preferred_element_type=jnp.float32)
        cross = jnp.dot(lefts_ref[b, :k, :], m_mid_ref[b], preferred_element_type=jnp.float32)
        local_ref[b] = both[:k] + (both[k:] + cross)

    allreduce_body(nx, ny, False, divisor, local_ref, right_ref, *second, with_barrier=False,
                   produce=right_product)
    write_pieces(right_ref, ((0, 1, 0, 2, 1, 0),), (rights_ref,))


def allreduce_scratch(nx, ny, nb, rows):
    vmem = pltpu.VMEM
    nt = nb * (rows // SUB)
    return [
        vmem((ny, nb, rows, LANES), jnp.float32),
        vmem((nt, SUB, LANES), jnp.float32),
        vmem((nx, SUB, LANES), jnp.float32),
        vmem((nt, SUB, LANES), jnp.float32),
        vmem((ny, nb, rows, LANES), jnp.float32),
        pltpu.SemaphoreType.DMA((ny,)),
        pltpu.SemaphoreType.DMA((ny,)),
        pltpu.SemaphoreType.DMA((nx,)),
        pltpu.SemaphoreType.DMA((nx,)),
        pltpu.SemaphoreType.DMA((nt,)),
        pltpu.SemaphoreType.DMA((nt,)),
        pltpu.SemaphoreType.DMA((ny,)),
        pltpu.SemaphoreType.DMA((ny,)),
    ]


def factors(x, query_merged, key_merged, nx, ny, divisor):
    nb, rows, cols = x.shape
    assert cols == ny * LANES and rows % SUB == 0
    assert nx % (nb * (rows // SUB)) == 0
    vmem = pltpu.VMEM
    f32, bf16 = jnp.float32, jnp.bfloat16
    return pl.pallas_call(
        functools.partial(factors_kernel, nx, ny, divisor),
        out_shape=[
            jax.ShapeDtypeStruct(x.shape, f32),
            jax.ShapeDtypeStruct((nb, 6 * rows, cols), bf16),
            jax.ShapeDtypeStruct(x.shape, f32),
            jax.ShapeDtypeStruct((nb, 6 * rows, cols), bf16),
        ],
        in_specs=[pl.BlockSpec(memory_space=vmem)] * 3,
        out_specs=[pl.BlockSpec(memory_space=vmem)] * 4,
        scratch_shapes=[vmem((nb, 2 * rows, cols), bf16), vmem(x.shape, f32),
                        vmem((2,) + query_merged.shape, bf16), vmem((2,) + query_merged.shape, bf16)]
        + allreduce_scratch(nx, ny, nb, rows) + allreduce_scratch(nx, ny, nb, rows),
        compiler_params=pltpu.CompilerParams(
            collective_id=0, has_side_effects=True,
            vmem_limit_bytes=24 * 1024 * 1024,
        ),
    )(x, query_merged, key_merged)


def allreduce(x, nx, ny, collective_id, orthonormalize=False, divisor=None, patterns=()):
    nb, rows, cols = x.shape
    assert cols == ny * LANES and rows % SUB == 0
    nt = nb * (rows // SUB)
    assert nx % nt == 0
    vmem = pltpu.VMEM
    return pl.pallas_call(
        functools.partial(allreduce_kernel, nx, ny, orthonormalize, divisor, patterns),
        out_shape=[jax.ShapeDtypeStruct(x.shape, jnp.float32)] + [
            jax.ShapeDtypeStruct((nb, len(p) * rows, cols), jnp.bfloat16) for p in patterns],
        in_specs=[pl.BlockSpec(memory_space=vmem)],
        out_specs=[pl.BlockSpec(memory_space=vmem)] * (1 + len(patterns)),
        scratch_shapes=[
            vmem((ny, nb, rows, LANES), jnp.float32),
            vmem((nt, SUB, LANES), jnp.float32),
            vmem((nx, SUB, LANES), jnp.float32),
            vmem((nt, SUB, LANES), jnp.float32),
            vmem((ny, nb, rows, LANES), jnp.float32),
            pltpu.SemaphoreType.DMA((ny,)),
            pltpu.SemaphoreType.DMA((ny,)),
            pltpu.SemaphoreType.DMA((nx,)),
            pltpu.SemaphoreType.DMA((nx,)),
            pltpu.SemaphoreType.DMA((nt,)),
            pltpu.SemaphoreType.DMA((nt,)),
            pltpu.SemaphoreType.DMA((ny,)),
            pltpu.SemaphoreType.DMA((ny,)),
        ],
        compiler_params=pltpu.CompilerParams(
            collective_id=collective_id, has_side_effects=True,
            vmem_limit_bytes=8 * 1024 * 1024,
        ),
    )(x)


def gram_of(factor_rows):
    return jnp.einsum("bki,bli->bkl", factor_rows, factor_rows, precision=HIGHEST)


def solve_rows(gram_matrix, factor_rows):
    width = gram_matrix.shape[-1]
    identity = jnp.eye(width, dtype=jnp.float32)
    trace_value = jnp.trace(gram_matrix, axis1=1, axis2=2)
    shift_value = 1e-06 * (trace_value / width + 1.0)
    lower_factor = jnp.linalg.cholesky(gram_matrix + shift_value[:, None, None] * identity)
    return lax.linalg.triangular_solve(lower_factor, factor_rows, left_side=True, lower=True)


def on_device(nx, ny, normed, grad_query, grad_key, error, start_factor):
    replicas = nx * ny
    query_grad = lax.dot_general(normed, grad_query, CONTRACT, preferred_element_type=jnp.float32)
    key_grad = lax.dot_general(normed, grad_key, CONTRACT, preferred_element_type=jnp.float32)
    query_merged = query_grad + error[0].astype(jnp.float32)
    key_merged = key_grad + error[1].astype(jnp.float32)
    merged = jnp.stack([query_merged, key_merged])
    m_hi, m_mid, m_lo = split3(merged)
    s_hi, s_mid, s_lo = split3(start_factor)
    left_local = combine6(*rows_times(
        [[s_hi, s_mid, s_lo], [s_hi, s_mid], [s_hi]], [m_hi, m_mid, m_lo], "bkj,bij->bki"))
    left_rows, lefts, right_rows, rights = factors(
        left_local, query_merged, key_merged, nx, ny, float(replicas))
    approx = jnp.einsum("bki,bkj->bij", lefts, rights, preferred_element_type=jnp.float32)
    k = left_rows.shape[1]
    left_out = exact_sum(lefts[:, :k], lefts[:, 2 * k:3 * k], lefts[:, 5 * k:])
    right_out = exact_sum(rights[:, :k], rights[:, k:2 * k], rights[:, 3 * k:4 * k])
    return ((merged - approx).astype(jnp.bfloat16), left_out, right_out)


def exact_sum(hi, mid, lo):
    f32 = jnp.float32
    return (hi.astype(f32) + mid.astype(f32)) + lo.astype(f32)


def split3(x):
    hi = lax.reduce_precision(x, exponent_bits=8, mantissa_bits=7)
    rest = x - hi
    mid = lax.reduce_precision(rest, exponent_bits=8, mantissa_bits=7)
    lo = rest - mid
    return (hi.astype(jnp.bfloat16), mid.astype(jnp.bfloat16), lo.astype(jnp.bfloat16))


def rows_times(row_groups, big_pieces, spec):
    out = []
    for group, big in zip(row_groups, big_pieces):
        k = group[0].shape[1]
        prod = jnp.einsum(spec, jnp.concatenate(group, axis=1), big,
                          preferred_element_type=jnp.float32)
        out.append([prod[:, g * k:(g + 1) * k] for g in range(len(group))])
    return out


def combine6(first, second, third):
    small = (first[2] + second[1]) + third[0]
    return first[0] + ((first[1] + second[0]) + small)


def solution(mesh):
    nx, ny = mesh.shape["gx"], mesh.shape["gy"]
    placed = (
        P(("gx", "gy"), None),
        P(("gx", "gy"), None),
        P(("gx", "gy"), None),
        P(("gx", "gy"), None, None),
        P(),
    )
    return jax.shard_map(
        functools.partial(on_device, nx, ny),
        mesh=mesh,
        in_specs=placed,
        out_specs=(P(("gx", "gy"), None, None), P(), P()),
        check_vma=False,
    )
```
